256 devices in a mesh: rows: 64 (over x, z, core), cols: 4 (over y).
Axes of the slice: x: 4, y: 4, z: 8, core: 2. Of those that a mesh axis runs over, the one named last changes fastest.
Arguments:
- block_list: int32 [512, 24], P('rows', 'cols'), may hold values from -1 to 511, as said below
- points: bfloat16 [16, 131072], P(None, 'rows'), may hold values from -4 to 4
- targets: float32 [32, 131072], P(None, 'rows'), may hold values from -6 to 6
Outputs:
- solution: float32 [32, 131072], P(None, 'rows')
- residual: float32 [32, 131072], P(None, 'rows')
The draws below stay inside these ranges and needn't reach their ends.
Inputs may be any that keep to these rules, and one draw needn't show every extreme that they name: `block_list`: A non-empty entry j of block row i satisfies j <= i. Within the 6 slots of a block row held by one index of cols, the entries lie in different groups of 8 consecutive blocks. Of all slots held by one device (8 block rows of 6 slots), at most 1 name blocks of any one group of 8 consecutive blocks, and in every draw some device reaches 1.
All inputs are finite; a program needn't handle non-finite values.
Results may differ from the reference program's by a relative error of at most 0.0057.
Values may be sent and summed in bfloat16 or wider, within the bound.
A program may use at most 64 MiB of HBM per device.

```python
import math
import jax
import jax.numpy as jnp
from jax import lax

DIM = 16
OUTS = 32
BLOCK = 256
SLOTS = 24
BR_DEV = 8
ITERS = 2
NB = 512
NPTS = 131072
N_ROWS = 64
N_COLS = 4


def draw_points(key, part):
    spread = 0.7 ** jnp.arange(DIM, dtype=jnp.float32)
    width = 0.31
    cycle = 0.57 * width / math.sin(math.pi / BR_DEV)
    block_id = jnp.arange(NPTS, dtype=jnp.int32) // BLOCK
    family = (block_id % BR_DEV).astype(jnp.float32)
    turn = family * (2.0 * math.pi / BR_DEV)
    dims = jnp.arange(DIM, dtype=jnp.int32)[:, None]
    center = jnp.where(dims == 0, cycle * jnp.cos(turn)[None, :], jnp.where(dims == 1, cycle * jnp.sin(turn)[None, :], 0.0))
    keys_two = jax.random.split(key, 2)
    drift = jnp.clip(jax.random.normal(keys_two[0], (DIM, NB), jnp.float32), -3.0, 3.0) * 0.15
    drift_all = drift[:, block_id]
    noise = jnp.clip(jax.random.normal(keys_two[1], (DIM, NPTS), jnp.float32), -4.0, 4.0)
    return (center + width * spread[:, None] * (noise + drift_all)).astype(jnp.bfloat16)


def draw_targets(key, part):
    position = jnp.arange(NPTS, dtype=jnp.float32) / NPTS
    noise = jnp.clip(jax.random.normal(key, (OUTS, NPTS), jnp.float32), -3.5, 3.5)
    return noise * (0.5 * 3.0 ** position)[None, :]


def draw_block_list(key, part):
    slot_width = SLOTS // N_COLS
    slot_count = BR_DEV * slot_width
    group_keys = jax.random.split(key, N_ROWS * N_COLS)

    def one_share(share_key, group):
        row_dev = group // N_COLS
        keys_six = jax.random.split(share_key, 6)
        owner_order = jax.random.permutation(keys_six[0], N_ROWS).astype(jnp.int32)
        offset = jax.random.randint(keys_six[1], (), 0, N_ROWS, dtype=jnp.int32)
        serial = jnp.arange(slot_count, dtype=jnp.int32)
        steps_back = owner_order[(serial + offset) % N_ROWS]
        owners = row_dev - steps_back
        row_line = serial // slot_width
        shift_by = jax.random.randint(keys_six[2], (slot_count,), -1, 2, dtype=jnp.int32)
        any_family = jax.random.randint(keys_six[4], (slot_count,), 0, BR_DEV, dtype=jnp.int32)
        rare = jax.random.randint(keys_six[5], (slot_count,), 0, 8, dtype=jnp.int32)
        distant = jnp.where(rare == 0, any_family, (row_line + shift_by + BR_DEV) % BR_DEV)
        nearby = jnp.maximum(row_line - jax.random.randint(keys_six[3], (slot_count,), 0, 2, dtype=jnp.int32), 0)
        chosen = jnp.where(steps_back == 0, row_dev * BR_DEV + nearby, owners * BR_DEV + distant)
        return jnp.where(owners >= 0, chosen, -1).reshape(BR_DEV, slot_width)
    shares = jax.vmap(one_share)(group_keys, jnp.arange(N_ROWS * N_COLS, dtype=jnp.int32))
    shares = shares.reshape(N_ROWS, N_COLS, BR_DEV, slot_width).transpose(0, 2, 1, 3)
    return shares.reshape(N_ROWS * BR_DEV, SLOTS).astype(jnp.int32)


def setup_inputs(seed: int = 0) -> dict:
    splits = jax.random.split(jax.random.key(seed), 4)
    return {
        "block_list": draw_block_list(jax.random.fold_in(splits[3], 71), 0),
        "points": draw_points(jax.random.fold_in(splits[3], 71), 0),
        "targets": draw_targets(jax.random.fold_in(splits[3], 71), 0),
    }


REG = 1.5
RADIUS = 0.25

def wendland(left_x, right_x):
    left_f = left_x.astype(jnp.float32)
    right_f = right_x.astype(jnp.float32)
    left_sq = lax.optimization_barrier(jnp.sum(left_f * left_f, axis=1))
    right_sq = lax.optimization_barrier(jnp.sum(right_f * right_f, axis=1))
    inner_prod = jnp.einsum('nda,ndb->nab', left_f, right_f, precision=lax.Precision.HIGHEST)
    dist_sq = left_sq[:, :, None] + right_sq[:, None, :] - 2.0 * inner_prod
    scaled = jnp.sqrt(jnp.maximum(dist_sq, 0.0)) / RADIUS
    remain = jnp.maximum(1.0 - scaled, 0.0)
    square = remain * remain
    return square * square * (4.0 * scaled + 1.0)

def accumulate(coords, block_list, weights):
    count = coords.shape[0]
    slots_all = block_list.shape[1]
    channels = 1 if weights is None else weights.shape[1]

    def row_step(total, row):
        entries = block_list[row]
        is_live = entries >= 0
        clipped = jnp.maximum(entries, 0)
        off_diag = is_live & (entries != row)
        near_x = jnp.broadcast_to(coords[row][None], (slots_all,) + coords.shape[1:])
        values = jnp.where(is_live[:, None, None], wendland(near_x, coords[clipped]), 0.0)
        if weights is None:
            direct = lax.optimization_barrier(jnp.sum(values, axis=(0, 2)))[None, :]
            mirror = jnp.where(off_diag[:, None], lax.optimization_barrier(jnp.sum(values, axis=1)), 0.0)[:, None, :]
        else:
            kernel_f = lax.optimization_barrier(values.astype(jnp.bfloat16)).astype(jnp.float32)
            direct = jnp.einsum('sab,sob->oa', kernel_f, weights[clipped])
            mirror = jnp.einsum('sab,oa->sob', kernel_f, weights[row])
            mirror = jnp.where(off_diag[:, None, None], mirror, 0.0)
        total = total.at[row].add(direct)
        total = total.at[clipped].add(mirror)
        return (total, None)
    start = jnp.zeros((count, channels, coords.shape[2]), jnp.float32)
    return lax.scan(row_step, start, jnp.arange(count, dtype=jnp.int32))[0]

def reference(block_list, points, targets):
    coord_dim, npoints = points.shape
    count = npoints // BLOCK
    outputs = targets.shape[0]
    coords = points.reshape(coord_dim, count, BLOCK).transpose(1, 0, 2)
    degree = 1.0 + accumulate(coords, block_list, None)
    inv_root = 1.0 / jnp.sqrt(degree)

    def apply_matrix(direction):
        weights = lax.optimization_barrier((direction * inv_root).astype(jnp.bfloat16)).astype(jnp.float32)
        return REG * direction + inv_root * accumulate(coords, block_list, weights)
    resid = targets.reshape(outputs, count, BLOCK).transpose(1, 0, 2)
    direction = resid
    solution = jnp.zeros_like(resid)
    norm_now = lax.optimization_barrier(jnp.sum(resid * resid, axis=(0, 2)))
    for iteration in range(ITERS):
        applied = apply_matrix(direction)
        step_size = norm_now / lax.optimization_barrier(jnp.sum(direction * applied, axis=(0, 2)))
        solution = solution + step_size[None, :, None] * direction
        resid = resid - step_size[None, :, None] * applied
        norm_next = lax.optimization_barrier(jnp.sum(resid * resid, axis=(0, 2)))
        direction = resid + (norm_next / norm_now)[None, :, None] * direction
        norm_now = norm_next
    return (solution.transpose(1, 0, 2).reshape(outputs, npoints), resid.transpose(1, 0, 2).reshape(outputs, npoints))
```

```python
import jax
import jax.numpy as jnp
from jax import lax
from jax.sharding import PartitionSpec as P

ITERS = 2


REG = 1.5
RADIUS = 0.25


def wendland(left_x, right_x):
    left_f = left_x.astype(jnp.float32)
    right_f = right_x.astype(jnp.float32)
    left_sq = jnp.sum(left_f * left_f, axis=1)
    right_sq = jnp.sum(right_f * right_f, axis=1)
    inner_prod = jnp.einsum("nda,ndb->nab", left_f, right_f, precision=lax.Precision.HIGHEST)
    dist_sq = left_sq[:, :, None] + right_sq[:, None, :] - 2.0 * inner_prod
    scaled = jnp.sqrt(jnp.maximum(dist_sq, 0.0)) / RADIUS
    remain = jnp.maximum(1.0 - scaled, 0.0)
    square = remain * remain
    return square * square * (4.0 * scaled + 1.0)


def local(block_list, points, targets):
    row_count = lax.axis_size("rows")
    row_index = lax.axis_index("rows")
    block_rows, slot_width = block_list.shape
    coord_dim, npoints = points.shape
    outputs = targets.shape[0]
    block_len = npoints // block_rows
    slot_count = block_rows * slot_width
    capacity = (slot_count + row_count - 1) // row_count
    buffer_len = row_count * capacity
    turn_rows = 4
    turn_count = block_rows // turn_rows
    entries = block_list.reshape(slot_count)
    is_live = entries >= 0
    owners = jnp.where(is_live, entries // block_rows, 0)
    local_idx = jnp.where(is_live, entries - owners * block_rows, 0)
    first_row = row_index * block_rows
    row_global = first_row + jnp.arange(slot_count, dtype=jnp.int32) // slot_width
    off_diag = is_live & (entries != row_global)
    owner_hits = (
        (owners[:, None] == jnp.arange(row_count, dtype=jnp.int32)[None, :]) & is_live[:, None]
    ).astype(jnp.int32)
    slot_rank = jnp.sum((jnp.cumsum(owner_hits, axis=0) - owner_hits) * owner_hits, axis=1)
    place_at = jnp.where(is_live, owners * capacity + slot_rank, buffer_len)
    pick_at = jnp.minimum(place_at, buffer_len - 1)
    wanted = jnp.full((buffer_len,), -1, jnp.int32).at[place_at].set(local_idx, mode="drop")
    askers = jnp.full((buffer_len,), -1, jnp.int32).at[place_at].set(row_global, mode="drop")
    request = jnp.stack([wanted, askers], axis=1).reshape(row_count, capacity, 2)
    incoming = lax.all_to_all(request, "rows", split_axis=0, concat_axis=0, tiled=True).reshape(
        buffer_len, 2
    )
    in_live = incoming[:, 0] >= 0
    in_idx = jnp.maximum(incoming[:, 0], 0)
    collect_map = (
        (in_idx[None, :] == jnp.arange(block_rows, dtype=jnp.int32)[:, None]) & in_live[None, :]
    ).astype(jnp.float32)

    def serve(blocks):
        chosen = jnp.where(in_live[:, None, None], blocks[in_idx], jnp.zeros((), blocks.dtype))
        arrived = lax.all_to_all(
            chosen.reshape(row_count, capacity, blocks.shape[1], block_len),
            "rows",
            split_axis=0,
            concat_axis=0,
            tiled=True,
        )
        gotten = arrived.reshape(buffer_len, blocks.shape[1], block_len)[pick_at]
        return jnp.where(is_live[:, None, None], gotten, jnp.zeros((), gotten.dtype))

    def collect(terms):
        flat = terms.reshape(buffer_len, -1)
        summed = jnp.dot(
            collect_map, flat, precision=lax.Precision.HIGHEST, preferred_element_type=jnp.float32
        )
        return summed.reshape(block_rows, terms.shape[1], block_len)

    def give_back(mirror):
        placed = (
            jnp.zeros((buffer_len,) + mirror.shape[1:], jnp.float32)
            .at[place_at]
            .set(mirror, mode="drop")
        )
        arrived = lax.all_to_all(
            placed.reshape(row_count, capacity, mirror.shape[1], block_len),
            "rows",
            split_axis=0,
            concat_axis=0,
            tiled=True,
        )
        return collect(arrived.reshape(buffer_len, mirror.shape[1], block_len))

    def column_total(partial_value):
        return lax.psum(partial_value, "cols")

    col_index = lax.axis_index("cols")

    def global_sum(values):
        masked = jnp.where(col_index == 0, values, jnp.zeros_like(values))
        return lax.psum(masked, ("rows", "cols"))

    own_x = points.reshape(coord_dim, block_rows, block_len).transpose(1, 0, 2)
    far_x = serve(own_x)
    grouped_x = own_x.reshape(turn_count, turn_rows, coord_dim, block_len)
    grouped_far = far_x.reshape(turn_count, turn_rows * slot_width, coord_dim, block_len)
    grouped_live = is_live.reshape(turn_count, turn_rows * slot_width)
    grouped_off = off_diag.reshape(turn_count, turn_rows * slot_width)

    def row_pass(own_w, far_w):

        def row_step(pieces):
            near_x, remote_x, live_now, off_now = (pieces[0], pieces[1], pieces[2], pieces[3])
            values = jnp.where(
                live_now[:, None, None],
                wendland(jnp.repeat(near_x, slot_width, axis=0), remote_x),
                0.0,
            )
            if own_w is None:
                direct = jnp.sum(
                    jnp.sum(values, axis=2).reshape(turn_rows, slot_width, block_len), axis=1
                )[:, None, :]
                mirror = jnp.where(off_now[:, None], jnp.sum(values, axis=1), 0.0)[:, None, :]
                return (direct, mirror)
            kernel_bf = values.astype(jnp.bfloat16)
            direct = jnp.einsum(
                "nab,nob->noa", kernel_bf, pieces[5], preferred_element_type=jnp.float32
            )
            direct = jnp.sum(direct.reshape(turn_rows, slot_width, outputs, block_len), axis=1)
            mirror = jnp.einsum(
                "nab,noa->nob",
                kernel_bf,
                jnp.repeat(pieces[4], slot_width, axis=0),
                preferred_element_type=jnp.float32,
            )
            return (direct, jnp.where(off_now[:, None, None], mirror, 0.0))

        pieces = (grouped_x, grouped_far, grouped_live, grouped_off)
        if own_w is not None:
            pieces = pieces + (
                own_w.reshape(turn_count, turn_rows, outputs, block_len),
                far_w.reshape(turn_count, turn_rows * slot_width, outputs, block_len),
            )
        results = lax.map(row_step, pieces)
        channels = results[0].shape[2]
        direct = results[0].reshape(block_rows, channels, block_len)
        return (direct, results[1].reshape(slot_count, channels, block_len))

    direct, mirror = row_pass(None, None)
    degree_part = direct + give_back(mirror)
    inv_root = 1.0 / jnp.sqrt(1.0 + column_total(degree_part))
    resid = targets.reshape(outputs, block_rows, block_len).transpose(1, 0, 2)
    direction = resid
    solution = jnp.zeros_like(resid)
    norm_now = global_sum(jnp.sum(resid * resid, axis=(0, 2)))
    for iteration in range(ITERS):
        weights = (direction * inv_root).astype(jnp.bfloat16)
        apply_far_w = serve(weights)
        apply_direct, apply_mirror = row_pass(weights, apply_far_w)
        apply_partial_value = apply_direct + give_back(apply_mirror)
        applied = REG * direction + inv_root * column_total(apply_partial_value)
        step_size = norm_now / global_sum(jnp.sum(direction * applied, axis=(0, 2)))
        solution = solution + step_size[None, :, None] * direction
        resid = resid - step_size[None, :, None] * applied
        if iteration + 1 < ITERS:
            norm_next = global_sum(jnp.sum(resid * resid, axis=(0, 2)))
            direction = resid + (norm_next / norm_now)[None, :, None] * direction
            norm_now = norm_next
    return (
        solution.transpose(1, 0, 2).reshape(outputs, npoints),
        resid.transpose(1, 0, 2).reshape(outputs, npoints),
    )


def solution(mesh):
    placed = (P("rows", "cols"), P(None, "rows"), P(None, "rows"))
    return jax.shard_map(
        local,
        mesh=mesh,
        in_specs=placed,
        out_specs=(P(None, "rows"), P(None, "rows")),
        check_vma=False,
    )
```

```python
import functools

import jax
import jax.numpy as jnp
from jax import lax
from jax.experimental import pallas as pl
from jax.experimental.pallas import tpu as pltpu
from jax.sharding import PartitionSpec as P

MESH = pl.DeviceIdType.MESH

ITERS = 2


REG = 1.5
RADIUS = 0.25


def wendland(left_x, right_x):
    left_f = left_x.astype(jnp.float32)
    right_f = right_x.astype(jnp.float32)
    left_sq = jnp.sum(left_f * left_f, axis=1)
    right_sq = jnp.sum(right_f * right_f, axis=1)
    inner_prod = jnp.einsum("nda,ndb->nab", left_f, right_f, precision=lax.Precision.HIGHEST)
    dist_sq = left_sq[:, :, None] + right_sq[:, None, :] - 2.0 * inner_prod
    scaled = jnp.sqrt(jnp.maximum(dist_sq, 0.0)) / RADIUS
    remain = jnp.maximum(1.0 - scaled, 0.0)
    square = remain * remain
    return square * square * (4.0 * scaled + 1.0)


def allsum_kernel(axis, n, x_ref, o_ref, recv, send_sem, recv_sem):
    me = lax.axis_index(axis)
    barrier = pltpu.get_barrier_semaphore()

    def greet(k, carry):
        peer = lax.rem(me + k, n)
        pl.semaphore_signal(barrier, inc=1, device_id={axis: peer}, device_id_type=MESH)
        return carry

    lax.fori_loop(1, n, greet, 0)
    pl.semaphore_wait(barrier, n - 1)

    def outgoing(peer):
        return pltpu.make_async_remote_copy(
            src_ref=x_ref,
            dst_ref=recv.at[me],
            send_sem=send_sem.at[peer],
            recv_sem=recv_sem.at[me],
            device_id={axis: peer},
            device_id_type=MESH,
        )

    def incoming(peer):
        return pltpu.make_async_remote_copy(
            src_ref=x_ref,
            dst_ref=recv.at[peer],
            send_sem=send_sem.at[peer],
            recv_sem=recv_sem.at[peer],
            device_id={axis: peer},
            device_id_type=MESH,
        )

    def start(k, carry):
        outgoing(lax.rem(me + k, n)).start()
        return carry

    lax.fori_loop(1, n, start, 0)
    recv[me] = x_ref[...]

    def finish(k, carry):
        peer = lax.rem(me + k, n)
        outgoing(peer).wait_send()
        incoming(peer).wait_recv()
        return carry

    lax.fori_loop(1, n, finish, 0)
    o_ref[...] = recv[0]

    def add(s, carry):
        o_ref[...] += recv[s]
        return carry

    lax.fori_loop(1, n, add, 0)


def allsum(x, axis, cid):
    n = lax.axis_size(axis)
    shape = x.shape
    flat = x.reshape(-1)
    size = flat.shape[0]
    lanes = 128 if size % 128 == 0 else 0
    if lanes and (size // 128) % 8 == 0:
        tile = flat.reshape(size // 128, 128)
    else:
        rows_pad = -(-size // 1024) * 8
        tile = jnp.pad(flat, (0, rows_pad * 128 - size)).reshape(rows_pad, 128)
    out = pl.pallas_call(
        functools.partial(allsum_kernel, axis, n),
        out_shape=jax.ShapeDtypeStruct(tile.shape, jnp.float32),
        in_specs=[pl.BlockSpec(memory_space=pltpu.VMEM)],
        out_specs=pl.BlockSpec(memory_space=pltpu.VMEM),
        scratch_shapes=[
            pltpu.VMEM((n,) + tile.shape, jnp.float32),
            pltpu.SemaphoreType.DMA((n,)),
            pltpu.SemaphoreType.DMA((n,)),
        ],
        compiler_params=pltpu.CompilerParams(collective_id=cid, has_side_effects=True),
    )(tile)
    return out.reshape(-1)[:size].reshape(shape)


def local(block_list, points, targets):
    row_count = lax.axis_size("rows")
    row_index = lax.axis_index("rows")
    block_rows, slot_width = block_list.shape
    coord_dim, npoints = points.shape
    outputs = targets.shape[0]
    block_len = npoints // block_rows
    slot_count = block_rows * slot_width
    capacity = (slot_count + row_count - 1) // row_count
    buffer_len = row_count * capacity
    turn_rows = 4
    turn_count = block_rows // turn_rows
    entries = block_list.reshape(slot_count)
    is_live = entries >= 0
    owners = jnp.where(is_live, entries // block_rows, 0)
    local_idx = jnp.where(is_live, entries - owners * block_rows, 0)
    first_row = row_index * block_rows
    row_global = first_row + jnp.arange(slot_count, dtype=jnp.int32) // slot_width
    off_diag = is_live & (entries != row_global)
    owner_hits = (
        (owners[:, None] == jnp.arange(row_count, dtype=jnp.int32)[None, :]) & is_live[:, None]
    ).astype(jnp.int32)
    slot_rank = jnp.sum((jnp.cumsum(owner_hits, axis=0) - owner_hits) * owner_hits, axis=1)
    place_at = jnp.where(is_live, owners * capacity + slot_rank, buffer_len)
    pick_at = jnp.minimum(place_at, buffer_len - 1)
    wanted = jnp.full((buffer_len,), -1, jnp.int32).at[place_at].set(local_idx, mode="drop")
    askers = jnp.full((buffer_len,), -1, jnp.int32).at[place_at].set(row_global, mode="drop")
    request = jnp.stack([wanted, askers], axis=1).reshape(row_count, capacity, 2)
    incoming = lax.all_to_all(request, "rows", split_axis=0, concat_axis=0, tiled=True).reshape(
        buffer_len, 2
    )
    in_live = incoming[:, 0] >= 0
    in_idx = jnp.maximum(incoming[:, 0], 0)
    collect_map = (
        (in_idx[None, :] == jnp.arange(block_rows, dtype=jnp.int32)[:, None]) & in_live[None, :]
    ).astype(jnp.float32)

    def serve(blocks):
        chosen = jnp.where(in_live[:, None, None], blocks[in_idx], jnp.zeros((), blocks.dtype))
        arrived = lax.all_to_all(
            chosen.reshape(row_count, capacity, blocks.shape[1], block_len),
            "rows",
            split_axis=0,
            concat_axis=0,
            tiled=True,
        )
        gotten = arrived.reshape(buffer_len, blocks.shape[1], block_len)[pick_at]
        return jnp.where(is_live[:, None, None], gotten, jnp.zeros((), gotten.dtype))

    def collect(terms):
        flat = terms.reshape(buffer_len, -1)
        summed = jnp.dot(
            collect_map, flat, precision=lax.Precision.HIGHEST, preferred_element_type=jnp.float32
        )
        return summed.reshape(block_rows, terms.shape[1], block_len)

    def give_back(mirror):
        placed = (
            jnp.zeros((buffer_len,) + mirror.shape[1:], jnp.float32)
            .at[place_at]
            .set(mirror, mode="drop")
        )
        arrived = lax.all_to_all(
            placed.reshape(row_count, capacity, mirror.shape[1], block_len),
            "rows",
            split_axis=0,
            concat_axis=0,
            tiled=True,
        )
        return collect(arrived.reshape(buffer_len, mirror.shape[1], block_len))

    def column_total(partial_value):
        return allsum(partial_value, "cols", 1 if partial_value.shape[1] == 1 else 2)

    def global_sum(values):
        return allsum(values, "rows", 0)

    own_x = points.reshape(coord_dim, block_rows, block_len).transpose(1, 0, 2)
    far_x = serve(own_x)
    grouped_x = own_x.reshape(turn_count, turn_rows, coord_dim, block_len)
    grouped_far = far_x.reshape(turn_count, turn_rows * slot_width, coord_dim, block_len)
    grouped_live = is_live.reshape(turn_count, turn_rows * slot_width)
    grouped_off = off_diag.reshape(turn_count, turn_rows * slot_width)

    def row_pass(own_w, far_w):

        def row_step(pieces):
            near_x, remote_x, live_now, off_now = (pieces[0], pieces[1], pieces[2], pieces[3])
            values = jnp.where(
                live_now[:, None, None],
                wendland(jnp.repeat(near_x, slot_width, axis=0), remote_x),
                0.0,
            )
            if own_w is None:
                direct = jnp.sum(
                    jnp.sum(values, axis=2).reshape(turn_rows, slot_width, block_len), axis=1
                )[:, None, :]
                mirror = jnp.where(off_now[:, None], jnp.sum(values, axis=1), 0.0)[:, None, :]
                return (direct, mirror)
            kernel_bf = values.astype(jnp.bfloat16)
            direct = jnp.einsum(
                "nab,nob->noa", kernel_bf, pieces[5], preferred_element_type=jnp.float32
            )
            direct = jnp.sum(direct.reshape(turn_rows, slot_width, outputs, block_len), axis=1)
            mirror = jnp.einsum(
                "nab,noa->nob",
                kernel_bf,
                jnp.repeat(pieces[4], slot_width, axis=0),
                preferred_element_type=jnp.float32,
            )
            return (direct, jnp.where(off_now[:, None, None], mirror, 0.0))

        pieces = (grouped_x, grouped_far, grouped_live, grouped_off)
        if own_w is not None:
            pieces = pieces + (
                own_w.reshape(turn_count, turn_rows, outputs, block_len),
                far_w.reshape(turn_count, turn_rows * slot_width, outputs, block_len),
            )
        results = lax.map(row_step, pieces)
        channels = results[0].shape[2]
        direct = results[0].reshape(block_rows, channels, block_len)
        return (direct, results[1].reshape(slot_count, channels, block_len))

    direct, mirror = row_pass(None, None)
    degree_part = direct + give_back(mirror)
    inv_root = 1.0 / jnp.sqrt(1.0 + column_total(degree_part))
    resid = targets.reshape(outputs, block_rows, block_len).transpose(1, 0, 2)
    direction = resid
    solution = jnp.zeros_like(resid)
    norm_now = global_sum(jnp.sum(resid * resid, axis=(0, 2)))
    for iteration in range(ITERS):
        weights = (direction * inv_root).astype(jnp.bfloat16)
        apply_far_w = serve(weights)
        apply_direct, apply_mirror = row_pass(weights, apply_far_w)
        apply_partial_value = apply_direct + give_back(apply_mirror)
        applied = REG * direction + inv_root * column_total(apply_partial_value)
        step_size = norm_now / global_sum(jnp.sum(direction * applied, axis=(0, 2)))
        solution = solution + step_size[None, :, None] * direction
        resid = resid - step_size[None, :, None] * applied
        if iteration + 1 < ITERS:
            norm_next = global_sum(jnp.sum(resid * resid, axis=(0, 2)))
            direction = resid + (norm_next / norm_now)[None, :, None] * direction
            norm_now = norm_next
    return (
        solution.transpose(1, 0, 2).reshape(outputs, npoints),
        resid.transpose(1, 0, 2).reshape(outputs, npoints),
    )


def solution(mesh):
    placed = (P("rows", "cols"), P(None, "rows"), P(None, "rows"))
    return jax.shard_map(
        local,
        mesh=mesh,
        in_specs=placed,
        out_specs=(P(None, "rows"), P(None, "rows")),
        check_vma=False,
    )
```

```python
import functools

import jax
import jax.numpy as jnp
from jax import lax
from jax.experimental import pallas as pl
from jax.experimental.pallas import tpu as pltpu
from jax.sharding import PartitionSpec as P

MESH = pl.DeviceIdType.MESH

ITERS = 2


REG = 1.5
RADIUS = 0.25


def wendland(left_x, right_x):
    left_f = left_x.astype(jnp.float32)
    right_f = right_x.astype(jnp.float32)
    left_sq = jnp.sum(left_f * left_f, axis=1)
    right_sq = jnp.sum(right_f * right_f, axis=1)
    inner_prod = jnp.einsum("nda,ndb->nab", left_f, right_f, precision=lax.Precision.HIGHEST)
    dist_sq = left_sq[:, :, None] + right_sq[:, None, :] - 2.0 * inner_prod
    scaled = jnp.sqrt(jnp.maximum(dist_sq, 0.0)) / RADIUS
    remain = jnp.maximum(1.0 - scaled, 0.0)
    square = remain * remain
    return square * square * (4.0 * scaled + 1.0)


def allsum_kernel(axis, n, x_ref, o_ref, recv, send_sem, recv_sem):
    me = lax.axis_index(axis)
    barrier = pltpu.get_barrier_semaphore()

    def greet(k, carry):
        peer = lax.rem(me + k, n)
        pl.semaphore_signal(barrier, inc=1, device_id={axis: peer}, device_id_type=MESH)
        return carry

    lax.fori_loop(1, n, greet, 0)
    pl.semaphore_wait(barrier, n - 1)

    def outgoing(peer):
        return pltpu.make_async_remote_copy(
            src_ref=x_ref,
            dst_ref=recv.at[me],
            send_sem=send_sem.at[peer],
            recv_sem=recv_sem.at[me],
            device_id={axis: peer},
            device_id_type=MESH,
        )

    def incoming(peer):
        return pltpu.make_async_remote_copy(
            src_ref=x_ref,
            dst_ref=recv.at[peer],
            send_sem=send_sem.at[peer],
            recv_sem=recv_sem.at[peer],
            device_id={axis: peer},
            device_id_type=MESH,
        )

    def start(k, carry):
        outgoing(lax.rem(me + k, n)).start()
        return carry

    lax.fori_loop(1, n, start, 0)
    recv[me] = x_ref[...]

    def finish(k, carry):
        peer = lax.rem(me + k, n)
        outgoing(peer).wait_send()
        incoming(peer).wait_recv()
        return carry

    lax.fori_loop(1, n, finish, 0)
    o_ref[...] = recv[0]

    def add(s, carry):
        o_ref[...] += recv[s]
        return carry

    lax.fori_loop(1, n, add, 0)


def allsum(x, axis, cid):
    n = lax.axis_size(axis)
    shape = x.shape
    flat = x.reshape(-1)
    size = flat.shape[0]
    if size <= 128:
        tile = jnp.pad(flat, (0, 128 - size)).reshape(1, 128)
    elif size % 1024 == 0:
        tile = flat.reshape(size // 128, 128)
    else:
        rows_pad = -(-size // 1024) * 8
        tile = jnp.pad(flat, (0, rows_pad * 128 - size)).reshape(rows_pad, 128)
    out = pl.pallas_call(
        functools.partial(allsum_kernel, axis, n),
        out_shape=jax.ShapeDtypeStruct(tile.shape, jnp.float32),
        in_specs=[pl.BlockSpec(memory_space=pltpu.VMEM)],
        out_specs=pl.BlockSpec(memory_space=pltpu.VMEM),
        scratch_shapes=[
            pltpu.VMEM((n,) + tile.shape, jnp.float32),
            pltpu.SemaphoreType.DMA((n,)),
            pltpu.SemaphoreType.DMA((n,)),
        ],
        compiler_params=pltpu.CompilerParams(collective_id=cid, has_side_effects=True),
    )(tile)
    return out.reshape(-1)[:size].reshape(shape)


def local(block_list, points, targets):
    row_count = lax.axis_size("rows")
    row_index = lax.axis_index("rows")
    block_rows, slot_width = block_list.shape
    coord_dim, npoints = points.shape
    outputs = targets.shape[0]
    block_len = npoints // block_rows
    slot_count = block_rows * slot_width
    capacity = (slot_count + row_count - 1) // row_count
    buffer_len = row_count * capacity
    turn_rows = 4
    turn_count = block_rows // turn_rows
    entries = block_list.reshape(slot_count)
    is_live = entries >= 0
    owners = jnp.where(is_live, entries // block_rows, 0)
    local_idx = jnp.where(is_live, entries - owners * block_rows, 0)
    first_row = row_index * block_rows
    row_global = first_row + jnp.arange(slot_count, dtype=jnp.int32) // slot_width
    off_diag = is_live & (entries != row_global)
    owner_hits = (
        (owners[:, None] == jnp.arange(row_count, dtype=jnp.int32)[None, :]) & is_live[:, None]
    ).astype(jnp.int32)
    slot_rank = jnp.sum((jnp.cumsum(owner_hits, axis=0) - owner_hits) * owner_hits, axis=1)
    place_at = jnp.where(is_live, owners * capacity + slot_rank, buffer_len)
    pick_at = jnp.minimum(place_at, buffer_len - 1)
    wanted = jnp.full((buffer_len,), -1, jnp.int32).at[place_at].set(local_idx, mode="drop")
    askers = jnp.full((buffer_len,), -1, jnp.int32).at[place_at].set(row_global, mode="drop")
    request = jnp.stack([wanted, askers], axis=1).reshape(row_count, capacity, 2)
    incoming = lax.all_to_all(request, "rows", split_axis=0, concat_axis=0, tiled=True).reshape(
        buffer_len, 2
    )
    in_live = incoming[:, 0] >= 0
    in_idx = jnp.maximum(incoming[:, 0], 0)
    collect_map = (
        (in_idx[None, :] == jnp.arange(block_rows, dtype=jnp.int32)[:, None]) & in_live[None, :]
    ).astype(jnp.float32)

    def serve(blocks):
        chosen = jnp.where(in_live[:, None, None], blocks[in_idx], jnp.zeros((), blocks.dtype))
        arrived = lax.all_to_all(
            chosen.reshape(row_count, capacity, blocks.shape[1], block_len),
            "rows",
            split_axis=0,
            concat_axis=0,
            tiled=True,
        )
        gotten = arrived.reshape(buffer_len, blocks.shape[1], block_len)[pick_at]
        return jnp.where(is_live[:, None, None], gotten, jnp.zeros((), gotten.dtype))

    def collect(terms):
        flat = terms.reshape(buffer_len, -1)
        summed = jnp.dot(
            collect_map, flat, precision=lax.Precision.HIGHEST, preferred_element_type=jnp.float32
        )
        return summed.reshape(block_rows, terms.shape[1], block_len)

    def give_back(mirror):
        placed = (
            jnp.zeros((buffer_len,) + mirror.shape[1:], jnp.float32)
            .at[place_at]
            .set(mirror, mode="drop")
        )
        arrived = lax.all_to_all(
            placed.reshape(row_count, capacity, mirror.shape[1], block_len),
            "rows",
            split_axis=0,
            concat_axis=0,
            tiled=True,
        )
        return collect(arrived.reshape(buffer_len, mirror.shape[1], block_len))

    def column_total(partial_value):
        return allsum(partial_value, "cols", 1 if partial_value.shape[1] == 1 else 2)

    def global_sum(values):
        return allsum(values, "rows", 0)

    own_x = points.reshape(coord_dim, block_rows, block_len).transpose(1, 0, 2)
    far_x = serve(own_x)
    grouped_x = own_x.reshape(turn_count, turn_rows, coord_dim, block_len)
    grouped_far = far_x.reshape(turn_count, turn_rows * slot_width, coord_dim, block_len)
    grouped_live = is_live.reshape(turn_count, turn_rows * slot_width)
    grouped_off = off_diag.reshape(turn_count, turn_rows * slot_width)

    def row_pass(own_w, far_w):

        def row_step(pieces):
            near_x, remote_x, live_now, off_now = (pieces[0], pieces[1], pieces[2], pieces[3])
            values = jnp.where(
                live_now[:, None, None],
                wendland(jnp.repeat(near_x, slot_width, axis=0), remote_x),
                0.0,
            )
            if own_w is None:
                direct = jnp.sum(
                    jnp.sum(values, axis=2).reshape(turn_rows, slot_width, block_len), axis=1
                )[:, None, :]
                mirror = jnp.where(off_now[:, None], jnp.sum(values, axis=1), 0.0)[:, None, :]
                return (direct, mirror)
            kernel_bf = values.astype(jnp.bfloat16)
            direct = jnp.einsum(
                "nab,nob->noa", kernel_bf, pieces[5], preferred_element_type=jnp.float32
            )
            direct = jnp.sum(direct.reshape(turn_rows, slot_width, outputs, block_len), axis=1)
            mirror = jnp.einsum(
                "nab,noa->nob",
                kernel_bf,
                jnp.repeat(pieces[4], slot_width, axis=0),
                preferred_element_type=jnp.float32,
            )
            return (direct, jnp.where(off_now[:, None, None], mirror, 0.0))

        pieces = (grouped_x, grouped_far, grouped_live, grouped_off)
        if own_w is not None:
            pieces = pieces + (
                own_w.reshape(turn_count, turn_rows, outputs, block_len),
                far_w.reshape(turn_count, turn_rows * slot_width, outputs, block_len),
            )
        results = lax.map(row_step, pieces)
        channels = results[0].shape[2]
        direct = results[0].reshape(block_rows, channels, block_len)
        return (direct, results[1].reshape(slot_count, channels, block_len))

    direct, mirror = row_pass(None, None)
    degree_part = direct + give_back(mirror)
    inv_root = 1.0 / jnp.sqrt(1.0 + column_total(degree_part))
    resid = targets.reshape(outputs, block_rows, block_len).transpose(1, 0, 2)
    direction = resid
    solution = jnp.zeros_like(resid)
    norm_now = jnp.sum(resid * resid, axis=(0, 2))
    for iteration in range(ITERS):
        weights = (direction * inv_root).astype(jnp.bfloat16)
        apply_far_w = serve(weights)
        apply_direct, apply_mirror = row_pass(weights, apply_far_w)
        apply_partial_value = apply_direct + give_back(apply_mirror)
        applied = REG * direction + inv_root * column_total(apply_partial_value)
        curvature = jnp.sum(direction * applied, axis=(0, 2))
        if iteration == 0:
            both = global_sum(jnp.concatenate([norm_now, curvature]))
            norm_now, curvature = both[:outputs], both[outputs:]
        else:
            curvature = global_sum(curvature)
        step_size = norm_now / curvature
        solution = solution + step_size[None, :, None] * direction
        resid = resid - step_size[None, :, None] * applied
        if iteration + 1 < ITERS:
            norm_next = global_sum(jnp.sum(resid * resid, axis=(0, 2)))
            direction = resid + (norm_next / norm_now)[None, :, None] * direction
            norm_now = norm_next
    return (
        solution.transpose(1, 0, 2).reshape(outputs, npoints),
        resid.transpose(1, 0, 2).reshape(outputs, npoints),
    )


def solution(mesh):
    placed = (P("rows", "cols"), P(None, "rows"), P(None, "rows"))
    return jax.shard_map(
        local,
        mesh=mesh,
        in_specs=placed,
        out_specs=(P(None, "rows"), P(None, "rows")),
        check_vma=False,
    )
```

```python
import functools

import jax
import jax.numpy as jnp
from jax import lax
from jax.experimental import pallas as pl
from jax.experimental.pallas import tpu as pltpu
from jax.sharding import PartitionSpec as P

MESH = pl.DeviceIdType.MESH

ITERS = 2


REG = 1.5
RADIUS = 0.25


def wendland(left_x, right_x):
    left_f = left_x.astype(jnp.float32)
    right_f = right_x.astype(jnp.float32)
    left_sq = jnp.sum(left_f * left_f, axis=1)
    right_sq = jnp.sum(right_f * right_f, axis=1)
    inner_prod = jnp.einsum("nda,ndb->nab", left_f, right_f, precision=lax.Precision.HIGHEST)
    dist_sq = left_sq[:, :, None] + right_sq[:, None, :] - 2.0 * inner_prod
    scaled = jnp.sqrt(jnp.maximum(dist_sq, 0.0)) / RADIUS
    remain = jnp.maximum(1.0 - scaled, 0.0)
    square = remain * remain
    return square * square * (4.0 * scaled + 1.0)


def allsum_kernel(axis, n, x_ref, o_ref, recv, send_sem, recv_sem):
    me = lax.axis_index(axis)
    barrier = pltpu.get_barrier_semaphore()

    def greet(k, carry):
        peer = lax.rem(me + k, n)
        pl.semaphore_signal(barrier, inc=1, device_id={axis: peer}, device_id_type=MESH)
        return carry

    lax.fori_loop(1, n, greet, 0)
    pl.semaphore_wait(barrier, n - 1)

    def outgoing(peer):
        return pltpu.make_async_remote_copy(
            src_ref=x_ref,
            dst_ref=recv.at[me],
            send_sem=send_sem.at[peer],
            recv_sem=recv_sem.at[me],
            device_id={axis: peer},
            device_id_type=MESH,
        )

    def incoming(peer):
        return pltpu.make_async_remote_copy(
            src_ref=x_ref,
            dst_ref=recv.at[peer],
            send_sem=send_sem.at[peer],
            recv_sem=recv_sem.at[peer],
            device_id={axis: peer},
            device_id_type=MESH,
        )

    def start(k, carry):
        outgoing(lax.rem(me + k, n)).start()
        return carry

    lax.fori_loop(1, n, start, 0)
    recv[me] = x_ref[...]

    def finish(k, carry):
        peer = lax.rem(me + k, n)
        outgoing(peer).wait_send()
        incoming(peer).wait_recv()
        return carry

    lax.fori_loop(1, n, finish, 0)
    o_ref[...] = recv[0]

    def add(s, carry):
        o_ref[...] += recv[s]
        return carry

    lax.fori_loop(1, n, add, 0)


def allsum(x, axis, cid):
    n = lax.axis_size(axis)
    shape = x.shape
    flat = x.reshape(-1)
    size = flat.shape[0]
    if size <= 128:
        tile = jnp.pad(flat, (0, 128 - size)).reshape(1, 128)
    elif size % 1024 == 0:
        tile = flat.reshape(size // 128, 128)
    else:
        rows_pad = -(-size // 1024) * 8
        tile = jnp.pad(flat, (0, rows_pad * 128 - size)).reshape(rows_pad, 128)
    out = pl.pallas_call(
        functools.partial(allsum_kernel, axis, n),
        out_shape=jax.ShapeDtypeStruct(tile.shape, jnp.float32),
        in_specs=[pl.BlockSpec(memory_space=pltpu.VMEM)],
        out_specs=pl.BlockSpec(memory_space=pltpu.VMEM),
        scratch_shapes=[
            pltpu.VMEM((n,) + tile.shape, jnp.float32),
            pltpu.SemaphoreType.DMA((n,)),
            pltpu.SemaphoreType.DMA((n,)),
        ],
        compiler_params=pltpu.CompilerParams(collective_id=cid, has_side_effects=True),
    )(tile)
    return out.reshape(-1)[:size].reshape(shape)


def local(block_list, points, targets):
    row_count = lax.axis_size("rows")
    row_index = lax.axis_index("rows")
    block_rows, slot_width = block_list.shape
    coord_dim, npoints = points.shape
    outputs = targets.shape[0]
    block_len = npoints // block_rows
    slot_count = block_rows * slot_width
    entries = block_list.reshape(slot_count)
    is_live = entries >= 0
    owners = jnp.where(is_live, entries // block_rows, 0)
    local_idx = jnp.where(is_live, entries - owners * block_rows, 0)
    slot_row = jnp.arange(slot_count, dtype=jnp.int32) // slot_width
    first_row = row_index * block_rows
    place_at = jnp.where(is_live, owners, row_count)
    pick_at = jnp.minimum(place_at, row_count - 1)
    wanted = jnp.full((row_count,), -1, jnp.int32).at[place_at].set(local_idx, mode="drop")
    asking_row = jnp.full((row_count,), -1, jnp.int32).at[place_at].set(slot_row, mode="drop")
    ask_live = asking_row >= 0
    ask_row = jnp.maximum(asking_row, 0)
    request = jnp.stack([wanted, asking_row], axis=1).reshape(row_count, 1, 2)
    incoming = lax.all_to_all(request, "rows", split_axis=0, concat_axis=0, tiled=True).reshape(
        row_count, 2
    )
    in_live = incoming[:, 0] >= 0
    in_idx = jnp.maximum(incoming[:, 0], 0)
    their_row = jnp.arange(row_count, dtype=jnp.int32) * block_rows + jnp.maximum(incoming[:, 1], 0)
    in_off = in_live & (their_row != first_row + in_idx)
    collect_map = (
        (in_idx[None, :] == jnp.arange(block_rows, dtype=jnp.int32)[:, None]) & in_off[None, :]
    ).astype(jnp.float32)

    def swap(parts):
        return lax.all_to_all(parts, "rows", split_axis=0, concat_axis=0, tiled=True)

    def asked_part(blocks):
        return jnp.where(ask_live[:, None, None], blocks[ask_row], jnp.zeros((), blocks.dtype))

    def served_part(blocks):
        return jnp.where(in_live[:, None, None], blocks[in_idx], jnp.zeros((), blocks.dtype))

    def per_slot(got):
        chosen = got[pick_at]
        return jnp.where(is_live[:, None, None], chosen, jnp.zeros((), chosen.dtype))

    def collect(terms):
        flat = terms.reshape(row_count, -1)
        summed = jnp.dot(
            collect_map, flat, precision=lax.Precision.HIGHEST, preferred_element_type=jnp.float32
        )
        return summed.reshape((block_rows,) + terms.shape[1:])

    def column_total(partial_value):
        return allsum(partial_value, "cols", 1 if partial_value.shape[1] == 1 else 2)

    def global_sum(values):
        return allsum(values, "rows", 0)

    own_x = points.reshape(coord_dim, block_rows, block_len).transpose(1, 0, 2)
    their_x = swap(asked_part(own_x))
    far_x = per_slot(swap(served_part(own_x)))
    left_x = jnp.concatenate([own_x[slot_row], their_x], axis=0)
    right_x = jnp.concatenate([far_x, own_x[in_idx]], axis=0)
    pair_live = jnp.concatenate([is_live, in_off], axis=0)
    pair_count = slot_count + row_count
    chunk = 16
    pad = (-pair_count) % chunk
    left_x = jnp.pad(left_x, ((0, pad), (0, 0), (0, 0)))
    right_x = jnp.pad(right_x, ((0, pad), (0, 0), (0, 0)))
    pair_live = jnp.pad(pair_live, (0, pad))

    def pair_step(pieces):
        lx, rx, live = pieces
        values = jnp.where(live[:, None, None], wendland(lx, rx), 0.0)
        return (values.astype(jnp.bfloat16), jnp.sum(values, axis=2), jnp.sum(values, axis=1))

    kernel_bf, row_sums, col_sums = lax.map(
        pair_step,
        (
            left_x.reshape(-1, chunk, coord_dim, block_len),
            right_x.reshape(-1, chunk, coord_dim, block_len),
            pair_live.reshape(-1, chunk),
        ),
    )
    kernel_bf = kernel_bf.reshape(-1, block_len, block_len)
    row_sums = row_sums.reshape(-1, block_len)
    col_sums = col_sums.reshape(-1, block_len)
    own_k = kernel_bf[:slot_count]
    in_k = kernel_bf[slot_count:pair_count]
    degree_direct = jnp.sum(row_sums[:slot_count].reshape(block_rows, slot_width, block_len), axis=1)
    degree_mirror = collect(col_sums[slot_count:pair_count])
    degree_part = (degree_direct + degree_mirror)[:, None, :]
    inv_root = 1.0 / jnp.sqrt(1.0 + column_total(degree_part))

    def apply_partial(weights):
        got = swap(jnp.stack([asked_part(weights), served_part(weights)], axis=1))
        their_w = got[:, 0]
        far_w = per_slot(got[:, 1])
        direct = jnp.einsum("sab,sob->soa", own_k, far_w, preferred_element_type=jnp.float32)
        direct = jnp.sum(direct.reshape(block_rows, slot_width, outputs, block_len), axis=1)
        mirror = jnp.einsum("eab,eoa->eob", in_k, their_w, preferred_element_type=jnp.float32)
        return direct + collect(mirror)

    resid = targets.reshape(outputs, block_rows, block_len).transpose(1, 0, 2)
    direction = resid
    solution = jnp.zeros_like(resid)
    norm_now = jnp.sum(resid * resid, axis=(0, 2))
    for iteration in range(ITERS):
        weights = (direction * inv_root).astype(jnp.bfloat16)
        applied = REG * direction + inv_root * column_total(apply_partial(weights))
        curvature = jnp.sum(direction * applied, axis=(0, 2))
        if iteration == 0:
            both = global_sum(jnp.concatenate([norm_now, curvature]))
            norm_now, curvature = both[:outputs], both[outputs:]
        else:
            curvature = global_sum(curvature)
        step_size = norm_now / curvature
        solution = solution + step_size[None, :, None] * direction
        resid = resid - step_size[None, :, None] * applied
        if iteration + 1 < ITERS:
            norm_next = global_sum(jnp.sum(resid * resid, axis=(0, 2)))
            direction = resid + (norm_next / norm_now)[None, :, None] * direction
            norm_now = norm_next
    return (
        solution.transpose(1, 0, 2).reshape(outputs, npoints),
        resid.transpose(1, 0, 2).reshape(outputs, npoints),
    )


def solution(mesh):
    placed = (P("rows", "cols"), P(None, "rows"), P(None, "rows"))
    return jax.shard_map(
        local,
        mesh=mesh,
        in_specs=placed,
        out_specs=(P(None, "rows"), P(None, "rows")),
        check_vma=False,
    )
```

```python
import functools

import jax
import jax.numpy as jnp
from jax import lax
from jax.experimental import pallas as pl
from jax.experimental.pallas import tpu as pltpu
from jax.sharding import PartitionSpec as P

MESH = pl.DeviceIdType.MESH

ITERS = 2


REG = 1.5
RADIUS = 0.25


def wendland(left_x, right_x):
    left_f = left_x.astype(jnp.float32)
    right_f = right_x.astype(jnp.float32)
    left_sq = jnp.sum(left_f * left_f, axis=1)
    right_sq = jnp.sum(right_f * right_f, axis=1)
    inner_prod = jnp.einsum("nda,ndb->nab", left_f, right_f, precision=lax.Precision.HIGHEST)
    dist_sq = left_sq[:, :, None] + right_sq[:, None, :] - 2.0 * inner_prod
    scaled = jnp.sqrt(jnp.maximum(dist_sq, 0.0)) / RADIUS
    remain = jnp.maximum(1.0 - scaled, 0.0)
    square = remain * remain
    return square * square * (4.0 * scaled + 1.0)


def allsum_kernel(axis, n, x_ref, o_ref, recv, send_sem, recv_sem):
    me = lax.axis_index(axis)
    barrier = pltpu.get_barrier_semaphore()

    def greet(k, carry):
        peer = lax.rem(me + k, n)
        pl.semaphore_signal(barrier, inc=1, device_id={axis: peer}, device_id_type=MESH)
        return carry

    lax.fori_loop(1, n, greet, 0)
    pl.semaphore_wait(barrier, n - 1)

    def outgoing(peer):
        return pltpu.make_async_remote_copy(
            src_ref=x_ref,
            dst_ref=recv.at[me],
            send_sem=send_sem.at[peer],
            recv_sem=recv_sem.at[me],
            device_id={axis: peer},
            device_id_type=MESH,
        )

    def incoming(peer):
        return pltpu.make_async_remote_copy(
            src_ref=x_ref,
            dst_ref=recv.at[peer],
            send_sem=send_sem.at[peer],
            recv_sem=recv_sem.at[peer],
            device_id={axis: peer},
            device_id_type=MESH,
        )

    def start(k, carry):
        outgoing(lax.rem(me + k, n)).start()
        return carry

    lax.fori_loop(1, n, start, 0)
    recv[me] = x_ref[...]

    def finish(k, carry):
        peer = lax.rem(me + k, n)
        outgoing(peer).wait_send()
        incoming(peer).wait_recv()
        return carry

    lax.fori_loop(1, n, finish, 0)
    o_ref[...] = recv[0]

    def add(s, carry):
        o_ref[...] += recv[s]
        return carry

    lax.fori_loop(1, n, add, 0)


def allsum(x, axis, cid):
    n = lax.axis_size(axis)
    shape = x.shape
    flat = x.reshape(-1)
    size = flat.shape[0]
    if size <= 128:
        tile = jnp.pad(flat, (0, 128 - size)).reshape(1, 128)
    elif size % 1024 == 0:
        tile = flat.reshape(size // 128, 128)
    else:
        rows_pad = -(-size // 1024) * 8
        tile = jnp.pad(flat, (0, rows_pad * 128 - size)).reshape(rows_pad, 128)
    out = pl.pallas_call(
        functools.partial(allsum_kernel, axis, n),
        out_shape=jax.ShapeDtypeStruct(tile.shape, jnp.float32),
        in_specs=[pl.BlockSpec(memory_space=pltpu.VMEM)],
        out_specs=pl.BlockSpec(memory_space=pltpu.VMEM),
        scratch_shapes=[
            pltpu.VMEM((n,) + tile.shape, jnp.float32),
            pltpu.SemaphoreType.DMA((n,)),
            pltpu.SemaphoreType.DMA((n,)),
        ],
        compiler_params=pltpu.CompilerParams(collective_id=cid, has_side_effects=True),
    )(tile)
    return out.reshape(-1)[:size].reshape(shape)


def swap_kernel(axis, n, count, *refs):
    ins, outs = refs[:count], refs[count:2 * count]
    landed = refs[2 * count:3 * count]
    send_sem, recv_sem = refs[3 * count:]
    me = lax.axis_index(axis)
    barrier = pltpu.get_barrier_semaphore()

    def greet(k, carry):
        peer = lax.rem(me + k, n)
        pl.semaphore_signal(barrier, inc=1, device_id={axis: peer}, device_id_type=MESH)
        return carry

    lax.fori_loop(1, n, greet, 0)
    pl.semaphore_wait(barrier, n - 1)

    def outgoing(a, peer):
        return pltpu.make_async_remote_copy(
            src_ref=ins[a].at[peer],
            dst_ref=landed[a].at[me],
            send_sem=send_sem.at[a, peer],
            recv_sem=recv_sem.at[a, me],
            device_id={axis: peer},
            device_id_type=MESH,
        )

    def incoming(a, peer):
        return pltpu.make_async_remote_copy(
            src_ref=ins[a].at[peer],
            dst_ref=landed[a].at[peer],
            send_sem=send_sem.at[a, peer],
            recv_sem=recv_sem.at[a, peer],
            device_id={axis: peer},
            device_id_type=MESH,
        )

    def start(k, carry):
        peer = lax.rem(me + k, n)
        for a in range(count):
            outgoing(a, peer).start()
        return carry

    lax.fori_loop(1, n, start, 0)
    for a in range(count):
        landed[a][me] = ins[a][me]

    def finish(k, carry):
        peer = lax.rem(me + k, n)
        for a in range(count):
            outgoing(a, peer).wait_send()
            incoming(a, peer).wait_recv()
        return carry

    lax.fori_loop(1, n, finish, 0)
    for a in range(count):
        outs[a][...] = landed[a][...]


def swap_all(arrays, axis, cid):
    n = lax.axis_size(axis)
    count = len(arrays)
    vmem = pl.BlockSpec(memory_space=pltpu.VMEM)
    return pl.pallas_call(
        functools.partial(swap_kernel, axis, n, count),
        out_shape=[jax.ShapeDtypeStruct(a.shape, a.dtype) for a in arrays],
        in_specs=[vmem] * count,
        out_specs=[vmem] * count,
        scratch_shapes=[pltpu.VMEM(a.shape, a.dtype) for a in arrays]
        + [pltpu.SemaphoreType.DMA((count, n)), pltpu.SemaphoreType.DMA((count, n))],
        compiler_params=pltpu.CompilerParams(collective_id=cid, has_side_effects=True),
    )(*arrays)


def local(block_list, points, targets):
    row_count = lax.axis_size("rows")
    row_index = lax.axis_index("rows")
    block_rows, slot_width = block_list.shape
    coord_dim, npoints = points.shape
    outputs = targets.shape[0]
    block_len = npoints // block_rows
    slot_count = block_rows * slot_width
    entries = block_list.reshape(slot_count)
    is_live = entries >= 0
    owners = jnp.where(is_live, entries // block_rows, 0)
    local_idx = jnp.where(is_live, entries - owners * block_rows, 0)
    slot_row = jnp.arange(slot_count, dtype=jnp.int32) // slot_width
    first_row = row_index * block_rows
    place_at = jnp.where(is_live, owners, row_count)
    pick_at = jnp.minimum(place_at, row_count - 1)
    wanted = jnp.full((row_count,), -1, jnp.int32).at[place_at].set(local_idx, mode="drop")
    asking_row = jnp.full((row_count,), -1, jnp.int32).at[place_at].set(slot_row, mode="drop")
    ask_live = asking_row >= 0
    ask_row = jnp.maximum(asking_row, 0)
    request = jnp.zeros((row_count, 8, 128), jnp.int32)
    request = request.at[:, 0, 0].set(wanted).at[:, 0, 1].set(asking_row)
    own_x = points.reshape(coord_dim, block_rows, block_len).transpose(1, 0, 2)
    asked_x = jnp.where(ask_live[:, None, None], own_x[ask_row], jnp.zeros((), own_x.dtype))
    got_request, their_x = swap_all([request, asked_x], "rows", 3)
    incoming = got_request[:, 0, :2]
    in_live = incoming[:, 0] >= 0
    in_idx = jnp.maximum(incoming[:, 0], 0)
    their_row = jnp.arange(row_count, dtype=jnp.int32) * block_rows + jnp.maximum(incoming[:, 1], 0)
    in_off = in_live & (their_row != first_row + in_idx)
    collect_map = (
        (in_idx[None, :] == jnp.arange(block_rows, dtype=jnp.int32)[:, None]) & in_off[None, :]
    ).astype(jnp.float32)

    def swap(parts, cid):
        shape = parts.shape
        flat = parts.reshape(shape[0], -1, shape[-1])
        return swap_all([flat], "rows", cid)[0].reshape(shape)

    def asked_part(blocks):
        return jnp.where(ask_live[:, None, None], blocks[ask_row], jnp.zeros((), blocks.dtype))

    def served_part(blocks):
        return jnp.where(in_live[:, None, None], blocks[in_idx], jnp.zeros((), blocks.dtype))

    def per_slot(got):
        chosen = got[pick_at]
        return jnp.where(is_live[:, None, None], chosen, jnp.zeros((), chosen.dtype))

    def collect(terms):
        flat = terms.reshape(row_count, -1)
        summed = jnp.dot(
            collect_map, flat, precision=lax.Precision.HIGHEST, preferred_element_type=jnp.float32
        )
        return summed.reshape((block_rows,) + terms.shape[1:])

    def column_total(partial_value):
        return allsum(partial_value, "cols", 1 if partial_value.shape[1] == 1 else 2)

    def global_sum(values):
        return allsum(values, "rows", 0)

    far_x = per_slot(swap(served_part(own_x), 4))
    left_x = jnp.concatenate([own_x[slot_row], their_x], axis=0)
    right_x = jnp.concatenate([far_x, own_x[in_idx]], axis=0)
    pair_live = jnp.concatenate([is_live, in_off], axis=0)
    pair_count = slot_count + row_count
    chunk = 16
    pad = (-pair_count) % chunk
    left_x = jnp.pad(left_x, ((0, pad), (0, 0), (0, 0)))
    right_x = jnp.pad(right_x, ((0, pad), (0, 0), (0, 0)))
    pair_live = jnp.pad(pair_live, (0, pad))

    def pair_step(pieces):
        lx, rx, live = pieces
        values = jnp.where(live[:, None, None], wendland(lx, rx), 0.0)
        return (values.astype(jnp.bfloat16), jnp.sum(values, axis=2), jnp.sum(values, axis=1))

    kernel_bf, row_sums, col_sums = lax.map(
        pair_step,
        (
            left_x.reshape(-1, chunk, coord_dim, block_len),
            right_x.reshape(-1, chunk, coord_dim, block_len),
            pair_live.reshape(-1, chunk),
        ),
    )
    kernel_bf = kernel_bf.reshape(-1, block_len, block_len)
    row_sums = row_sums.reshape(-1, block_len)
    col_sums = col_sums.reshape(-1, block_len)
    own_k = kernel_bf[:slot_count]
    in_k = kernel_bf[slot_count:pair_count]
    degree_direct = jnp.sum(row_sums[:slot_count].reshape(block_rows, slot_width, block_len), axis=1)
    degree_mirror = collect(col_sums[slot_count:pair_count])
    degree_part = (degree_direct + degree_mirror)[:, None, :]
    inv_root = 1.0 / jnp.sqrt(1.0 + column_total(degree_part))

    def apply_partial(weights):
        got = swap(jnp.stack([asked_part(weights), served_part(weights)], axis=1), 5)
        their_w = got[:, 0]
        far_w = per_slot(got[:, 1])
        direct = jnp.einsum("sab,sob->soa", own_k, far_w, preferred_element_type=jnp.float32)
        direct = jnp.sum(direct.reshape(block_rows, slot_width, outputs, block_len), axis=1)
        mirror = jnp.einsum("eab,eoa->eob", in_k, their_w, preferred_element_type=jnp.float32)
        return direct + collect(mirror)

    resid = targets.reshape(outputs, block_rows, block_len).transpose(1, 0, 2)
    direction = resid
    solution = jnp.zeros_like(resid)
    norm_now = jnp.sum(resid * resid, axis=(0, 2))
    for iteration in range(ITERS):
        weights = (direction * inv_root).astype(jnp.bfloat16)
        applied = REG * direction + inv_root * column_total(apply_partial(weights))
        curvature = jnp.sum(direction * applied, axis=(0, 2))
        if iteration == 0:
            both = global_sum(jnp.concatenate([norm_now, curvature]))
            norm_now, curvature = both[:outputs], both[outputs:]
        else:
            curvature = global_sum(curvature)
        step_size = norm_now / curvature
        solution = solution + step_size[None, :, None] * direction
        resid = resid - step_size[None, :, None] * applied
        if iteration + 1 < ITERS:
            norm_next = global_sum(jnp.sum(resid * resid, axis=(0, 2)))
            direction = resid + (norm_next / norm_now)[None, :, None] * direction
            norm_now = norm_next
    return (
        solution.transpose(1, 0, 2).reshape(outputs, npoints),
        resid.transpose(1, 0, 2).reshape(outputs, npoints),
    )


def solution(mesh):
    placed = (P("rows", "cols"), P(None, "rows"), P(None, "rows"))
    return jax.shard_map(
        local,
        mesh=mesh,
        in_specs=placed,
        out_specs=(P(None, "rows"), P(None, "rows")),
        check_vma=False,
    )
```

```python
import functools

import jax
import jax.numpy as jnp
from jax import lax
from jax.experimental import pallas as pl
from jax.experimental.pallas import tpu as pltpu
from jax.sharding import PartitionSpec as P

MESH = pl.DeviceIdType.MESH

ITERS = 2


REG = 1.5
RADIUS = 0.25


def wendland(left_x, right_x):
    left_f = left_x.astype(jnp.float32)
    right_f = right_x.astype(jnp.float32)
    left_sq = jnp.sum(left_f * left_f, axis=1)
    right_sq = jnp.sum(right_f * right_f, axis=1)
    inner_prod = jnp.einsum("nda,ndb->nab", left_f, right_f, precision=lax.Precision.HIGHEST)
    dist_sq = left_sq[:, :, None] + right_sq[:, None, :] - 2.0 * inner_prod
    scaled = jnp.sqrt(jnp.maximum(dist_sq, 0.0)) / RADIUS
    remain = jnp.maximum(1.0 - scaled, 0.0)
    square = remain * remain
    return square * square * (4.0 * scaled + 1.0)


def allsum_kernel(axis, n, x_ref, o_ref, recv, send_sem, recv_sem):
    me = lax.axis_index(axis)
    barrier = pltpu.get_barrier_semaphore()

    def greet(k, carry):
        peer = lax.rem(me + k, n)
        pl.semaphore_signal(barrier, inc=1, device_id={axis: peer}, device_id_type=MESH)
        return carry

    lax.fori_loop(1, n, greet, 0)
    pl.semaphore_wait(barrier, n - 1)

    def outgoing(peer):
        return pltpu.make_async_remote_copy(
            src_ref=x_ref,
            dst_ref=recv.at[me],
            send_sem=send_sem.at[peer],
            recv_sem=recv_sem.at[me],
            device_id={axis: peer},
            device_id_type=MESH,
        )

    def incoming(peer):
        return pltpu.make_async_remote_copy(
            src_ref=x_ref,
            dst_ref=recv.at[peer],
            send_sem=send_sem.at[peer],
            recv_sem=recv_sem.at[peer],
            device_id={axis: peer},
            device_id_type=MESH,
        )

    def start(k, carry):
        outgoing(lax.rem(me + k, n)).start()
        return carry

    lax.fori_loop(1, n, start, 0)
    recv[me] = x_ref[...]

    def finish(k, carry):
        peer = lax.rem(me + k, n)
        outgoing(peer).wait_send()
        incoming(peer).wait_recv()
        return carry

    lax.fori_loop(1, n, finish, 0)
    o_ref[...] = recv[0]

    def add(s, carry):
        o_ref[...] += recv[s]
        return carry

    lax.fori_loop(1, n, add, 0)


def allsum(x, axis, cid):
    n = lax.axis_size(axis)
    shape = x.shape
    flat = x.reshape(-1)
    size = flat.shape[0]
    if size <= 128:
        tile = jnp.pad(flat, (0, 128 - size)).reshape(1, 128)
    elif size % 1024 == 0:
        tile = flat.reshape(size // 128, 128)
    else:
        rows_pad = -(-size // 1024) * 8
        tile = jnp.pad(flat, (0, rows_pad * 128 - size)).reshape(rows_pad, 128)
    out = pl.pallas_call(
        functools.partial(allsum_kernel, axis, n),
        out_shape=jax.ShapeDtypeStruct(tile.shape, jnp.float32),
        in_specs=[pl.BlockSpec(memory_space=pltpu.VMEM)],
        out_specs=pl.BlockSpec(memory_space=pltpu.VMEM),
        scratch_shapes=[
            pltpu.VMEM((n,) + tile.shape, jnp.float32),
            pltpu.SemaphoreType.DMA((n,)),
            pltpu.SemaphoreType.DMA((n,)),
        ],
        compiler_params=pltpu.CompilerParams(collective_id=cid, has_side_effects=True),
    )(tile)
    return out.reshape(-1)[:size].reshape(shape)


def local(block_list, points, targets):
    row_count = lax.axis_size("rows")
    row_index = lax.axis_index("rows")
    block_rows, slot_width = block_list.shape
    coord_dim, npoints = points.shape
    outputs = targets.shape[0]
    block_len = npoints // block_rows
    slot_count = block_rows * slot_width
    entries = block_list.reshape(slot_count)
    is_live = entries >= 0
    owners = jnp.where(is_live, entries // block_rows, 0)
    local_idx = jnp.where(is_live, entries - owners * block_rows, 0)
    slot_row = jnp.arange(slot_count, dtype=jnp.int32) // slot_width
    first_row = row_index * block_rows
    place_at = jnp.where(is_live, owners, row_count)
    pick_at = jnp.minimum(place_at, row_count - 1)
    wanted = jnp.full((row_count,), -1, jnp.int32).at[place_at].set(local_idx, mode="drop")
    asking_row = jnp.full((row_count,), -1, jnp.int32).at[place_at].set(slot_row, mode="drop")
    ask_live = asking_row >= 0
    ask_row = jnp.maximum(asking_row, 0)
    request = jnp.stack([wanted, asking_row], axis=1).reshape(row_count, 1, 2)
    incoming = lax.all_to_all(request, "rows", split_axis=0, concat_axis=0, tiled=True).reshape(
        row_count, 2
    )
    in_live = incoming[:, 0] >= 0
    in_idx = jnp.maximum(incoming[:, 0], 0)
    their_row = jnp.arange(row_count, dtype=jnp.int32) * block_rows + jnp.maximum(incoming[:, 1], 0)
    in_off = in_live & (their_row != first_row + in_idx)
    collect_map = (
        (in_idx[None, :] == jnp.arange(block_rows, dtype=jnp.int32)[:, None]) & in_off[None, :]
    ).astype(jnp.float32)

    def swap(parts):
        return lax.all_to_all(parts, "rows", split_axis=0, concat_axis=0, tiled=True)

    peer_ids = jnp.arange(row_count, dtype=jnp.int32)
    to_lower = (peer_ids <= row_index)[:, None, None]
    from_self = (peer_ids == row_index)[:, None, None]

    def both_ways(blocks):
        got = swap(jnp.where(to_lower, asked_part(blocks), served_part(blocks)))
        their = jnp.where(peer_ids[:, None, None] >= row_index, got, jnp.zeros((), got.dtype))
        served_self = blocks[in_idx[row_index]]
        far = jnp.where(from_self, served_self[None], got)
        return their, per_slot(far)

    def asked_part(blocks):
        return jnp.where(ask_live[:, None, None], blocks[ask_row], jnp.zeros((), blocks.dtype))

    def served_part(blocks):
        return jnp.where(in_live[:, None, None], blocks[in_idx], jnp.zeros((), blocks.dtype))

    def per_slot(got):
        chosen = got[pick_at]
        return jnp.where(is_live[:, None, None], chosen, jnp.zeros((), chosen.dtype))

    def collect(terms):
        flat = terms.reshape(row_count, -1)
        summed = jnp.dot(
            collect_map, flat, precision=lax.Precision.HIGHEST, preferred_element_type=jnp.float32
        )
        return summed.reshape((block_rows,) + terms.shape[1:])

    def column_total(partial_value):
        return allsum(partial_value, "cols", 1 if partial_value.shape[1] == 1 else 2)

    def global_sum(values):
        return allsum(values, "rows", 0)

    own_x = points.reshape(coord_dim, block_rows, block_len).transpose(1, 0, 2)
    their_x, far_x = both_ways(own_x)
    left_x = jnp.concatenate([own_x[slot_row], their_x], axis=0)
    right_x = jnp.concatenate([far_x, own_x[in_idx]], axis=0)
    pair_live = jnp.concatenate([is_live, in_off], axis=0)
    pair_count = slot_count + row_count
    chunk = 16
    pad = (-pair_count) % chunk
    left_x = jnp.pad(left_x, ((0, pad), (0, 0), (0, 0)))
    right_x = jnp.pad(right_x, ((0, pad), (0, 0), (0, 0)))
    pair_live = jnp.pad(pair_live, (0, pad))

    def pair_step(pieces):
        lx, rx, live = pieces
        values = jnp.where(live[:, None, None], wendland(lx, rx), 0.0)
        return (values.astype(jnp.bfloat16), jnp.sum(values, axis=2), jnp.sum(values, axis=1))

    kernel_bf, row_sums, col_sums = lax.map(
        pair_step,
        (
            left_x.reshape(-1, chunk, coord_dim, block_len),
            right_x.reshape(-1, chunk, coord_dim, block_len),
            pair_live.reshape(-1, chunk),
        ),
    )
    kernel_bf = kernel_bf.reshape(-1, block_len, block_len)
    row_sums = row_sums.reshape(-1, block_len)
    col_sums = col_sums.reshape(-1, block_len)
    own_k = kernel_bf[:slot_count]
    in_k = kernel_bf[slot_count:pair_count]
    degree_direct = jnp.sum(row_sums[:slot_count].reshape(block_rows, slot_width, block_len), axis=1)
    degree_mirror = collect(col_sums[slot_count:pair_count])
    degree_part = (degree_direct + degree_mirror)[:, None, :]
    inv_root = 1.0 / jnp.sqrt(1.0 + column_total(degree_part))

    def apply_partial(weights):
        their_w, far_w = both_ways(weights)
        direct = jnp.einsum("sab,sob->soa", own_k, far_w, preferred_element_type=jnp.float32)
        direct = jnp.sum(direct.reshape(block_rows, slot_width, outputs, block_len), axis=1)
        mirror = jnp.einsum("eab,eoa->eob", in_k, their_w, preferred_element_type=jnp.float32)
        return direct + collect(mirror)

    resid = targets.reshape(outputs, block_rows, block_len).transpose(1, 0, 2)
    direction = resid
    solution = jnp.zeros_like(resid)
    norm_now = jnp.sum(resid * resid, axis=(0, 2))
    for iteration in range(ITERS):
        weights = (direction * inv_root).astype(jnp.bfloat16)
        applied = REG * direction + inv_root * column_total(apply_partial(weights))
        curvature = jnp.sum(direction * applied, axis=(0, 2))
        if iteration == 0:
            both = global_sum(jnp.concatenate([norm_now, curvature]))
            norm_now, curvature = both[:outputs], both[outputs:]
        else:
            curvature = global_sum(curvature)
        step_size = norm_now / curvature
        solution = solution + step_size[None, :, None] * direction
        resid = resid - step_size[None, :, None] * applied
        if iteration + 1 < ITERS:
            norm_next = global_sum(jnp.sum(resid * resid, axis=(0, 2)))
            direction = resid + (norm_next / norm_now)[None, :, None] * direction
            norm_now = norm_next
    return (
        solution.transpose(1, 0, 2).reshape(outputs, npoints),
        resid.transpose(1, 0, 2).reshape(outputs, npoints),
    )


def solution(mesh):
    placed = (P("rows", "cols"), P(None, "rows"), P(None, "rows"))
    return jax.shard_map(
        local,
        mesh=mesh,
        in_specs=placed,
        out_specs=(P(None, "rows"), P(None, "rows")),
        check_vma=False,
    )
```

```python
import functools

import jax
import jax.numpy as jnp
from jax import lax
from jax.experimental import pallas as pl
from jax.experimental.pallas import tpu as pltpu
from jax.sharding import PartitionSpec as P

MESH = pl.DeviceIdType.MESH

ITERS = 2


REG = 1.5
RADIUS = 0.25


def wendland(left_x, right_x):
    left_f = left_x.astype(jnp.float32)
    right_f = right_x.astype(jnp.float32)
    left_sq = jnp.sum(left_f * left_f, axis=1)
    right_sq = jnp.sum(right_f * right_f, axis=1)
    inner_prod = jnp.einsum("nda,ndb->nab", left_f, right_f, precision=lax.Precision.HIGHEST)
    dist_sq = left_sq[:, :, None] + right_sq[:, None, :] - 2.0 * inner_prod
    scaled = jnp.sqrt(jnp.maximum(dist_sq, 0.0)) / RADIUS
    remain = jnp.maximum(1.0 - scaled, 0.0)
    square = remain * remain
    return square * square * (4.0 * scaled + 1.0)


def allsum_kernel(axis, n, x_ref, o_ref, recv, send_sem, recv_sem):
    me = lax.axis_index(axis)
    barrier = pltpu.get_barrier_semaphore()

    def greet(k, carry):
        peer = lax.rem(me + k, n)
        pl.semaphore_signal(barrier, inc=1, device_id={axis: peer}, device_id_type=MESH)
        return carry

    lax.fori_loop(1, n, greet, 0)
    pl.semaphore_wait(barrier, n - 1)

    def outgoing(peer):
        return pltpu.make_async_remote_copy(
            src_ref=x_ref,
            dst_ref=recv.at[me],
            send_sem=send_sem.at[peer],
            recv_sem=recv_sem.at[me],
            device_id={axis: peer},
            device_id_type=MESH,
        )

    def incoming(peer):
        return pltpu.make_async_remote_copy(
            src_ref=x_ref,
            dst_ref=recv.at[peer],
            send_sem=send_sem.at[peer],
            recv_sem=recv_sem.at[peer],
            device_id={axis: peer},
            device_id_type=MESH,
        )

    def start(k, carry):
        outgoing(lax.rem(me + k, n)).start()
        return carry

    lax.fori_loop(1, n, start, 0)
    recv[me] = x_ref[...]

    def finish(k, carry):
        peer = lax.rem(me + k, n)
        outgoing(peer).wait_send()
        incoming(peer).wait_recv()
        return carry

    lax.fori_loop(1, n, finish, 0)
    o_ref[...] = recv[0]

    def add(s, carry):
        o_ref[...] += recv[s]
        return carry

    lax.fori_loop(1, n, add, 0)


def allsum(x, axis, cid):
    n = lax.axis_size(axis)
    shape = x.shape
    flat = x.reshape(-1)
    size = flat.shape[0]
    if size <= 128:
        tile = jnp.pad(flat, (0, 128 - size)).reshape(1, 128)
    elif size % 1024 == 0:
        tile = flat.reshape(size // 128, 128)
    else:
        rows_pad = -(-size // 1024) * 8
        tile = jnp.pad(flat, (0, rows_pad * 128 - size)).reshape(rows_pad, 128)
    out = pl.pallas_call(
        functools.partial(allsum_kernel, axis, n),
        out_shape=jax.ShapeDtypeStruct(tile.shape, jnp.float32),
        in_specs=[pl.BlockSpec(memory_space=pltpu.VMEM)],
        out_specs=pl.BlockSpec(memory_space=pltpu.VMEM),
        scratch_shapes=[
            pltpu.VMEM((n,) + tile.shape, jnp.float32),
            pltpu.SemaphoreType.DMA((n,)),
            pltpu.SemaphoreType.DMA((n,)),
        ],
        compiler_params=pltpu.CompilerParams(collective_id=cid, has_side_effects=True),
    )(tile)
    return out.reshape(-1)[:size].reshape(shape)


def fused_kernel(n_rows, n_cols, z_ref, g_ref, zo_ref, go_ref, recv_z, recv_g, sems):
    row = lax.axis_index("rows")
    col = lax.axis_index("cols")
    total = n_rows * n_cols
    me = row * n_cols + col
    barrier = pltpu.get_barrier_semaphore()

    def peer_of(k):
        peer = lax.rem(me + k, total)
        return peer, (peer // n_cols, lax.rem(peer, n_cols))

    def greet(k, carry):
        _, device = peer_of(k)
        pl.semaphore_signal(barrier, inc=1, device_id=device, device_id_type=MESH)
        return carry

    lax.fori_loop(1, total, greet, 0)
    pl.semaphore_wait(barrier, total - 1)
    z_send, z_recv, g_send, g_recv = sems

    def z_copy(peer, slot):
        return pltpu.make_async_remote_copy(
            src_ref=z_ref,
            dst_ref=recv_z.at[slot],
            send_sem=z_send.at[peer],
            recv_sem=z_recv.at[slot],
            device_id={"cols": peer},
            device_id_type=MESH,
        )

    def g_copy(peer, slot):
        return pltpu.make_async_remote_copy(
            src_ref=g_ref,
            dst_ref=recv_g.at[slot],
            send_sem=g_send.at[peer],
            recv_sem=g_recv.at[slot],
            device_id=(peer // n_cols, lax.rem(peer, n_cols)),
            device_id_type=MESH,
        )

    for k in range(1, n_cols):
        z_copy(lax.rem(col + k, n_cols), col).start()

    def start(k, carry):
        peer, _ = peer_of(k)
        g_copy(peer, me).start()
        return carry

    lax.fori_loop(1, total, start, 0)
    recv_z[col] = z_ref[...]
    recv_g[me] = g_ref[...]
    for k in range(1, n_cols):
        peer = lax.rem(col + k, n_cols)
        z_copy(peer, col).wait_send()
        z_copy(peer, peer).wait_recv()
    zo_ref[...] = recv_z[0]
    for k in range(1, n_cols):
        zo_ref[...] += recv_z[k]

    def finish(k, carry):
        peer, _ = peer_of(k)
        g_copy(peer, me).wait_send()
        g_copy(peer, peer).wait_recv()
        return carry

    lax.fori_loop(1, total, finish, 0)
    go_ref[...] = recv_g[0]

    def add(s, carry):
        go_ref[...] += recv_g[s]
        return carry

    lax.fori_loop(1, total, add, 0)


def fused_sum(z, g, cid):
    n_rows = lax.axis_size("rows")
    n_cols = lax.axis_size("cols")
    total = n_rows * n_cols
    z_tile = z.reshape(-1, z.shape[-1])
    size = g.shape[0]
    g_tile = jnp.pad(g, (0, 128 - size)).reshape(1, 128)
    vmem = pl.BlockSpec(memory_space=pltpu.VMEM)
    z_out, g_out = pl.pallas_call(
        functools.partial(fused_kernel, n_rows, n_cols),
        out_shape=[
            jax.ShapeDtypeStruct(z_tile.shape, jnp.float32),
            jax.ShapeDtypeStruct(g_tile.shape, jnp.float32),
        ],
        in_specs=[vmem, vmem],
        out_specs=[vmem, vmem],
        scratch_shapes=[
            pltpu.VMEM((n_cols,) + z_tile.shape, jnp.float32),
            pltpu.VMEM((total,) + g_tile.shape, jnp.float32),
            [
                pltpu.SemaphoreType.DMA((n_cols,)),
                pltpu.SemaphoreType.DMA((n_cols,)),
                pltpu.SemaphoreType.DMA((total,)),
                pltpu.SemaphoreType.DMA((total,)),
            ],
        ],
        compiler_params=pltpu.CompilerParams(collective_id=cid, has_side_effects=True),
    )(z_tile, g_tile)
    return z_out.reshape(z.shape), g_out.reshape(-1)[:size]


def local(block_list, points, targets):
    row_count = lax.axis_size("rows")
    row_index = lax.axis_index("rows")
    block_rows, slot_width = block_list.shape
    coord_dim, npoints = points.shape
    outputs = targets.shape[0]
    block_len = npoints // block_rows
    slot_count = block_rows * slot_width
    entries = block_list.reshape(slot_count)
    is_live = entries >= 0
    owners = jnp.where(is_live, entries // block_rows, 0)
    local_idx = jnp.where(is_live, entries - owners * block_rows, 0)
    slot_row = jnp.arange(slot_count, dtype=jnp.int32) // slot_width
    first_row = row_index * block_rows
    place_at = jnp.where(is_live, owners, row_count)
    pick_at = jnp.minimum(place_at, row_count - 1)
    wanted = jnp.full((row_count,), -1, jnp.int32).at[place_at].set(local_idx, mode="drop")
    asking_row = jnp.full((row_count,), -1, jnp.int32).at[place_at].set(slot_row, mode="drop")
    ask_live = asking_row >= 0
    ask_row = jnp.maximum(asking_row, 0)
    request = jnp.stack([wanted, asking_row], axis=1).reshape(row_count, 1, 2)
    incoming = lax.all_to_all(request, "rows", split_axis=0, concat_axis=0, tiled=True).reshape(
        row_count, 2
    )
    in_live = incoming[:, 0] >= 0
    in_idx = jnp.maximum(incoming[:, 0], 0)
    their_row = jnp.arange(row_count, dtype=jnp.int32) * block_rows + jnp.maximum(incoming[:, 1], 0)
    in_off = in_live & (their_row != first_row + in_idx)
    collect_map = (
        (in_idx[None, :] == jnp.arange(block_rows, dtype=jnp.int32)[:, None]) & in_off[None, :]
    ).astype(jnp.float32)

    def swap(parts):
        return lax.all_to_all(parts, "rows", split_axis=0, concat_axis=0, tiled=True)

    peer_ids = jnp.arange(row_count, dtype=jnp.int32)
    to_lower = (peer_ids <= row_index)[:, None, None]
    from_self = (peer_ids == row_index)[:, None, None]

    def both_ways(blocks):
        got = swap(jnp.where(to_lower, asked_part(blocks), served_part(blocks)))
        their = jnp.where(peer_ids[:, None, None] >= row_index, got, jnp.zeros((), got.dtype))
        served_self = blocks[in_idx[row_index]]
        far = jnp.where(from_self, served_self[None], got)
        return their, per_slot(far)

    def asked_part(blocks):
        return jnp.where(ask_live[:, None, None], blocks[ask_row], jnp.zeros((), blocks.dtype))

    def served_part(blocks):
        return jnp.where(in_live[:, None, None], blocks[in_idx], jnp.zeros((), blocks.dtype))

    def per_slot(got):
        chosen = got[pick_at]
        return jnp.where(is_live[:, None, None], chosen, jnp.zeros((), chosen.dtype))

    def collect(terms):
        flat = terms.reshape(row_count, -1)
        summed = jnp.dot(
            collect_map, flat, precision=lax.Precision.HIGHEST, preferred_element_type=jnp.float32
        )
        return summed.reshape((block_rows,) + terms.shape[1:])

    def column_total(partial_value):
        return allsum(partial_value, "cols", 1 if partial_value.shape[1] == 1 else 2)

    def global_sum(values):
        return allsum(values, "rows", 0)

    own_x = points.reshape(coord_dim, block_rows, block_len).transpose(1, 0, 2)
    their_x, far_x = both_ways(own_x)
    left_x = jnp.concatenate([own_x[slot_row], their_x], axis=0)
    right_x = jnp.concatenate([far_x, own_x[in_idx]], axis=0)
    pair_live = jnp.concatenate([is_live, in_off], axis=0)
    pair_count = slot_count + row_count
    chunk = 16
    pad = (-pair_count) % chunk
    left_x = jnp.pad(left_x, ((0, pad), (0, 0), (0, 0)))
    right_x = jnp.pad(right_x, ((0, pad), (0, 0), (0, 0)))
    pair_live = jnp.pad(pair_live, (0, pad))

    def pair_step(pieces):
        lx, rx, live = pieces
        values = jnp.where(live[:, None, None], wendland(lx, rx), 0.0)
        return (values.astype(jnp.bfloat16), jnp.sum(values, axis=2), jnp.sum(values, axis=1))

    kernel_bf, row_sums, col_sums = lax.map(
        pair_step,
        (
            left_x.reshape(-1, chunk, coord_dim, block_len),
            right_x.reshape(-1, chunk, coord_dim, block_len),
            pair_live.reshape(-1, chunk),
        ),
    )
    kernel_bf = kernel_bf.reshape(-1, block_len, block_len)
    row_sums = row_sums.reshape(-1, block_len)
    col_sums = col_sums.reshape(-1, block_len)
    own_k = kernel_bf[:slot_count]
    in_k = kernel_bf[slot_count:pair_count]
    degree_direct = jnp.sum(row_sums[:slot_count].reshape(block_rows, slot_width, block_len), axis=1)
    degree_mirror = collect(col_sums[slot_count:pair_count])
    degree_part = (degree_direct + degree_mirror)[:, None, :]
    inv_root = 1.0 / jnp.sqrt(1.0 + column_total(degree_part))

    def apply_partial(weights):
        their_w, far_w = both_ways(weights)
        direct = jnp.einsum("sab,sob->soa", own_k, far_w, preferred_element_type=jnp.float32)
        direct = jnp.sum(direct.reshape(block_rows, slot_width, outputs, block_len), axis=1)
        mirror = jnp.einsum("eab,eoa->eob", in_k, their_w, preferred_element_type=jnp.float32)
        return direct + collect(mirror)

    resid = targets.reshape(outputs, block_rows, block_len).transpose(1, 0, 2)
    direction = resid
    solution = jnp.zeros_like(resid)
    norm_now = jnp.sum(resid * resid, axis=(0, 2))
    first_col = lax.axis_index("cols") == 0
    for iteration in range(ITERS):
        weights = (direction * inv_root).astype(jnp.bfloat16)
        z_part = apply_partial(weights)
        own_term = jnp.where(first_col, REG * jnp.sum(direction * direction, axis=(0, 2)), 0.0)
        curv_part = own_term + jnp.sum(direction * (inv_root * z_part), axis=(0, 2))
        if iteration == 0:
            norm_part = jnp.where(first_col, norm_now, 0.0)
            z_total, both = fused_sum(z_part, jnp.concatenate([norm_part, curv_part]), 6)
            norm_now, curvature = both[:outputs], both[outputs:]
        else:
            z_total, curvature = fused_sum(z_part, curv_part, 7)
        applied = REG * direction + inv_root * z_total
        step_size = norm_now / curvature
        solution = solution + step_size[None, :, None] * direction
        resid = resid - step_size[None, :, None] * applied
        if iteration + 1 < ITERS:
            norm_next = global_sum(jnp.sum(resid * resid, axis=(0, 2)))
            direction = resid + (norm_next / norm_now)[None, :, None] * direction
            norm_now = norm_next
    return (
        solution.transpose(1, 0, 2).reshape(outputs, npoints),
        resid.transpose(1, 0, 2).reshape(outputs, npoints),
    )


def solution(mesh):
    placed = (P("rows", "cols"), P(None, "rows"), P(None, "rows"))
    return jax.shard_map(
        local,
        mesh=mesh,
        in_specs=placed,
        out_specs=(P(None, "rows"), P(None, "rows")),
        check_vma=False,
    )
```

```python
import functools

import jax
import jax.numpy as jnp
from jax import lax
from jax.experimental import pallas as pl
from jax.experimental.pallas import tpu as pltpu
from jax.sharding import PartitionSpec as P

MESH = pl.DeviceIdType.MESH

ITERS = 2


REG = 1.5
RADIUS = 0.25


def wendland(left_x, right_x):
    left_f = left_x.astype(jnp.float32)
    right_f = right_x.astype(jnp.float32)
    left_sq = jnp.sum(left_f * left_f, axis=1)
    right_sq = jnp.sum(right_f * right_f, axis=1)
    inner_prod = jnp.einsum("nda,ndb->nab", left_f, right_f, precision=lax.Precision.HIGHEST)
    dist_sq = left_sq[:, :, None] + right_sq[:, None, :] - 2.0 * inner_prod
    scaled = jnp.sqrt(jnp.maximum(dist_sq, 0.0)) / RADIUS
    remain = jnp.maximum(1.0 - scaled, 0.0)
    square = remain * remain
    return square * square * (4.0 * scaled + 1.0)


def allsum_kernel(axis, n, x_ref, o_ref, recv, send_sem, recv_sem):
    me = lax.axis_index(axis)
    barrier = pltpu.get_barrier_semaphore()

    def greet(k, carry):
        peer = lax.rem(me + k, n)
        pl.semaphore_signal(barrier, inc=1, device_id={axis: peer}, device_id_type=MESH)
        return carry

    lax.fori_loop(1, n, greet, 0)
    pl.semaphore_wait(barrier, n - 1)

    def outgoing(peer):
        return pltpu.make_async_remote_copy(
            src_ref=x_ref,
            dst_ref=recv.at[me],
            send_sem=send_sem.at[peer],
            recv_sem=recv_sem.at[me],
            device_id={axis: peer},
            device_id_type=MESH,
        )

    def incoming(peer):
        return pltpu.make_async_remote_copy(
            src_ref=x_ref,
            dst_ref=recv.at[peer],
            send_sem=send_sem.at[peer],
            recv_sem=recv_sem.at[peer],
            device_id={axis: peer},
            device_id_type=MESH,
        )

    def start(k, carry):
        outgoing(lax.rem(me + k, n)).start()
        return carry

    lax.fori_loop(1, n, start, 0)
    recv[me] = x_ref[...]

    def finish(k, carry):
        peer = lax.rem(me + k, n)
        outgoing(peer).wait_send()
        incoming(peer).wait_recv()
        return carry

    lax.fori_loop(1, n, finish, 0)
    o_ref[...] = recv[0]

    def add(s, carry):
        o_ref[...] += recv[s]
        return carry

    lax.fori_loop(1, n, add, 0)


def allsum(x, axis, cid):
    n = lax.axis_size(axis)
    shape = x.shape
    flat = x.reshape(-1)
    size = flat.shape[0]
    if size <= 128:
        tile = jnp.pad(flat, (0, 128 - size)).reshape(1, 128)
    elif size % 1024 == 0:
        tile = flat.reshape(size // 128, 128)
    else:
        rows_pad = -(-size // 1024) * 8
        tile = jnp.pad(flat, (0, rows_pad * 128 - size)).reshape(rows_pad, 128)
    out = pl.pallas_call(
        functools.partial(allsum_kernel, axis, n),
        out_shape=jax.ShapeDtypeStruct(tile.shape, jnp.float32),
        in_specs=[pl.BlockSpec(memory_space=pltpu.VMEM)],
        out_specs=pl.BlockSpec(memory_space=pltpu.VMEM),
        scratch_shapes=[
            pltpu.VMEM((n,) + tile.shape, jnp.float32),
            pltpu.SemaphoreType.DMA((n,)),
            pltpu.SemaphoreType.DMA((n,)),
        ],
        compiler_params=pltpu.CompilerParams(collective_id=cid, has_side_effects=True),
    )(tile)
    return out.reshape(-1)[:size].reshape(shape)


def fused_kernel(n_rows, n_cols, z_ref, g_ref, zo_ref, go_ref, recv_z, recv_g, recv_s, rows_sum, sems):
    row = lax.axis_index("rows")
    col = lax.axis_index("cols")
    barrier = pltpu.get_barrier_semaphore()

    def greet(k, carry):
        pl.semaphore_signal(
            barrier, inc=1, device_id={"rows": lax.rem(row + k, n_rows)}, device_id_type=MESH
        )
        return carry

    lax.fori_loop(1, n_rows, greet, 0)
    for k in range(1, n_cols):
        pl.semaphore_signal(
            barrier, inc=1, device_id={"cols": lax.rem(col + k, n_cols)}, device_id_type=MESH
        )
    pl.semaphore_wait(barrier, n_rows - 1 + n_cols - 1)
    z_send, z_recv, g_send, g_recv, s_send, s_recv = sems

    def col_copy(src, dst, send, recv, peer, slot):
        return pltpu.make_async_remote_copy(
            src_ref=src,
            dst_ref=dst.at[slot],
            send_sem=send.at[peer],
            recv_sem=recv.at[slot],
            device_id={"cols": peer},
            device_id_type=MESH,
        )

    def g_copy(peer, slot):
        return pltpu.make_async_remote_copy(
            src_ref=g_ref,
            dst_ref=recv_g.at[slot],
            send_sem=g_send.at[peer],
            recv_sem=g_recv.at[slot],
            device_id={"rows": peer},
            device_id_type=MESH,
        )

    for k in range(1, n_cols):
        col_copy(z_ref, recv_z, z_send, z_recv, lax.rem(col + k, n_cols), col).start()

    def start(k, carry):
        g_copy(lax.rem(row + k, n_rows), row).start()
        return carry

    lax.fori_loop(1, n_rows, start, 0)
    recv_z[col] = z_ref[...]
    recv_g[row] = g_ref[...]

    def finish(k, carry):
        peer = lax.rem(row + k, n_rows)
        g_copy(peer, row).wait_send()
        g_copy(peer, peer).wait_recv()
        return carry

    lax.fori_loop(1, n_rows, finish, 0)
    rows_sum[...] = recv_g[0]

    def add(s, carry):
        rows_sum[...] += recv_g[s]
        return carry

    lax.fori_loop(1, n_rows, add, 0)
    for k in range(1, n_cols):
        col_copy(rows_sum, recv_s, s_send, s_recv, lax.rem(col + k, n_cols), col).start()
    recv_s[col] = rows_sum[...]
    for k in range(1, n_cols):
        peer = lax.rem(col + k, n_cols)
        col_copy(z_ref, recv_z, z_send, z_recv, peer, col).wait_send()
        col_copy(z_ref, recv_z, z_send, z_recv, peer, peer).wait_recv()
    zo_ref[...] = recv_z[0]
    for k in range(1, n_cols):
        zo_ref[...] += recv_z[k]
    for k in range(1, n_cols):
        peer = lax.rem(col + k, n_cols)
        col_copy(rows_sum, recv_s, s_send, s_recv, peer, col).wait_send()
        col_copy(rows_sum, recv_s, s_send, s_recv, peer, peer).wait_recv()
    go_ref[...] = recv_s[0]
    for k in range(1, n_cols):
        go_ref[...] += recv_s[k]


def fused_sum(z, g, cid):
    n_rows = lax.axis_size("rows")
    n_cols = lax.axis_size("cols")
    z_tile = z.reshape(-1, z.shape[-1])
    size = g.shape[0]
    g_tile = jnp.pad(g, (0, 128 - size)).reshape(1, 128)
    vmem = pl.BlockSpec(memory_space=pltpu.VMEM)
    z_out, g_out = pl.pallas_call(
        functools.partial(fused_kernel, n_rows, n_cols),
        out_shape=[
            jax.ShapeDtypeStruct(z_tile.shape, jnp.float32),
            jax.ShapeDtypeStruct(g_tile.shape, jnp.float32),
        ],
        in_specs=[vmem, vmem],
        out_specs=[vmem, vmem],
        scratch_shapes=[
            pltpu.VMEM((n_cols,) + z_tile.shape, jnp.float32),
            pltpu.VMEM((n_rows,) + g_tile.shape, jnp.float32),
            pltpu.VMEM((n_cols,) + g_tile.shape, jnp.float32),
            pltpu.VMEM(g_tile.shape, jnp.float32),
            [
                pltpu.SemaphoreType.DMA((n_cols,)),
                pltpu.SemaphoreType.DMA((n_cols,)),
                pltpu.SemaphoreType.DMA((n_rows,)),
                pltpu.SemaphoreType.DMA((n_rows,)),
                pltpu.SemaphoreType.DMA((n_cols,)),
                pltpu.SemaphoreType.DMA((n_cols,)),
            ],
        ],
        compiler_params=pltpu.CompilerParams(collective_id=cid, has_side_effects=True),
    )(z_tile, g_tile)
    return z_out.reshape(z.shape), g_out.reshape(-1)[:size]


def local(block_list, points, targets):
    row_count = lax.axis_size("rows")
    row_index = lax.axis_index("rows")
    block_rows, slot_width = block_list.shape
    coord_dim, npoints = points.shape
    outputs = targets.shape[0]
    block_len = npoints // block_rows
    slot_count = block_rows * slot_width
    entries = block_list.reshape(slot_count)
    is_live = entries >= 0
    owners = jnp.where(is_live, entries // block_rows, 0)
    local_idx = jnp.where(is_live, entries - owners * block_rows, 0)
    slot_row = jnp.arange(slot_count, dtype=jnp.int32) // slot_width
    first_row = row_index * block_rows
    place_at = jnp.where(is_live, owners, row_count)
    pick_at = jnp.minimum(place_at, row_count - 1)
    wanted = jnp.full((row_count,), -1, jnp.int32).at[place_at].set(local_idx, mode="drop")
    asking_row = jnp.full((row_count,), -1, jnp.int32).at[place_at].set(slot_row, mode="drop")
    ask_live = asking_row >= 0
    ask_row = jnp.maximum(asking_row, 0)
    request = jnp.stack([wanted, asking_row], axis=1).reshape(row_count, 1, 2)
    incoming = lax.all_to_all(request, "rows", split_axis=0, concat_axis=0, tiled=True).reshape(
        row_count, 2
    )
    in_live = incoming[:, 0] >= 0
    in_idx = jnp.maximum(incoming[:, 0], 0)
    their_row = jnp.arange(row_count, dtype=jnp.int32) * block_rows + jnp.maximum(incoming[:, 1], 0)
    in_off = in_live & (their_row != first_row + in_idx)
    collect_map = (
        (in_idx[None, :] == jnp.arange(block_rows, dtype=jnp.int32)[:, None]) & in_off[None, :]
    ).astype(jnp.float32)

    def swap(parts):
        return lax.all_to_all(parts, "rows", split_axis=0, concat_axis=0, tiled=True)

    peer_ids = jnp.arange(row_count, dtype=jnp.int32)
    to_lower = (peer_ids <= row_index)[:, None, None]
    from_self = (peer_ids == row_index)[:, None, None]

    def both_ways(blocks):
        got = swap(jnp.where(to_lower, asked_part(blocks), served_part(blocks)))
        their = jnp.where(peer_ids[:, None, None] >= row_index, got, jnp.zeros((), got.dtype))
        served_self = blocks[in_idx[row_index]]
        far = jnp.where(from_self, served_self[None], got)
        return their, per_slot(far)

    def asked_part(blocks):
        return jnp.where(ask_live[:, None, None], blocks[ask_row], jnp.zeros((), blocks.dtype))

    def served_part(blocks):
        return jnp.where(in_live[:, None, None], blocks[in_idx], jnp.zeros((), blocks.dtype))

    def per_slot(got):
        chosen = got[pick_at]
        return jnp.where(is_live[:, None, None], chosen, jnp.zeros((), chosen.dtype))

    def collect(terms):
        flat = terms.reshape(row_count, -1)
        summed = jnp.dot(
            collect_map, flat, precision=lax.Precision.HIGHEST, preferred_element_type=jnp.float32
        )
        return summed.reshape((block_rows,) + terms.shape[1:])

    def column_total(partial_value):
        return allsum(partial_value, "cols", 1 if partial_value.shape[1] == 1 else 2)

    def global_sum(values):
        return allsum(values, "rows", 0)

    own_x = points.reshape(coord_dim, block_rows, block_len).transpose(1, 0, 2)
    their_x, far_x = both_ways(own_x)
    left_x = jnp.concatenate([own_x[slot_row], their_x], axis=0)
    right_x = jnp.concatenate([far_x, own_x[in_idx]], axis=0)
    pair_live = jnp.concatenate([is_live, in_off], axis=0)
    pair_count = slot_count + row_count
    chunk = 16
    pad = (-pair_count) % chunk
    left_x = jnp.pad(left_x, ((0, pad), (0, 0), (0, 0)))
    right_x = jnp.pad(right_x, ((0, pad), (0, 0), (0, 0)))
    pair_live = jnp.pad(pair_live, (0, pad))

    def pair_step(pieces):
        lx, rx, live = pieces
        values = jnp.where(live[:, None, None], wendland(lx, rx), 0.0)
        return (values.astype(jnp.bfloat16), jnp.sum(values, axis=2), jnp.sum(values, axis=1))

    kernel_bf, row_sums, col_sums = lax.map(
        pair_step,
        (
            left_x.reshape(-1, chunk, coord_dim, block_len),
            right_x.reshape(-1, chunk, coord_dim, block_len),
            pair_live.reshape(-1, chunk),
        ),
    )
    kernel_bf = kernel_bf.reshape(-1, block_len, block_len)
    row_sums = row_sums.reshape(-1, block_len)
    col_sums = col_sums.reshape(-1, block_len)
    own_k = kernel_bf[:slot_count]
    in_k = kernel_bf[slot_count:pair_count]
    degree_direct = jnp.sum(row_sums[:slot_count].reshape(block_rows, slot_width, block_len), axis=1)
    degree_mirror = collect(col_sums[slot_count:pair_count])
    degree_part = (degree_direct + degree_mirror)[:, None, :]
    inv_root = 1.0 / jnp.sqrt(1.0 + column_total(degree_part))

    def apply_partial(weights):
        their_w, far_w = both_ways(weights)
        direct = jnp.einsum("sab,sob->soa", own_k, far_w, preferred_element_type=jnp.float32)
        direct = jnp.sum(direct.reshape(block_rows, slot_width, outputs, block_len), axis=1)
        mirror = jnp.einsum("eab,eoa->eob", in_k, their_w, preferred_element_type=jnp.float32)
        return direct + collect(mirror)

    resid = targets.reshape(outputs, block_rows, block_len).transpose(1, 0, 2)
    direction = resid
    solution = jnp.zeros_like(resid)
    norm_now = jnp.sum(resid * resid, axis=(0, 2))
    first_col = lax.axis_index("cols") == 0
    for iteration in range(ITERS):
        weights = (direction * inv_root).astype(jnp.bfloat16)
        z_part = apply_partial(weights)
        own_term = jnp.where(first_col, REG * jnp.sum(direction * direction, axis=(0, 2)), 0.0)
        curv_part = own_term + jnp.sum(direction * (inv_root * z_part), axis=(0, 2))
        if iteration == 0:
            norm_part = jnp.where(first_col, norm_now, 0.0)
            z_total, both = fused_sum(z_part, jnp.concatenate([norm_part, curv_part]), 6)
            norm_now, curvature = both[:outputs], both[outputs:]
        else:
            z_total, curvature = fused_sum(z_part, curv_part, 7)
        applied = REG * direction + inv_root * z_total
        step_size = norm_now / curvature
        solution = solution + step_size[None, :, None] * direction
        resid = resid - step_size[None, :, None] * applied
        if iteration + 1 < ITERS:
            norm_next = global_sum(jnp.sum(resid * resid, axis=(0, 2)))
            direction = resid + (norm_next / norm_now)[None, :, None] * direction
            norm_now = norm_next
    return (
        solution.transpose(1, 0, 2).reshape(outputs, npoints),
        resid.transpose(1, 0, 2).reshape(outputs, npoints),
    )


def solution(mesh):
    placed = (P("rows", "cols"), P(None, "rows"), P(None, "rows"))
    return jax.shard_map(
        local,
        mesh=mesh,
        in_specs=placed,
        out_specs=(P(None, "rows"), P(None, "rows")),
        check_vma=False,
    )
```

```python
import functools

import jax
import jax.numpy as jnp
from jax import lax
from jax.experimental import pallas as pl
from jax.experimental.pallas import tpu as pltpu
from jax.sharding import PartitionSpec as P

MESH = pl.DeviceIdType.MESH

ITERS = 2


REG = 1.5
RADIUS = 0.25


def wendland(left_x, right_x):
    left_f = left_x.astype(jnp.float32)
    right_f = right_x.astype(jnp.float32)
    left_sq = jnp.sum(left_f * left_f, axis=1)
    right_sq = jnp.sum(right_f * right_f, axis=1)
    inner_prod = jnp.einsum("nda,ndb->nab", left_f, right_f, precision=lax.Precision.HIGHEST)
    dist_sq = left_sq[:, :, None] + right_sq[:, None, :] - 2.0 * inner_prod
    scaled = jnp.sqrt(jnp.maximum(dist_sq, 0.0)) / RADIUS
    remain = jnp.maximum(1.0 - scaled, 0.0)
    square = remain * remain
    return square * square * (4.0 * scaled + 1.0)


def allsum_kernel(axis, n, x_ref, o_ref, recv, send_sem, recv_sem):
    me = lax.axis_index(axis)
    barrier = pltpu.get_barrier_semaphore()

    def greet(k, carry):
        peer = lax.rem(me + k, n)
        pl.semaphore_signal(barrier, inc=1, device_id={axis: peer}, device_id_type=MESH)
        return carry

    lax.fori_loop(1, n, greet, 0)
    pl.semaphore_wait(barrier, n - 1)

    def outgoing(peer):
        return pltpu.make_async_remote_copy(
            src_ref=x_ref,
            dst_ref=recv.at[me],
            send_sem=send_sem.at[peer],
            recv_sem=recv_sem.at[me],
            device_id={axis: peer},
            device_id_type=MESH,
        )

    def incoming(peer):
        return pltpu.make_async_remote_copy(
            src_ref=x_ref,
            dst_ref=recv.at[peer],
            send_sem=send_sem.at[peer],
            recv_sem=recv_sem.at[peer],
            device_id={axis: peer},
            device_id_type=MESH,
        )

    def start(k, carry):
        outgoing(lax.rem(me + k, n)).start()
        return carry

    lax.fori_loop(1, n, start, 0)
    recv[me] = x_ref[...]

    def finish(k, carry):
        peer = lax.rem(me + k, n)
        outgoing(peer).wait_send()
        incoming(peer).wait_recv()
        return carry

    lax.fori_loop(1, n, finish, 0)
    o_ref[...] = recv[0]

    def add(s, carry):
        o_ref[...] += recv[s]
        return carry

    lax.fori_loop(1, n, add, 0)


def allsum(x, axis, cid):
    n = lax.axis_size(axis)
    shape = x.shape
    flat = x.reshape(-1)
    size = flat.shape[0]
    if size <= 128:
        tile = jnp.pad(flat, (0, 128 - size)).reshape(1, 128)
    elif size % 1024 == 0:
        tile = flat.reshape(size // 128, 128)
    else:
        rows_pad = -(-size // 1024) * 8
        tile = jnp.pad(flat, (0, rows_pad * 128 - size)).reshape(rows_pad, 128)
    out = pl.pallas_call(
        functools.partial(allsum_kernel, axis, n),
        out_shape=jax.ShapeDtypeStruct(tile.shape, jnp.float32),
        in_specs=[pl.BlockSpec(memory_space=pltpu.VMEM)],
        out_specs=pl.BlockSpec(memory_space=pltpu.VMEM),
        scratch_shapes=[
            pltpu.VMEM((n,) + tile.shape, jnp.float32),
            pltpu.SemaphoreType.DMA((n,)),
            pltpu.SemaphoreType.DMA((n,)),
        ],
        compiler_params=pltpu.CompilerParams(collective_id=cid, has_side_effects=True),
    )(tile)
    return out.reshape(-1)[:size].reshape(shape)


def fused_kernel(n_rows, n_cols, z_ref, g_ref, zo_ref, go_ref, recv_z, recv_g, recv_s, rows_sum, sems):
    row = lax.axis_index("rows")
    col = lax.axis_index("cols")
    barrier = pltpu.get_barrier_semaphore()

    def greet(k, carry):
        pl.semaphore_signal(
            barrier, inc=1, device_id={"rows": lax.rem(row + k, n_rows)}, device_id_type=MESH
        )
        return carry

    lax.fori_loop(1, n_rows, greet, 0)
    for k in range(1, n_cols):
        pl.semaphore_signal(
            barrier, inc=1, device_id={"cols": lax.rem(col + k, n_cols)}, device_id_type=MESH
        )
    pl.semaphore_wait(barrier, n_rows - 1 + n_cols - 1)
    z_send, z_recv, g_send, g_recv, s_send, s_recv = sems

    def col_copy(src, dst, send, recv, peer, slot):
        return pltpu.make_async_remote_copy(
            src_ref=src,
            dst_ref=dst.at[slot],
            send_sem=send.at[peer],
            recv_sem=recv.at[slot],
            device_id={"cols": peer},
            device_id_type=MESH,
        )

    def g_copy(peer, slot):
        return pltpu.make_async_remote_copy(
            src_ref=g_ref,
            dst_ref=recv_g.at[slot],
            send_sem=g_send.at[peer],
            recv_sem=g_recv.at[slot],
            device_id={"rows": peer},
            device_id_type=MESH,
        )

    for k in range(1, n_cols):
        col_copy(z_ref, recv_z, z_send, z_recv, lax.rem(col + k, n_cols), col).start()

    def start(k, carry):
        g_copy(lax.rem(row + k, n_rows), row).start()
        return carry

    lax.fori_loop(1, n_rows, start, 0)
    recv_z[col] = z_ref[...]
    recv_g[row] = g_ref[...]

    def finish(k, carry):
        peer = lax.rem(row + k, n_rows)
        g_copy(peer, row).wait_send()
        g_copy(peer, peer).wait_recv()
        return carry

    lax.fori_loop(1, n_rows, finish, 0)
    rows_sum[...] = recv_g[0]

    def add(s, carry):
        rows_sum[...] += recv_g[s]
        return carry

    lax.fori_loop(1, n_rows, add, 0)
    for k in range(1, n_cols):
        col_copy(rows_sum, recv_s, s_send, s_recv, lax.rem(col + k, n_cols), col).start()
    recv_s[col] = rows_sum[...]
    for k in range(1, n_cols):
        peer = lax.rem(col + k, n_cols)
        col_copy(z_ref, recv_z, z_send, z_recv, peer, col).wait_send()
        col_copy(z_ref, recv_z, z_send, z_recv, peer, peer).wait_recv()
    zo_ref[...] = recv_z[0]
    for k in range(1, n_cols):
        zo_ref[...] += recv_z[k]
    for k in range(1, n_cols):
        peer = lax.rem(col + k, n_cols)
        col_copy(rows_sum, recv_s, s_send, s_recv, peer, col).wait_send()
        col_copy(rows_sum, recv_s, s_send, s_recv, peer, peer).wait_recv()
    go_ref[...] = recv_s[0]
    for k in range(1, n_cols):
        go_ref[...] += recv_s[k]


def fused_sum(z, g, cid):
    n_rows = lax.axis_size("rows")
    n_cols = lax.axis_size("cols")
    z_tile = z.reshape(-1, z.shape[-1])
    size = g.shape[0]
    g_tile = jnp.pad(g, (0, 128 - size)).reshape(1, 128)
    vmem = pl.BlockSpec(memory_space=pltpu.VMEM)
    z_out, g_out = pl.pallas_call(
        functools.partial(fused_kernel, n_rows, n_cols),
        out_shape=[
            jax.ShapeDtypeStruct(z_tile.shape, jnp.float32),
            jax.ShapeDtypeStruct(g_tile.shape, jnp.float32),
        ],
        in_specs=[vmem, vmem],
        out_specs=[vmem, vmem],
        scratch_shapes=[
            pltpu.VMEM((n_cols,) + z_tile.shape, jnp.float32),
            pltpu.VMEM((n_rows,) + g_tile.shape, jnp.float32),
            pltpu.VMEM((n_cols,) + g_tile.shape, jnp.float32),
            pltpu.VMEM(g_tile.shape, jnp.float32),
            [
                pltpu.SemaphoreType.DMA((n_cols,)),
                pltpu.SemaphoreType.DMA((n_cols,)),
                pltpu.SemaphoreType.DMA((n_rows,)),
                pltpu.SemaphoreType.DMA((n_rows,)),
                pltpu.SemaphoreType.DMA((n_cols,)),
                pltpu.SemaphoreType.DMA((n_cols,)),
            ],
        ],
        compiler_params=pltpu.CompilerParams(collective_id=cid, has_side_effects=True),
    )(z_tile, g_tile)
    return z_out.reshape(z.shape), g_out.reshape(-1)[:size]


def pair_kernel(chunk, live_ref, lsq_ref, rsq_ref, left_ref, right_ref, k_ref, row_ref, col_ref):
    base = pl.program_id(0) * chunk

    def body(p, carry):
        inner = lax.dot_general(
            left_ref[p].astype(jnp.float32),
            right_ref[p].astype(jnp.float32),
            (((0,), (0,)), ((), ())),
            precision=lax.Precision.HIGHEST,
            preferred_element_type=jnp.float32,
        )
        dist_sq = lsq_ref[p] + rsq_ref[p] - 2.0 * inner
        scaled = jnp.sqrt(jnp.maximum(dist_sq, 0.0)) * (1.0 / RADIUS)
        remain = jnp.maximum(1.0 - scaled, 0.0)
        square = remain * remain
        values = square * square * (4.0 * scaled + 1.0)
        values = jnp.where(live_ref[base + p] != 0, values, 0.0)
        k_ref[p] = values.astype(jnp.bfloat16)
        row_ref[p] = jnp.sum(values, axis=1, keepdims=True)
        col_ref[p] = jnp.sum(values, axis=0, keepdims=True)
        return carry

    lax.fori_loop(0, chunk, body, 0)


def pair_blocks(left_x, right_x, live, chunk):
    count, coord_dim, block_len = left_x.shape
    left_f = left_x.astype(jnp.float32)
    right_f = right_x.astype(jnp.float32)
    left_sq = jnp.sum(left_f * left_f, axis=1)[:, :, None]
    right_sq = jnp.sum(right_f * right_f, axis=1)[:, None, :]

    def spec(*tail):
        return pl.BlockSpec((chunk,) + tail, lambda i, live_ref: (i,) + (0,) * len(tail))

    return pl.pallas_call(
        functools.partial(pair_kernel, chunk),
        out_shape=[
            jax.ShapeDtypeStruct((count, block_len, block_len), jnp.bfloat16),
            jax.ShapeDtypeStruct((count, block_len, 1), jnp.float32),
            jax.ShapeDtypeStruct((count, 1, block_len), jnp.float32),
        ],
        grid_spec=pltpu.PrefetchScalarGridSpec(
            num_scalar_prefetch=1,
            grid=(count // chunk,),
            in_specs=[
                spec(block_len, 1),
                spec(1, block_len),
                spec(coord_dim, block_len),
                spec(coord_dim, block_len),
            ],
            out_specs=[spec(block_len, block_len), spec(block_len, 1), spec(1, block_len)],
        ),
    )(live.astype(jnp.int32), left_sq, right_sq, left_x, right_x)


def local(block_list, points, targets):
    row_count = lax.axis_size("rows")
    row_index = lax.axis_index("rows")
    block_rows, slot_width = block_list.shape
    coord_dim, npoints = points.shape
    outputs = targets.shape[0]
    block_len = npoints // block_rows
    slot_count = block_rows * slot_width
    entries = block_list.reshape(slot_count)
    is_live = entries >= 0
    owners = jnp.where(is_live, entries // block_rows, 0)
    local_idx = jnp.where(is_live, entries - owners * block_rows, 0)
    slot_row = jnp.arange(slot_count, dtype=jnp.int32) // slot_width
    first_row = row_index * block_rows
    place_at = jnp.where(is_live, owners, row_count)
    pick_at = jnp.minimum(place_at, row_count - 1)
    wanted = jnp.full((row_count,), -1, jnp.int32).at[place_at].set(local_idx, mode="drop")
    asking_row = jnp.full((row_count,), -1, jnp.int32).at[place_at].set(slot_row, mode="drop")
    ask_live = asking_row >= 0
    ask_row = jnp.maximum(asking_row, 0)
    request = jnp.stack([wanted, asking_row], axis=1).reshape(row_count, 1, 2)
    incoming = lax.all_to_all(request, "rows", split_axis=0, concat_axis=0, tiled=True).reshape(
        row_count, 2
    )
    in_live = incoming[:, 0] >= 0
    in_idx = jnp.maximum(incoming[:, 0], 0)
    their_row = jnp.arange(row_count, dtype=jnp.int32) * block_rows + jnp.maximum(incoming[:, 1], 0)
    in_off = in_live & (their_row != first_row + in_idx)
    collect_map = (
        (in_idx[None, :] == jnp.arange(block_rows, dtype=jnp.int32)[:, None]) & in_off[None, :]
    ).astype(jnp.float32)

    def swap(parts):
        return lax.all_to_all(parts, "rows", split_axis=0, concat_axis=0, tiled=True)

    peer_ids = jnp.arange(row_count, dtype=jnp.int32)
    to_lower = (peer_ids <= row_index)[:, None, None]
    from_self = (peer_ids == row_index)[:, None, None]

    def both_ways(blocks):
        got = swap(jnp.where(to_lower, asked_part(blocks), served_part(blocks)))
        their = jnp.where(peer_ids[:, None, None] >= row_index, got, jnp.zeros((), got.dtype))
        served_self = blocks[in_idx[row_index]]
        far = jnp.where(from_self, served_self[None], got)
        return their, per_slot(far)

    def asked_part(blocks):
        return jnp.where(ask_live[:, None, None], blocks[ask_row], jnp.zeros((), blocks.dtype))

    def served_part(blocks):
        return jnp.where(in_live[:, None, None], blocks[in_idx], jnp.zeros((), blocks.dtype))

    def per_slot(got):
        chosen = got[pick_at]
        return jnp.where(is_live[:, None, None], chosen, jnp.zeros((), chosen.dtype))

    def collect(terms):
        flat = terms.reshape(row_count, -1)
        summed = jnp.dot(
            collect_map, flat, precision=lax.Precision.HIGHEST, preferred_element_type=jnp.float32
        )
        return summed.reshape((block_rows,) + terms.shape[1:])

    def column_total(partial_value):
        return allsum(partial_value, "cols", 1 if partial_value.shape[1] == 1 else 2)

    def global_sum(values):
        return allsum(values, "rows", 0)

    own_x = points.reshape(coord_dim, block_rows, block_len).transpose(1, 0, 2)
    their_x, far_x = both_ways(own_x)
    left_x = jnp.concatenate([own_x[slot_row], their_x], axis=0)
    right_x = jnp.concatenate([far_x, own_x[in_idx]], axis=0)
    pair_live = jnp.concatenate([is_live, in_off], axis=0)
    pair_count = slot_count + row_count
    chunk = 8
    pad = (-pair_count) % chunk
    left_x = jnp.pad(left_x, ((0, pad), (0, 0), (0, 0)))
    right_x = jnp.pad(right_x, ((0, pad), (0, 0), (0, 0)))
    pair_live = jnp.pad(pair_live, (0, pad))
    kernel_bf, row_sums, col_sums = pair_blocks(left_x, right_x, pair_live, chunk)
    row_sums = row_sums.reshape(-1, block_len)
    col_sums = col_sums.reshape(-1, block_len)
    own_k = kernel_bf[:slot_count]
    in_k = kernel_bf[slot_count:pair_count]
    degree_direct = jnp.sum(row_sums[:slot_count].reshape(block_rows, slot_width, block_len), axis=1)
    degree_mirror = collect(col_sums[slot_count:pair_count])
    degree_part = (degree_direct + degree_mirror)[:, None, :]
    inv_root = 1.0 / jnp.sqrt(1.0 + column_total(degree_part))

    def apply_partial(weights):
        their_w, far_w = both_ways(weights)
        direct = jnp.einsum("sab,sob->soa", own_k, far_w, preferred_element_type=jnp.float32)
        direct = jnp.sum(direct.reshape(block_rows, slot_width, outputs, block_len), axis=1)
        mirror = jnp.einsum("eab,eoa->eob", in_k, their_w, preferred_element_type=jnp.float32)
        return direct + collect(mirror)

    resid = targets.reshape(outputs, block_rows, block_len).transpose(1, 0, 2)
    direction = resid
    solution = jnp.zeros_like(resid)
    norm_now = jnp.sum(resid * resid, axis=(0, 2))
    first_col = lax.axis_index("cols") == 0
    for iteration in range(ITERS):
        weights = (direction * inv_root).astype(jnp.bfloat16)
        z_part = apply_partial(weights)
        own_term = jnp.where(first_col, REG * jnp.sum(direction * direction, axis=(0, 2)), 0.0)
        curv_part = own_term + jnp.sum(direction * (inv_root * z_part), axis=(0, 2))
        if iteration == 0:
            norm_part = jnp.where(first_col, norm_now, 0.0)
            z_total, both = fused_sum(z_part, jnp.concatenate([norm_part, curv_part]), 6)
            norm_now, curvature = both[:outputs], both[outputs:]
        else:
            z_total, curvature = fused_sum(z_part, curv_part, 7)
        applied = REG * direction + inv_root * z_total
        step_size = norm_now / curvature
        solution = solution + step_size[None, :, None] * direction
        resid = resid - step_size[None, :, None] * applied
        if iteration + 1 < ITERS:
            norm_next = global_sum(jnp.sum(resid * resid, axis=(0, 2)))
            direction = resid + (norm_next / norm_now)[None, :, None] * direction
            norm_now = norm_next
    return (
        solution.transpose(1, 0, 2).reshape(outputs, npoints),
        resid.transpose(1, 0, 2).reshape(outputs, npoints),
    )


def solution(mesh):
    placed = (P("rows", "cols"), P(None, "rows"), P(None, "rows"))
    return jax.shard_map(
        local,
        mesh=mesh,
        in_specs=placed,
        out_specs=(P(None, "rows"), P(None, "rows")),
        check_vma=False,
    )
```

```python
import functools

import jax
import jax.numpy as jnp
from jax import lax
from jax.experimental import pallas as pl
from jax.experimental.pallas import tpu as pltpu
from jax.sharding import PartitionSpec as P

MESH = pl.DeviceIdType.MESH

ITERS = 2


REG = 1.5
RADIUS = 0.25


def wendland(left_x, right_x):
    left_f = left_x.astype(jnp.float32)
    right_f = right_x.astype(jnp.float32)
    left_sq = jnp.sum(left_f * left_f, axis=1)
    right_sq = jnp.sum(right_f * right_f, axis=1)
    inner_prod = jnp.einsum("nda,ndb->nab", left_f, right_f, precision=lax.Precision.HIGHEST)
    dist_sq = left_sq[:, :, None] + right_sq[:, None, :] - 2.0 * inner_prod
    scaled = jnp.sqrt(jnp.maximum(dist_sq, 0.0)) / RADIUS
    remain = jnp.maximum(1.0 - scaled, 0.0)
    square = remain * remain
    return square * square * (4.0 * scaled + 1.0)


def allsum_kernel(axis, n, x_ref, o_ref, recv, send_sem, recv_sem):
    me = lax.axis_index(axis)
    barrier = pltpu.get_barrier_semaphore()

    def greet(k, carry):
        peer = lax.rem(me + k, n)
        pl.semaphore_signal(barrier, inc=1, device_id={axis: peer}, device_id_type=MESH)
        return carry

    lax.fori_loop(1, n, greet, 0)
    pl.semaphore_wait(barrier, n - 1)

    def outgoing(peer):
        return pltpu.make_async_remote_copy(
            src_ref=x_ref,
            dst_ref=recv.at[me],
            send_sem=send_sem.at[peer],
            recv_sem=recv_sem.at[me],
            device_id={axis: peer},
            device_id_type=MESH,
        )

    def incoming(peer):
        return pltpu.make_async_remote_copy(
            src_ref=x_ref,
            dst_ref=recv.at[peer],
            send_sem=send_sem.at[peer],
            recv_sem=recv_sem.at[peer],
            device_id={axis: peer},
            device_id_type=MESH,
        )

    def start(k, carry):
        outgoing(lax.rem(me + k, n)).start()
        return carry

    lax.fori_loop(1, n, start, 0)
    recv[me] = x_ref[...]

    def finish(k, carry):
        peer = lax.rem(me + k, n)
        outgoing(peer).wait_send()
        incoming(peer).wait_recv()
        return carry

    lax.fori_loop(1, n, finish, 0)
    o_ref[...] = recv[0]

    def add(s, carry):
        o_ref[...] += recv[s]
        return carry

    lax.fori_loop(1, n, add, 0)


def allsum(x, axis, cid):
    n = lax.axis_size(axis)
    shape = x.shape
    flat = x.reshape(-1)
    size = flat.shape[0]
    if size <= 128:
        tile = jnp.pad(flat, (0, 128 - size)).reshape(1, 128)
    elif size % 1024 == 0:
        tile = flat.reshape(size // 128, 128)
    else:
        rows_pad = -(-size // 1024) * 8
        tile = jnp.pad(flat, (0, rows_pad * 128 - size)).reshape(rows_pad, 128)
    out = pl.pallas_call(
        functools.partial(allsum_kernel, axis, n),
        out_shape=jax.ShapeDtypeStruct(tile.shape, jnp.float32),
        in_specs=[pl.BlockSpec(memory_space=pltpu.VMEM)],
        out_specs=pl.BlockSpec(memory_space=pltpu.VMEM),
        scratch_shapes=[
            pltpu.VMEM((n,) + tile.shape, jnp.float32),
            pltpu.SemaphoreType.DMA((n,)),
            pltpu.SemaphoreType.DMA((n,)),
        ],
        compiler_params=pltpu.CompilerParams(collective_id=cid, has_side_effects=True),
    )(tile)
    return out.reshape(-1)[:size].reshape(shape)


def fused_kernel(n_rows, n_cols, z_ref, g_ref, zo_ref, go_ref, recv_z, recv_g, recv_s, rows_sum, sems):
    row = lax.axis_index("rows")
    col = lax.axis_index("cols")
    barrier = pltpu.get_barrier_semaphore()

    def greet(k, carry):
        pl.semaphore_signal(
            barrier, inc=1, device_id={"rows": lax.rem(row + k, n_rows)}, device_id_type=MESH
        )
        return carry

    lax.fori_loop(1, n_rows, greet, 0)
    for k in range(1, n_cols):
        pl.semaphore_signal(
            barrier, inc=1, device_id={"cols": lax.rem(col + k, n_cols)}, device_id_type=MESH
        )
    pl.semaphore_wait(barrier, n_rows - 1 + n_cols - 1)
    z_send, z_recv, g_send, g_recv, s_send, s_recv = sems

    def col_copy(src, dst, send, recv, peer, slot):
        return pltpu.make_async_remote_copy(
            src_ref=src,
            dst_ref=dst.at[slot],
            send_sem=send.at[peer],
            recv_sem=recv.at[slot],
            device_id={"cols": peer},
            device_id_type=MESH,
        )

    def g_copy(peer, slot):
        return pltpu.make_async_remote_copy(
            src_ref=g_ref,
            dst_ref=recv_g.at[slot],
            send_sem=g_send.at[peer],
            recv_sem=g_recv.at[slot],
            device_id={"rows": peer},
            device_id_type=MESH,
        )

    for k in range(1, n_cols):
        col_copy(z_ref, recv_z, z_send, z_recv, lax.rem(col + k, n_cols), col).start()

    def start(k, carry):
        g_copy(lax.rem(row + k, n_rows), row).start()
        return carry

    lax.fori_loop(1, n_rows, start, 0)
    recv_z[col] = z_ref[...]
    recv_g[row] = g_ref[...]

    def finish(k, carry):
        peer = lax.rem(row + k, n_rows)
        g_copy(peer, row).wait_send()
        g_copy(peer, peer).wait_recv()
        return carry

    lax.fori_loop(1, n_rows, finish, 0)
    rows_sum[...] = recv_g[0]

    def add(s, carry):
        rows_sum[...] += recv_g[s]
        return carry

    lax.fori_loop(1, n_rows, add, 0)
    for k in range(1, n_cols):
        col_copy(rows_sum, recv_s, s_send, s_recv, lax.rem(col + k, n_cols), col).start()
    recv_s[col] = rows_sum[...]
    for k in range(1, n_cols):
        peer = lax.rem(col + k, n_cols)
        col_copy(z_ref, recv_z, z_send, z_recv, peer, col).wait_send()
        col_copy(z_ref, recv_z, z_send, z_recv, peer, peer).wait_recv()
    zo_ref[...] = recv_z[0]
    for k in range(1, n_cols):
        zo_ref[...] += recv_z[k]
    for k in range(1, n_cols):
        peer = lax.rem(col + k, n_cols)
        col_copy(rows_sum, recv_s, s_send, s_recv, peer, col).wait_send()
        col_copy(rows_sum, recv_s, s_send, s_recv, peer, peer).wait_recv()
    go_ref[...] = recv_s[0]
    for k in range(1, n_cols):
        go_ref[...] += recv_s[k]


def fused_sum(z, g, cid):
    n_rows = lax.axis_size("rows")
    n_cols = lax.axis_size("cols")
    z_tile = z.reshape(-1, z.shape[-1])
    size = g.shape[0]
    g_tile = jnp.pad(g, (0, 128 - size)).reshape(1, 128)
    vmem = pl.BlockSpec(memory_space=pltpu.VMEM)
    z_out, g_out = pl.pallas_call(
        functools.partial(fused_kernel, n_rows, n_cols),
        out_shape=[
            jax.ShapeDtypeStruct(z_tile.shape, jnp.float32),
            jax.ShapeDtypeStruct(g_tile.shape, jnp.float32),
        ],
        in_specs=[vmem, vmem],
        out_specs=[vmem, vmem],
        scratch_shapes=[
            pltpu.VMEM((n_cols,) + z_tile.shape, jnp.float32),
            pltpu.VMEM((n_rows,) + g_tile.shape, jnp.float32),
            pltpu.VMEM((n_cols,) + g_tile.shape, jnp.float32),
            pltpu.VMEM(g_tile.shape, jnp.float32),
            [
                pltpu.SemaphoreType.DMA((n_cols,)),
                pltpu.SemaphoreType.DMA((n_cols,)),
                pltpu.SemaphoreType.DMA((n_rows,)),
                pltpu.SemaphoreType.DMA((n_rows,)),
                pltpu.SemaphoreType.DMA((n_cols,)),
                pltpu.SemaphoreType.DMA((n_cols,)),
            ],
        ],
        compiler_params=pltpu.CompilerParams(collective_id=cid, has_side_effects=True),
    )(z_tile, g_tile)
    return z_out.reshape(z.shape), g_out.reshape(-1)[:size]


def local(block_list, points, targets):
    row_count = lax.axis_size("rows")
    row_index = lax.axis_index("rows")
    block_rows, slot_width = block_list.shape
    coord_dim, npoints = points.shape
    outputs = targets.shape[0]
    block_len = npoints // block_rows
    slot_count = block_rows * slot_width
    entries = block_list.reshape(slot_count)
    is_live = entries >= 0
    owners = jnp.where(is_live, entries // block_rows, 0)
    local_idx = jnp.where(is_live, entries - owners * block_rows, 0)
    slot_row = jnp.arange(slot_count, dtype=jnp.int32) // slot_width
    first_row = row_index * block_rows
    place_at = jnp.where(is_live, owners, row_count)
    pick_at = jnp.minimum(place_at, row_count - 1)
    wanted = jnp.full((row_count,), -1, jnp.int32).at[place_at].set(local_idx, mode="drop")
    asking_row = jnp.full((row_count,), -1, jnp.int32).at[place_at].set(slot_row, mode="drop")
    ask_live = asking_row >= 0
    ask_row = jnp.maximum(asking_row, 0)
    request = jnp.stack([wanted, asking_row], axis=1).reshape(row_count, 1, 2)
    incoming = lax.all_to_all(request, "rows", split_axis=0, concat_axis=0, tiled=True).reshape(
        row_count, 2
    )
    in_live = incoming[:, 0] >= 0
    in_idx = jnp.maximum(incoming[:, 0], 0)
    their_row = jnp.arange(row_count, dtype=jnp.int32) * block_rows + jnp.maximum(incoming[:, 1], 0)
    in_off = in_live & (their_row != first_row + in_idx)
    collect_map = (
        (in_idx[None, :] == jnp.arange(block_rows, dtype=jnp.int32)[:, None]) & in_off[None, :]
    ).astype(jnp.float32)

    def swap(parts):
        return lax.all_to_all(parts, "rows", split_axis=0, concat_axis=0, tiled=True)

    peer_ids = jnp.arange(row_count, dtype=jnp.int32)
    to_lower = (peer_ids <= row_index)[:, None, None]
    from_self = (peer_ids == row_index)[:, None, None]

    def both_ways(blocks):
        got = swap(jnp.where(to_lower, asked_part(blocks), served_part(blocks)))
        their = jnp.where(peer_ids[:, None, None] >= row_index, got, jnp.zeros((), got.dtype))
        served_self = blocks[in_idx[row_index]]
        far = jnp.where(from_self, served_self[None], got)
        return their, per_slot(far)

    def asked_part(blocks):
        return jnp.where(ask_live[:, None, None], blocks[ask_row], jnp.zeros((), blocks.dtype))

    def served_part(blocks):
        return jnp.where(in_live[:, None, None], blocks[in_idx], jnp.zeros((), blocks.dtype))

    def per_slot(got):
        chosen = got[pick_at]
        return jnp.where(is_live[:, None, None], chosen, jnp.zeros((), chosen.dtype))

    def collect(terms):
        flat = terms.reshape(row_count, -1)
        summed = jnp.dot(
            collect_map, flat, precision=lax.Precision.HIGHEST, preferred_element_type=jnp.float32
        )
        return summed.reshape((block_rows,) + terms.shape[1:])

    def column_total(partial_value):
        return allsum(partial_value, "cols", 1 if partial_value.shape[1] == 1 else 2)

    def global_sum(values):
        return allsum(values, "rows", 0)

    own_x = points.reshape(coord_dim, block_rows, block_len).transpose(1, 0, 2)
    their_x, far_x = both_ways(own_x)
    left_x = jnp.concatenate([own_x[slot_row], their_x], axis=0)
    right_x = jnp.concatenate([far_x, own_x[in_idx]], axis=0)
    pair_live = jnp.concatenate([is_live, in_off], axis=0)
    pair_count = slot_count + row_count
    chunk = 112
    pad = (-pair_count) % chunk
    left_x = jnp.pad(left_x, ((0, pad), (0, 0), (0, 0)))
    right_x = jnp.pad(right_x, ((0, pad), (0, 0), (0, 0)))
    pair_live = jnp.pad(pair_live, (0, pad))

    def pair_step(pieces):
        lx, rx, live = pieces
        values = jnp.where(live[:, None, None], wendland(lx, rx), 0.0)
        return (values.astype(jnp.bfloat16), jnp.sum(values, axis=2), jnp.sum(values, axis=1))

    kernel_bf, row_sums, col_sums = lax.map(
        pair_step,
        (
            left_x.reshape(-1, chunk, coord_dim, block_len),
            right_x.reshape(-1, chunk, coord_dim, block_len),
            pair_live.reshape(-1, chunk),
        ),
    )
    kernel_bf = kernel_bf.reshape(-1, block_len, block_len)
    row_sums = row_sums.reshape(-1, block_len)
    col_sums = col_sums.reshape(-1, block_len)
    own_k = kernel_bf[:slot_count]
    in_k = kernel_bf[slot_count:pair_count]
    degree_direct = jnp.sum(row_sums[:slot_count].reshape(block_rows, slot_width, block_len), axis=1)
    degree_mirror = collect(col_sums[slot_count:pair_count])
    degree_part = (degree_direct + degree_mirror)[:, None, :]
    inv_root = 1.0 / jnp.sqrt(1.0 + column_total(degree_part))

    def apply_partial(weights):
        their_w, far_w = both_ways(weights)
        direct = jnp.einsum("sab,sob->soa", own_k, far_w, preferred_element_type=jnp.float32)
        direct = jnp.sum(direct.reshape(block_rows, slot_width, outputs, block_len), axis=1)
        mirror = jnp.einsum("eab,eoa->eob", in_k, their_w, preferred_element_type=jnp.float32)
        return direct + collect(mirror)

    resid = targets.reshape(outputs, block_rows, block_len).transpose(1, 0, 2)
    direction = resid
    solution = jnp.zeros_like(resid)
    norm_now = jnp.sum(resid * resid, axis=(0, 2))
    first_col = lax.axis_index("cols") == 0
    for iteration in range(ITERS):
        weights = (direction * inv_root).astype(jnp.bfloat16)
        z_part = apply_partial(weights)
        own_term = jnp.where(first_col, REG * jnp.sum(direction * direction, axis=(0, 2)), 0.0)
        curv_part = own_term + jnp.sum(direction * (inv_root * z_part), axis=(0, 2))
        if iteration == 0:
            norm_part = jnp.where(first_col, norm_now, 0.0)
            z_total, both = fused_sum(z_part, jnp.concatenate([norm_part, curv_part]), 6)
            norm_now, curvature = both[:outputs], both[outputs:]
        else:
            z_total, curvature = fused_sum(z_part, curv_part, 7)
        applied = REG * direction + inv_root * z_total
        step_size = norm_now / curvature
        solution = solution + step_size[None, :, None] * direction
        resid = resid - step_size[None, :, None] * applied
        if iteration + 1 < ITERS:
            norm_next = global_sum(jnp.sum(resid * resid, axis=(0, 2)))
            direction = resid + (norm_next / norm_now)[None, :, None] * direction
            norm_now = norm_next
    return (
        solution.transpose(1, 0, 2).reshape(outputs, npoints),
        resid.transpose(1, 0, 2).reshape(outputs, npoints),
    )


def solution(mesh):
    placed = (P("rows", "cols"), P(None, "rows"), P(None, "rows"))
    return jax.shard_map(
        local,
        mesh=mesh,
        in_specs=placed,
        out_specs=(P(None, "rows"), P(None, "rows")),
        check_vma=False,
    )
```

```python
import functools

import jax
import jax.numpy as jnp
from jax import lax
from jax.experimental import pallas as pl
from jax.experimental.pallas import tpu as pltpu
from jax.sharding import PartitionSpec as P

MESH = pl.DeviceIdType.MESH

ITERS = 2


REG = 1.5
RADIUS = 0.25


def wendland(left_x, right_x):
    left_f = left_x.astype(jnp.float32)
    right_f = right_x.astype(jnp.float32)
    left_sq = jnp.sum(left_f * left_f, axis=1, keepdims=True)
    right_sq = jnp.sum(right_f * right_f, axis=1, keepdims=True)
    ones = jnp.ones_like(left_sq)
    left_aug = jnp.concatenate([left_f, left_sq, ones], axis=1)
    right_aug = jnp.concatenate([-2.0 * right_f, ones, right_sq], axis=1)
    dist_sq = jnp.einsum("nda,ndb->nab", left_aug, right_aug, precision=lax.Precision.HIGHEST)
    scaled = jnp.sqrt(jnp.maximum(dist_sq, 0.0)) / RADIUS
    remain = jnp.maximum(1.0 - scaled, 0.0)
    square = remain * remain
    return square * square * (4.0 * scaled + 1.0)


def allsum_kernel(axis, n, x_ref, o_ref, recv, send_sem, recv_sem):
    me = lax.axis_index(axis)
    barrier = pltpu.get_barrier_semaphore()

    def greet(k, carry):
        peer = lax.rem(me + k, n)
        pl.semaphore_signal(barrier, inc=1, device_id={axis: peer}, device_id_type=MESH)
        return carry

    lax.fori_loop(1, n, greet, 0)
    pl.semaphore_wait(barrier, n - 1)

    def outgoing(peer):
        return pltpu.make_async_remote_copy(
            src_ref=x_ref,
            dst_ref=recv.at[me],
            send_sem=send_sem.at[peer],
            recv_sem=recv_sem.at[me],
            device_id={axis: peer},
            device_id_type=MESH,
        )

    def incoming(peer):
        return pltpu.make_async_remote_copy(
            src_ref=x_ref,
            dst_ref=recv.at[peer],
            send_sem=send_sem.at[peer],
            recv_sem=recv_sem.at[peer],
            device_id={axis: peer},
            device_id_type=MESH,
        )

    def start(k, carry):
        outgoing(lax.rem(me + k, n)).start()
        return carry

    lax.fori_loop(1, n, start, 0)
    recv[me] = x_ref[...]

    def finish(k, carry):
        peer = lax.rem(me + k, n)
        outgoing(peer).wait_send()
        incoming(peer).wait_recv()
        return carry

    lax.fori_loop(1, n, finish, 0)
    o_ref[...] = recv[0]

    def add(s, carry):
        o_ref[...] += recv[s]
        return carry

    lax.fori_loop(1, n, add, 0)


def allsum(x, axis, cid):
    n = lax.axis_size(axis)
    shape = x.shape
    flat = x.reshape(-1)
    size = flat.shape[0]
    if size <= 128:
        tile = jnp.pad(flat, (0, 128 - size)).reshape(1, 128)
    elif size % 1024 == 0:
        tile = flat.reshape(size // 128, 128)
    else:
        rows_pad = -(-size // 1024) * 8
        tile = jnp.pad(flat, (0, rows_pad * 128 - size)).reshape(rows_pad, 128)
    out = pl.pallas_call(
        functools.partial(allsum_kernel, axis, n),
        out_shape=jax.ShapeDtypeStruct(tile.shape, jnp.float32),
        in_specs=[pl.BlockSpec(memory_space=pltpu.VMEM)],
        out_specs=pl.BlockSpec(memory_space=pltpu.VMEM),
        scratch_shapes=[
            pltpu.VMEM((n,) + tile.shape, jnp.float32),
            pltpu.SemaphoreType.DMA((n,)),
            pltpu.SemaphoreType.DMA((n,)),
        ],
        compiler_params=pltpu.CompilerParams(collective_id=cid, has_side_effects=True),
    )(tile)
    return out.reshape(-1)[:size].reshape(shape)


def fused_kernel(n_rows, n_cols, z_ref, g_ref, zo_ref, go_ref, recv_z, recv_g, recv_s, rows_sum, sems):
    row = lax.axis_index("rows")
    col = lax.axis_index("cols")
    barrier = pltpu.get_barrier_semaphore()

    def greet(k, carry):
        pl.semaphore_signal(
            barrier, inc=1, device_id={"rows": lax.rem(row + k, n_rows)}, device_id_type=MESH
        )
        return carry

    lax.fori_loop(1, n_rows, greet, 0)
    for k in range(1, n_cols):
        pl.semaphore_signal(
            barrier, inc=1, device_id={"cols": lax.rem(col + k, n_cols)}, device_id_type=MESH
        )
    pl.semaphore_wait(barrier, n_rows - 1 + n_cols - 1)
    z_send, z_recv, g_send, g_recv, s_send, s_recv = sems

    def col_copy(src, dst, send, recv, peer, slot):
        return pltpu.make_async_remote_copy(
            src_ref=src,
            dst_ref=dst.at[slot],
            send_sem=send.at[peer],
            recv_sem=recv.at[slot],
            device_id={"cols": peer},
            device_id_type=MESH,
        )

    def g_copy(peer, slot):
        return pltpu.make_async_remote_copy(
            src_ref=g_ref,
            dst_ref=recv_g.at[slot],
            send_sem=g_send.at[peer],
            recv_sem=g_recv.at[slot],
            device_id={"rows": peer},
            device_id_type=MESH,
        )

    for k in range(1, n_cols):
        col_copy(z_ref, recv_z, z_send, z_recv, lax.rem(col + k, n_cols), col).start()

    def start(k, carry):
        g_copy(lax.rem(row + k, n_rows), row).start()
        return carry

    lax.fori_loop(1, n_rows, start, 0)
    recv_z[col] = z_ref[...]
    recv_g[row] = g_ref[...]

    def finish(k, carry):
        peer = lax.rem(row + k, n_rows)
        g_copy(peer, row).wait_send()
        g_copy(peer, peer).wait_recv()
        return carry

    lax.fori_loop(1, n_rows, finish, 0)
    rows_sum[...] = recv_g[0]

    def add(s, carry):
        rows_sum[...] += recv_g[s]
        return carry

    lax.fori_loop(1, n_rows, add, 0)
    for k in range(1, n_cols):
        col_copy(rows_sum, recv_s, s_send, s_recv, lax.rem(col + k, n_cols), col).start()
    recv_s[col] = rows_sum[...]
    for k in range(1, n_cols):
        peer = lax.rem(col + k, n_cols)
        col_copy(z_ref, recv_z, z_send, z_recv, peer, col).wait_send()
        col_copy(z_ref, recv_z, z_send, z_recv, peer, peer).wait_recv()
    zo_ref[...] = recv_z[0]
    for k in range(1, n_cols):
        zo_ref[...] += recv_z[k]
    for k in range(1, n_cols):
        peer = lax.rem(col + k, n_cols)
        col_copy(rows_sum, recv_s, s_send, s_recv, peer, col).wait_send()
        col_copy(rows_sum, recv_s, s_send, s_recv, peer, peer).wait_recv()
    go_ref[...] = recv_s[0]
    for k in range(1, n_cols):
        go_ref[...] += recv_s[k]


def fused_sum(z, g, cid):
    n_rows = lax.axis_size("rows")
    n_cols = lax.axis_size("cols")
    z_tile = z.reshape(-1, z.shape[-1])
    size = g.shape[0]
    g_tile = jnp.pad(g, (0, 128 - size)).reshape(1, 128)
    vmem = pl.BlockSpec(memory_space=pltpu.VMEM)
    z_out, g_out = pl.pallas_call(
        functools.partial(fused_kernel, n_rows, n_cols),
        out_shape=[
            jax.ShapeDtypeStruct(z_tile.shape, jnp.float32),
            jax.ShapeDtypeStruct(g_tile.shape, jnp.float32),
        ],
        in_specs=[vmem, vmem],
        out_specs=[vmem, vmem],
        scratch_shapes=[
            pltpu.VMEM((n_cols,) + z_tile.shape, jnp.float32),
            pltpu.VMEM((n_rows,) + g_tile.shape, jnp.float32),
            pltpu.VMEM((n_cols,) + g_tile.shape, jnp.float32),
            pltpu.VMEM(g_tile.shape, jnp.float32),
            [
                pltpu.SemaphoreType.DMA((n_cols,)),
                pltpu.SemaphoreType.DMA((n_cols,)),
                pltpu.SemaphoreType.DMA((n_rows,)),
                pltpu.SemaphoreType.DMA((n_rows,)),
                pltpu.SemaphoreType.DMA((n_cols,)),
                pltpu.SemaphoreType.DMA((n_cols,)),
            ],
        ],
        compiler_params=pltpu.CompilerParams(collective_id=cid, has_side_effects=True),
    )(z_tile, g_tile)
    return z_out.reshape(z.shape), g_out.reshape(-1)[:size]


def local(block_list, points, targets):
    row_count = lax.axis_size("rows")
    row_index = lax.axis_index("rows")
    block_rows, slot_width = block_list.shape
    coord_dim, npoints = points.shape
    outputs = targets.shape[0]
    block_len = npoints // block_rows
    slot_count = block_rows * slot_width
    entries = block_list.reshape(slot_count)
    is_live = entries >= 0
    owners = jnp.where(is_live, entries // block_rows, 0)
    local_idx = jnp.where(is_live, entries - owners * block_rows, 0)
    slot_row = jnp.arange(slot_count, dtype=jnp.int32) // slot_width
    first_row = row_index * block_rows
    place_at = jnp.where(is_live, owners, row_count)
    pick_at = jnp.minimum(place_at, row_count - 1)
    wanted = jnp.full((row_count,), -1, jnp.int32).at[place_at].set(local_idx, mode="drop")
    asking_row = jnp.full((row_count,), -1, jnp.int32).at[place_at].set(slot_row, mode="drop")
    ask_live = asking_row >= 0
    ask_row = jnp.maximum(asking_row, 0)
    request = jnp.stack([wanted, asking_row], axis=1).reshape(row_count, 1, 2)
    incoming = lax.all_to_all(request, "rows", split_axis=0, concat_axis=0, tiled=True).reshape(
        row_count, 2
    )
    in_live = incoming[:, 0] >= 0
    in_idx = jnp.maximum(incoming[:, 0], 0)
    their_row = jnp.arange(row_count, dtype=jnp.int32) * block_rows + jnp.maximum(incoming[:, 1], 0)
    in_off = in_live & (their_row != first_row + in_idx)
    collect_map = (
        (in_idx[None, :] == jnp.arange(block_rows, dtype=jnp.int32)[:, None]) & in_off[None, :]
    ).astype(jnp.float32)

    def swap(parts):
        return lax.all_to_all(parts, "rows", split_axis=0, concat_axis=0, tiled=True)

    peer_ids = jnp.arange(row_count, dtype=jnp.int32)
    to_lower = (peer_ids <= row_index)[:, None, None]
    from_self = (peer_ids == row_index)[:, None, None]

    def both_ways(blocks):
        got = swap(jnp.where(to_lower, asked_part(blocks), served_part(blocks)))
        their = jnp.where(peer_ids[:, None, None] >= row_index, got, jnp.zeros((), got.dtype))
        served_self = blocks[in_idx[row_index]]
        far = jnp.where(from_self, served_self[None], got)
        return their, per_slot(far)

    def asked_part(blocks):
        return jnp.where(ask_live[:, None, None], blocks[ask_row], jnp.zeros((), blocks.dtype))

    def served_part(blocks):
        return jnp.where(in_live[:, None, None], blocks[in_idx], jnp.zeros((), blocks.dtype))

    def per_slot(got):
        chosen = got[pick_at]
        return jnp.where(is_live[:, None, None], chosen, jnp.zeros((), chosen.dtype))

    def collect(terms):
        flat = terms.reshape(row_count, -1)
        summed = jnp.dot(
            collect_map, flat, precision=lax.Precision.HIGHEST, preferred_element_type=jnp.float32
        )
        return summed.reshape((block_rows,) + terms.shape[1:])

    def column_total(partial_value):
        return allsum(partial_value, "cols", 1 if partial_value.shape[1] == 1 else 2)

    def global_sum(values):
        return allsum(values, "rows", 0)

    own_x = points.reshape(coord_dim, block_rows, block_len).transpose(1, 0, 2)
    their_x, far_x = both_ways(own_x)
    left_x = jnp.concatenate([own_x[slot_row], their_x], axis=0)
    right_x = jnp.concatenate([far_x, own_x[in_idx]], axis=0)
    pair_live = jnp.concatenate([is_live, in_off], axis=0)
    pair_count = slot_count + row_count
    chunk = 112
    pad = (-pair_count) % chunk
    left_x = jnp.pad(left_x, ((0, pad), (0, 0), (0, 0)))
    right_x = jnp.pad(right_x, ((0, pad), (0, 0), (0, 0)))
    pair_live = jnp.pad(pair_live, (0, pad))

    def pair_step(pieces):
        lx, rx, live = pieces
        values = jnp.where(live[:, None, None], wendland(lx, rx), 0.0)
        return (values.astype(jnp.bfloat16), jnp.sum(values, axis=2), jnp.sum(values, axis=1))

    kernel_bf, row_sums, col_sums = lax.map(
        pair_step,
        (
            left_x.reshape(-1, chunk, coord_dim, block_len),
            right_x.reshape(-1, chunk, coord_dim, block_len),
            pair_live.reshape(-1, chunk),
        ),
    )
    kernel_bf = kernel_bf.reshape(-1, block_len, block_len)
    row_sums = row_sums.reshape(-1, block_len)
    col_sums = col_sums.reshape(-1, block_len)
    own_k = kernel_bf[:slot_count]
    in_k = kernel_bf[slot_count:pair_count]
    degree_direct = jnp.sum(row_sums[:slot_count].reshape(block_rows, slot_width, block_len), axis=1)
    degree_mirror = collect(col_sums[slot_count:pair_count])
    degree_part = (degree_direct + degree_mirror)[:, None, :]
    inv_root = 1.0 / jnp.sqrt(1.0 + column_total(degree_part))

    def apply_partial(weights):
        their_w, far_w = both_ways(weights)
        direct = jnp.einsum(
            "rkab,rkob->roa",
            own_k.reshape(block_rows, slot_width, block_len, block_len),
            far_w.reshape(block_rows, slot_width, outputs, block_len),
            preferred_element_type=jnp.float32,
        )
        mirror = jnp.einsum("eab,eoa->eob", in_k, their_w, preferred_element_type=jnp.float32)
        return direct + collect(mirror)

    resid = targets.reshape(outputs, block_rows, block_len).transpose(1, 0, 2)
    direction = resid
    solution = jnp.zeros_like(resid)
    norm_now = jnp.sum(resid * resid, axis=(0, 2))
    first_col = lax.axis_index("cols") == 0
    for iteration in range(ITERS):
        weights = (direction * inv_root).astype(jnp.bfloat16)
        z_part = apply_partial(weights)
        own_term = jnp.where(first_col, REG * jnp.sum(direction * direction, axis=(0, 2)), 0.0)
        curv_part = own_term + jnp.sum(direction * (inv_root * z_part), axis=(0, 2))
        if iteration == 0:
            norm_part = jnp.where(first_col, norm_now, 0.0)
            z_total, both = fused_sum(z_part, jnp.concatenate([norm_part, curv_part]), 6)
            norm_now, curvature = both[:outputs], both[outputs:]
        else:
            z_total, curvature = fused_sum(z_part, curv_part, 7)
        applied = REG * direction + inv_root * z_total
        step_size = norm_now / curvature
        solution = solution + step_size[None, :, None] * direction
        resid = resid - step_size[None, :, None] * applied
        if iteration + 1 < ITERS:
            norm_next = global_sum(jnp.sum(resid * resid, axis=(0, 2)))
            direction = resid + (norm_next / norm_now)[None, :, None] * direction
            norm_now = norm_next
    return (
        solution.transpose(1, 0, 2).reshape(outputs, npoints),
        resid.transpose(1, 0, 2).reshape(outputs, npoints),
    )


def solution(mesh):
    placed = (P("rows", "cols"), P(None, "rows"), P(None, "rows"))
    return jax.shard_map(
        local,
        mesh=mesh,
        in_specs=placed,
        out_specs=(P(None, "rows"), P(None, "rows")),
        check_vma=False,
    )
```

```python
import functools

import jax
import jax.numpy as jnp
from jax import lax
from jax.experimental import pallas as pl
from jax.experimental.pallas import tpu as pltpu
from jax.sharding import PartitionSpec as P

MESH = pl.DeviceIdType.MESH

ITERS = 2


REG = 1.5
RADIUS = 0.25


def wendland(left_x, right_x):
    left_f = left_x.astype(jnp.float32)
    right_f = right_x.astype(jnp.float32)
    left_sq = jnp.sum(left_f * left_f, axis=1)
    right_sq = jnp.sum(right_f * right_f, axis=1)
    inner_prod = jnp.einsum("nda,ndb->nab", left_f, right_f, precision=lax.Precision.HIGHEST)
    dist_sq = left_sq[:, :, None] + right_sq[:, None, :] - 2.0 * inner_prod
    scaled = jnp.sqrt(jnp.maximum(dist_sq, 0.0)) / RADIUS
    remain = jnp.maximum(1.0 - scaled, 0.0)
    square = remain * remain
    return square * square * (4.0 * scaled + 1.0)


def allsum_kernel(axis, n, x_ref, o_ref, recv, send_sem, recv_sem):
    me = lax.axis_index(axis)
    barrier = pltpu.get_barrier_semaphore()

    def greet(k, carry):
        peer = lax.rem(me + k, n)
        pl.semaphore_signal(barrier, inc=1, device_id={axis: peer}, device_id_type=MESH)
        return carry

    lax.fori_loop(1, n, greet, 0)
    pl.semaphore_wait(barrier, n - 1)

    def outgoing(peer):
        return pltpu.make_async_remote_copy(
            src_ref=x_ref,
            dst_ref=recv.at[me],
            send_sem=send_sem.at[peer],
            recv_sem=recv_sem.at[me],
            device_id={axis: peer},
            device_id_type=MESH,
        )

    def incoming(peer):
        return pltpu.make_async_remote_copy(
            src_ref=x_ref,
            dst_ref=recv.at[peer],
            send_sem=send_sem.at[peer],
            recv_sem=recv_sem.at[peer],
            device_id={axis: peer},
            device_id_type=MESH,
        )

    def start(k, carry):
        outgoing(lax.rem(me + k, n)).start()
        return carry

    lax.fori_loop(1, n, start, 0)
    recv[me] = x_ref[...]

    def finish(k, carry):
        peer = lax.rem(me + k, n)
        outgoing(peer).wait_send()
        incoming(peer).wait_recv()
        return carry

    lax.fori_loop(1, n, finish, 0)
    o_ref[...] = recv[0]

    def add(s, carry):
        o_ref[...] += recv[s]
        return carry

    lax.fori_loop(1, n, add, 0)


def allsum(x, axis, cid):
    n = lax.axis_size(axis)
    shape = x.shape
    flat = x.reshape(-1)
    size = flat.shape[0]
    if size <= 128:
        tile = jnp.pad(flat, (0, 128 - size)).reshape(1, 128)
    elif size % 1024 == 0:
        tile = flat.reshape(size // 128, 128)
    else:
        rows_pad = -(-size // 1024) * 8
        tile = jnp.pad(flat, (0, rows_pad * 128 - size)).reshape(rows_pad, 128)
    out = pl.pallas_call(
        functools.partial(allsum_kernel, axis, n),
        out_shape=jax.ShapeDtypeStruct(tile.shape, jnp.float32),
        in_specs=[pl.BlockSpec(memory_space=pltpu.VMEM)],
        out_specs=pl.BlockSpec(memory_space=pltpu.VMEM),
        scratch_shapes=[
            pltpu.VMEM((n,) + tile.shape, jnp.float32),
            pltpu.SemaphoreType.DMA((n,)),
            pltpu.SemaphoreType.DMA((n,)),
        ],
        compiler_params=pltpu.CompilerParams(collective_id=cid, has_side_effects=True),
    )(tile)
    return out.reshape(-1)[:size].reshape(shape)


def fused_kernel(n_rows, n_cols, z_ref, g_ref, zo_ref, go_ref, recv_z, recv_g, recv_s, rows_sum, sems):
    row = lax.axis_index("rows")
    col = lax.axis_index("cols")
    barrier = pltpu.get_barrier_semaphore()

    def greet(k, carry):
        pl.semaphore_signal(
            barrier, inc=1, device_id={"rows": lax.rem(row + k, n_rows)}, device_id_type=MESH
        )
        return carry

    lax.fori_loop(1, n_rows, greet, 0)
    for k in range(1, n_cols):
        pl.semaphore_signal(
            barrier, inc=1, device_id={"cols": lax.rem(col + k, n_cols)}, device_id_type=MESH
        )
    pl.semaphore_wait(barrier, n_rows - 1 + n_cols - 1)
    z_send, z_recv, g_send, g_recv, s_send, s_recv = sems

    def col_copy(src, dst, send, recv, peer, slot):
        return pltpu.make_async_remote_copy(
            src_ref=src,
            dst_ref=dst.at[slot],
            send_sem=send.at[peer],
            recv_sem=recv.at[slot],
            device_id={"cols": peer},
            device_id_type=MESH,
        )

    def g_copy(peer, slot):
        return pltpu.make_async_remote_copy(
            src_ref=g_ref,
            dst_ref=recv_g.at[slot],
            send_sem=g_send.at[peer],
            recv_sem=g_recv.at[slot],
            device_id={"rows": peer},
            device_id_type=MESH,
        )

    for k in range(1, n_cols):
        col_copy(z_ref, recv_z, z_send, z_recv, lax.rem(col + k, n_cols), col).start()

    def start(k, carry):
        g_copy(lax.rem(row + k, n_rows), row).start()
        return carry

    lax.fori_loop(1, n_rows, start, 0)
    recv_z[col] = z_ref[...]
    recv_g[row] = g_ref[...]

    def finish(k, carry):
        peer = lax.rem(row + k, n_rows)
        g_copy(peer, row).wait_send()
        g_copy(peer, peer).wait_recv()
        return carry

    lax.fori_loop(1, n_rows, finish, 0)
    rows_sum[...] = recv_g[0]

    def add(s, carry):
        rows_sum[...] += recv_g[s]
        return carry

    lax.fori_loop(1, n_rows, add, 0)
    for k in range(1, n_cols):
        col_copy(rows_sum, recv_s, s_send, s_recv, lax.rem(col + k, n_cols), col).start()
    recv_s[col] = rows_sum[...]
    for k in range(1, n_cols):
        peer = lax.rem(col + k, n_cols)
        col_copy(z_ref, recv_z, z_send, z_recv, peer, col).wait_send()
        col_copy(z_ref, recv_z, z_send, z_recv, peer, peer).wait_recv()
    zo_ref[...] = recv_z[0]
    for k in range(1, n_cols):
        zo_ref[...] += recv_z[k]
    for k in range(1, n_cols):
        peer = lax.rem(col + k, n_cols)
        col_copy(rows_sum, recv_s, s_send, s_recv, peer, col).wait_send()
        col_copy(rows_sum, recv_s, s_send, s_recv, peer, peer).wait_recv()
    go_ref[...] = recv_s[0]
    for k in range(1, n_cols):
        go_ref[...] += recv_s[k]


def fused_sum(z, g, cid):
    n_rows = lax.axis_size("rows")
    n_cols = lax.axis_size("cols")
    z_tile = z.reshape(-1, z.shape[-1])
    size = g.shape[0]
    g_tile = jnp.pad(g, (0, 128 - size)).reshape(1, 128)
    vmem = pl.BlockSpec(memory_space=pltpu.VMEM)
    z_out, g_out = pl.pallas_call(
        functools.partial(fused_kernel, n_rows, n_cols),
        out_shape=[
            jax.ShapeDtypeStruct(z_tile.shape, jnp.float32),
            jax.ShapeDtypeStruct(g_tile.shape, jnp.float32),
        ],
        in_specs=[vmem, vmem],
        out_specs=[vmem, vmem],
        scratch_shapes=[
            pltpu.VMEM((n_cols,) + z_tile.shape, jnp.float32),
            pltpu.VMEM((n_rows,) + g_tile.shape, jnp.float32),
            pltpu.VMEM((n_cols,) + g_tile.shape, jnp.float32),
            pltpu.VMEM(g_tile.shape, jnp.float32),
            [
                pltpu.SemaphoreType.DMA((n_cols,)),
                pltpu.SemaphoreType.DMA((n_cols,)),
                pltpu.SemaphoreType.DMA((n_rows,)),
                pltpu.SemaphoreType.DMA((n_rows,)),
                pltpu.SemaphoreType.DMA((n_cols,)),
                pltpu.SemaphoreType.DMA((n_cols,)),
            ],
        ],
        compiler_params=pltpu.CompilerParams(collective_id=cid, has_side_effects=True),
    )(z_tile, g_tile)
    return z_out.reshape(z.shape), g_out.reshape(-1)[:size]


def local(block_list, points, targets):
    row_count = lax.axis_size("rows")
    row_index = lax.axis_index("rows")
    block_rows, slot_width = block_list.shape
    coord_dim, npoints = points.shape
    outputs = targets.shape[0]
    block_len = npoints // block_rows
    slot_count = block_rows * slot_width
    entries = block_list.reshape(slot_count)
    is_live = entries >= 0
    owners = jnp.where(is_live, entries // block_rows, 0)
    local_idx = jnp.where(is_live, entries - owners * block_rows, 0)
    slot_row = jnp.arange(slot_count, dtype=jnp.int32) // slot_width
    first_row = row_index * block_rows
    place_at = jnp.where(is_live, owners, row_count)
    pick_at = jnp.minimum(place_at, row_count - 1)
    wanted = jnp.full((row_count,), -1, jnp.int32).at[place_at].set(local_idx, mode="drop")
    asking_row = jnp.full((row_count,), -1, jnp.int32).at[place_at].set(slot_row, mode="drop")
    ask_live = asking_row >= 0
    ask_row = jnp.maximum(asking_row, 0)
    request = jnp.stack([wanted, asking_row], axis=1).reshape(row_count, 1, 2)
    incoming = lax.all_to_all(request, "rows", split_axis=0, concat_axis=0, tiled=True).reshape(
        row_count, 2
    )
    in_live = incoming[:, 0] >= 0
    in_idx = jnp.maximum(incoming[:, 0], 0)
    their_row = jnp.arange(row_count, dtype=jnp.int32) * block_rows + jnp.maximum(incoming[:, 1], 0)
    in_off = in_live & (their_row != first_row + in_idx)
    collect_map = (
        (in_idx[None, :] == jnp.arange(block_rows, dtype=jnp.int32)[:, None]) & in_off[None, :]
    ).astype(jnp.float32)

    def swap(parts):
        return lax.all_to_all(parts, "rows", split_axis=0, concat_axis=0, tiled=True)

    peer_ids = jnp.arange(row_count, dtype=jnp.int32)
    to_lower = (peer_ids <= row_index)[:, None, None]
    from_self = (peer_ids == row_index)[:, None, None]

    def both_ways(blocks):
        got = swap(jnp.where(to_lower, asked_part(blocks), served_part(blocks)))
        their = jnp.where(peer_ids[:, None, None] >= row_index, got, jnp.zeros((), got.dtype))
        served_self = blocks[in_idx[row_index]]
        far = jnp.where(from_self, served_self[None], got)
        return their, per_slot(far)

    def asked_part(blocks):
        return jnp.where(ask_live[:, None, None], blocks[ask_row], jnp.zeros((), blocks.dtype))

    def served_part(blocks):
        return jnp.where(in_live[:, None, None], blocks[in_idx], jnp.zeros((), blocks.dtype))

    def per_slot(got):
        chosen = got[pick_at]
        return jnp.where(is_live[:, None, None], chosen, jnp.zeros((), chosen.dtype))

    def collect(terms):
        flat = terms.reshape(row_count, -1)
        summed = jnp.dot(
            collect_map, flat, precision=lax.Precision.HIGHEST, preferred_element_type=jnp.float32
        )
        return summed.reshape((block_rows,) + terms.shape[1:])

    def column_total(partial_value):
        return allsum(partial_value, "cols", 1 if partial_value.shape[1] == 1 else 2)

    def global_sum(values):
        return allsum(values, "rows", 0)

    own_x = points.reshape(coord_dim, block_rows, block_len).transpose(1, 0, 2)
    their_x, far_x = both_ways(own_x)
    left_x = jnp.concatenate([own_x[slot_row], their_x], axis=0)
    right_x = jnp.concatenate([far_x, own_x[in_idx]], axis=0)
    pair_live = jnp.concatenate([is_live, in_off], axis=0)
    pair_count = slot_count + row_count
    chunk = 112
    pad = (-pair_count) % chunk
    left_x = jnp.pad(left_x, ((0, pad), (0, 0), (0, 0)))
    right_x = jnp.pad(right_x, ((0, pad), (0, 0), (0, 0)))
    pair_live = jnp.pad(pair_live, (0, pad))

    def pair_step(pieces):
        lx, rx, live = pieces
        values = jnp.where(live[:, None, None], wendland(lx, rx), 0.0)
        return (values.astype(jnp.bfloat16), jnp.sum(values, axis=2), jnp.sum(values, axis=1))

    kernel_bf, row_sums, col_sums = lax.map(
        pair_step,
        (
            left_x.reshape(-1, chunk, coord_dim, block_len),
            right_x.reshape(-1, chunk, coord_dim, block_len),
            pair_live.reshape(-1, chunk),
        ),
    )
    kernel_bf = kernel_bf.reshape(-1, block_len, block_len)
    row_sums = row_sums.reshape(-1, block_len)
    col_sums = col_sums.reshape(-1, block_len)
    own_k = kernel_bf[:slot_count]
    in_k = kernel_bf[slot_count:pair_count]
    degree_direct = jnp.sum(row_sums[:slot_count].reshape(block_rows, slot_width, block_len), axis=1)
    degree_mirror = collect(col_sums[slot_count:pair_count])
    degree_part = (degree_direct + degree_mirror)[:, None, :]
    inv_root = 1.0 / jnp.sqrt(1.0 + column_total(degree_part))

    def apply_partial(weights):
        their_w, far_w = both_ways(weights)
        direct = jnp.einsum(
            "rkab,rkob->roa",
            own_k.reshape(block_rows, slot_width, block_len, block_len),
            far_w.reshape(block_rows, slot_width, outputs, block_len),
            preferred_element_type=jnp.float32,
        )
        mirror = jnp.einsum("eab,eoa->eob", in_k, their_w, preferred_element_type=jnp.float32)
        return direct + collect(mirror)

    resid = targets.reshape(outputs, block_rows, block_len).transpose(1, 0, 2)
    direction = resid
    solution = jnp.zeros_like(resid)
    norm_now = jnp.sum(resid * resid, axis=(0, 2))
    first_col = lax.axis_index("cols") == 0
    for iteration in range(ITERS):
        weights = (direction * inv_root).astype(jnp.bfloat16)
        z_part = apply_partial(weights)
        own_term = jnp.where(first_col, REG * jnp.sum(direction * direction, axis=(0, 2)), 0.0)
        curv_part = own_term + jnp.sum(direction * (inv_root * z_part), axis=(0, 2))
        if iteration == 0:
            norm_part = jnp.where(first_col, norm_now, 0.0)
            z_total, both = fused_sum(z_part, jnp.concatenate([norm_part, curv_part]), 6)
            norm_now, curvature = both[:outputs], both[outputs:]
        else:
            z_total, curvature = fused_sum(z_part, curv_part, 7)
        applied = REG * direction + inv_root * z_total
        step_size = norm_now / curvature
        solution = solution + step_size[None, :, None] * direction
        resid = resid - step_size[None, :, None] * applied
        if iteration + 1 < ITERS:
            norm_next = global_sum(jnp.sum(resid * resid, axis=(0, 2)))
            direction = resid + (norm_next / norm_now)[None, :, None] * direction
            norm_now = norm_next
    return (
        solution.transpose(1, 0, 2).reshape(outputs, npoints),
        resid.transpose(1, 0, 2).reshape(outputs, npoints),
    )


def solution(mesh):
    placed = (P("rows", "cols"), P(None, "rows"), P(None, "rows"))
    return jax.shard_map(
        local,
        mesh=mesh,
        in_specs=placed,
        out_specs=(P(None, "rows"), P(None, "rows")),
        check_vma=False,
    )
```

```python
import functools

import jax
import jax.numpy as jnp
from jax import lax
from jax.experimental import pallas as pl
from jax.experimental.pallas import tpu as pltpu
from jax.sharding import PartitionSpec as P

MESH = pl.DeviceIdType.MESH

ITERS = 2


REG = 1.5
RADIUS = 0.25


def wendland(left_x, right_x):
    left_f = left_x.astype(jnp.float32)
    right_f = right_x.astype(jnp.float32)
    left_sq = jnp.sum(left_f * left_f, axis=1)
    right_sq = jnp.sum(right_f * right_f, axis=1)
    inner_prod = jnp.einsum("nda,ndb->nab", left_f, right_f, precision=lax.Precision.HIGHEST)
    dist_sq = left_sq[:, :, None] + right_sq[:, None, :] - 2.0 * inner_prod
    scaled = jnp.sqrt(jnp.maximum(dist_sq, 0.0)) / RADIUS
    remain = jnp.maximum(1.0 - scaled, 0.0)
    square = remain * remain
    return square * square * (4.0 * scaled + 1.0)


def allsum_kernel(axis, n, x_ref, o_ref, recv, send_sem, recv_sem):
    me = lax.axis_index(axis)
    barrier = pltpu.get_barrier_semaphore()

    def greet(k, carry):
        peer = lax.rem(me + k, n)
        pl.semaphore_signal(barrier, inc=1, device_id={axis: peer}, device_id_type=MESH)
        return carry

    lax.fori_loop(1, n, greet, 0)
    pl.semaphore_wait(barrier, n - 1)

    def outgoing(peer):
        return pltpu.make_async_remote_copy(
            src_ref=x_ref,
            dst_ref=recv.at[me],
            send_sem=send_sem.at[peer],
            recv_sem=recv_sem.at[me],
            device_id={axis: peer},
            device_id_type=MESH,
        )

    def incoming(peer):
        return pltpu.make_async_remote_copy(
            src_ref=x_ref,
            dst_ref=recv.at[peer],
            send_sem=send_sem.at[peer],
            recv_sem=recv_sem.at[peer],
            device_id={axis: peer},
            device_id_type=MESH,
        )

    def start(k, carry):
        outgoing(lax.rem(me + k, n)).start()
        return carry

    lax.fori_loop(1, n, start, 0)
    recv[me] = x_ref[...]

    def finish(k, carry):
        peer = lax.rem(me + k, n)
        outgoing(peer).wait_send()
        incoming(peer).wait_recv()
        return carry

    lax.fori_loop(1, n, finish, 0)
    o_ref[...] = recv[0]

    def add(s, carry):
        o_ref[...] += recv[s]
        return carry

    lax.fori_loop(1, n, add, 0)


def allsum(x, axis, cid):
    n = lax.axis_size(axis)
    shape = x.shape
    flat = x.reshape(-1)
    size = flat.shape[0]
    if size <= 128:
        tile = jnp.pad(flat, (0, 128 - size)).reshape(1, 128)
    elif size % 1024 == 0:
        tile = flat.reshape(size // 128, 128)
    else:
        rows_pad = -(-size // 1024) * 8
        tile = jnp.pad(flat, (0, rows_pad * 128 - size)).reshape(rows_pad, 128)
    out = pl.pallas_call(
        functools.partial(allsum_kernel, axis, n),
        out_shape=jax.ShapeDtypeStruct(tile.shape, jnp.float32),
        in_specs=[pl.BlockSpec(memory_space=pltpu.VMEM)],
        out_specs=pl.BlockSpec(memory_space=pltpu.VMEM),
        scratch_shapes=[
            pltpu.VMEM((n,) + tile.shape, jnp.float32),
            pltpu.SemaphoreType.DMA((n,)),
            pltpu.SemaphoreType.DMA((n,)),
        ],
        compiler_params=pltpu.CompilerParams(collective_id=cid, has_side_effects=True),
    )(tile)
    return out.reshape(-1)[:size].reshape(shape)


def fused_kernel(n_rows, n_cols, z_ref, g_ref, zo_ref, go_ref, recv_z, recv_g, recv_s, rows_sum, sems):
    row = lax.axis_index("rows")
    col = lax.axis_index("cols")
    barrier = pltpu.get_barrier_semaphore()

    def greet(k, carry):
        pl.semaphore_signal(
            barrier, inc=1, device_id={"rows": lax.rem(row + k, n_rows)}, device_id_type=MESH
        )
        return carry

    lax.fori_loop(1, n_rows, greet, 0)
    for k in range(1, n_cols):
        pl.semaphore_signal(
            barrier, inc=1, device_id={"cols": lax.rem(col + k, n_cols)}, device_id_type=MESH
        )
    pl.semaphore_wait(barrier, n_rows - 1 + n_cols - 1)
    z_send, z_recv, g_send, g_recv, s_send, s_recv = sems

    def col_copy(src, dst, send, recv, peer, slot):
        return pltpu.make_async_remote_copy(
            src_ref=src,
            dst_ref=dst.at[slot],
            send_sem=send.at[peer],
            recv_sem=recv.at[slot],
            device_id={"cols": peer},
            device_id_type=MESH,
        )

    def g_copy(peer, slot):
        return pltpu.make_async_remote_copy(
            src_ref=g_ref,
            dst_ref=recv_g.at[slot],
            send_sem=g_send.at[peer],
            recv_sem=g_recv.at[slot],
            device_id={"rows": peer},
            device_id_type=MESH,
        )

    for k in range(1, n_cols):
        col_copy(z_ref, recv_z, z_send, z_recv, lax.rem(col + k, n_cols), col).start()

    def start(k, carry):
        g_copy(lax.rem(row + k, n_rows), row).start()
        return carry

    lax.fori_loop(1, n_rows, start, 0)
    recv_z[col] = z_ref[...]
    recv_g[row] = g_ref[...]

    def finish(k, carry):
        peer = lax.rem(row + k, n_rows)
        g_copy(peer, row).wait_send()
        g_copy(peer, peer).wait_recv()
        return carry

    lax.fori_loop(1, n_rows, finish, 0)
    rows_sum[...] = recv_g[0]

    def add(s, carry):
        rows_sum[...] += recv_g[s]
        return carry

    lax.fori_loop(1, n_rows, add, 0)
    for k in range(1, n_cols):
        col_copy(rows_sum, recv_s, s_send, s_recv, lax.rem(col + k, n_cols), col).start()
    recv_s[col] = rows_sum[...]
    for k in range(1, n_cols):
        peer = lax.rem(col + k, n_cols)
        col_copy(z_ref, recv_z, z_send, z_recv, peer, col).wait_send()
        col_copy(z_ref, recv_z, z_send, z_recv, peer, peer).wait_recv()
    zo_ref[...] = recv_z[0]
    for k in range(1, n_cols):
        zo_ref[...] += recv_z[k]
    for k in range(1, n_cols):
        peer = lax.rem(col + k, n_cols)
        col_copy(rows_sum, recv_s, s_send, s_recv, peer, col).wait_send()
        col_copy(rows_sum, recv_s, s_send, s_recv, peer, peer).wait_recv()
    go_ref[...] = recv_s[0]
    for k in range(1, n_cols):
        go_ref[...] += recv_s[k]


def fused_sum(z, g, cid):
    n_rows = lax.axis_size("rows")
    n_cols = lax.axis_size("cols")
    z_tile = z.reshape(-1, z.shape[-1])
    size = g.shape[0]
    g_tile = jnp.pad(g, (0, 128 - size)).reshape(1, 128)
    vmem = pl.BlockSpec(memory_space=pltpu.VMEM)
    z_out, g_out = pl.pallas_call(
        functools.partial(fused_kernel, n_rows, n_cols),
        out_shape=[
            jax.ShapeDtypeStruct(z_tile.shape, jnp.float32),
            jax.ShapeDtypeStruct(g_tile.shape, jnp.float32),
        ],
        in_specs=[vmem, vmem],
        out_specs=[vmem, vmem],
        scratch_shapes=[
            pltpu.VMEM((n_cols,) + z_tile.shape, jnp.float32),
            pltpu.VMEM((n_rows,) + g_tile.shape, jnp.float32),
            pltpu.VMEM((n_cols,) + g_tile.shape, jnp.float32),
            pltpu.VMEM(g_tile.shape, jnp.float32),
            [
                pltpu.SemaphoreType.DMA((n_cols,)),
                pltpu.SemaphoreType.DMA((n_cols,)),
                pltpu.SemaphoreType.DMA((n_rows,)),
                pltpu.SemaphoreType.DMA((n_rows,)),
                pltpu.SemaphoreType.DMA((n_cols,)),
                pltpu.SemaphoreType.DMA((n_cols,)),
            ],
        ],
        compiler_params=pltpu.CompilerParams(collective_id=cid, has_side_effects=True),
    )(z_tile, g_tile)
    return z_out.reshape(z.shape), g_out.reshape(-1)[:size]


def local(block_list, points, targets):
    row_count = lax.axis_size("rows")
    row_index = lax.axis_index("rows")
    block_rows, slot_width = block_list.shape
    coord_dim, npoints = points.shape
    outputs = targets.shape[0]
    block_len = npoints // block_rows
    slot_count = block_rows * slot_width
    entries = block_list.reshape(slot_count)
    is_live = entries >= 0
    owners = jnp.where(is_live, entries // block_rows, 0)
    local_idx = jnp.where(is_live, entries - owners * block_rows, 0)
    slot_row = jnp.arange(slot_count, dtype=jnp.int32) // slot_width
    first_row = row_index * block_rows
    place_at = jnp.where(is_live, owners, row_count)
    pick_at = jnp.minimum(place_at, row_count - 1)
    wanted = jnp.full((row_count,), -1, jnp.int32).at[place_at].set(local_idx, mode="drop")
    asking_row = jnp.full((row_count,), -1, jnp.int32).at[place_at].set(slot_row, mode="drop")
    ask_live = asking_row >= 0
    ask_row = jnp.maximum(asking_row, 0)
    own_x = points.reshape(coord_dim, block_rows, block_len).transpose(1, 0, 2)
    asked_x = jnp.where(ask_live[:, None, None], own_x[ask_row], jnp.zeros((), own_x.dtype))
    request = jnp.zeros((row_count, coord_dim, 128), own_x.dtype)
    request = request.at[:, 0, 0].set(wanted.astype(own_x.dtype))
    request = request.at[:, 0, 1].set(asking_row.astype(own_x.dtype))
    first_swap = lax.all_to_all(
        jnp.concatenate([asked_x, request], axis=2), "rows", split_axis=0, concat_axis=0, tiled=True
    )
    their_x = first_swap[:, :, :block_len]
    incoming = first_swap[:, 0, block_len:block_len + 2].astype(jnp.int32)
    in_live = incoming[:, 0] >= 0
    in_idx = jnp.maximum(incoming[:, 0], 0)
    their_row = jnp.arange(row_count, dtype=jnp.int32) * block_rows + jnp.maximum(incoming[:, 1], 0)
    in_off = in_live & (their_row != first_row + in_idx)
    collect_map = (
        (in_idx[None, :] == jnp.arange(block_rows, dtype=jnp.int32)[:, None]) & in_off[None, :]
    ).astype(jnp.float32)

    def swap(parts):
        return lax.all_to_all(parts, "rows", split_axis=0, concat_axis=0, tiled=True)

    peer_ids = jnp.arange(row_count, dtype=jnp.int32)
    to_lower = (peer_ids <= row_index)[:, None, None]
    from_self = (peer_ids == row_index)[:, None, None]

    def both_ways(blocks):
        got = swap(jnp.where(to_lower, asked_part(blocks), served_part(blocks)))
        their = jnp.where(peer_ids[:, None, None] >= row_index, got, jnp.zeros((), got.dtype))
        served_self = blocks[in_idx[row_index]]
        far = jnp.where(from_self, served_self[None], got)
        return their, per_slot(far)

    def asked_part(blocks):
        return jnp.where(ask_live[:, None, None], blocks[ask_row], jnp.zeros((), blocks.dtype))

    def served_part(blocks):
        return jnp.where(in_live[:, None, None], blocks[in_idx], jnp.zeros((), blocks.dtype))

    def per_slot(got):
        chosen = got[pick_at]
        return jnp.where(is_live[:, None, None], chosen, jnp.zeros((), chosen.dtype))

    def collect(terms):
        flat = terms.reshape(row_count, -1)
        summed = jnp.dot(
            collect_map, flat, precision=lax.Precision.HIGHEST, preferred_element_type=jnp.float32
        )
        return summed.reshape((block_rows,) + terms.shape[1:])

    def column_total(partial_value):
        return allsum(partial_value, "cols", 1 if partial_value.shape[1] == 1 else 2)

    def global_sum(values):
        return allsum(values, "rows", 0)

    far_x = per_slot(swap(served_part(own_x)))

    def pair_pass(lx, rx, live):
        values = jnp.where(live[:, None, None], wendland(lx, rx), 0.0)
        return (values.astype(jnp.bfloat16), jnp.sum(values, axis=2), jnp.sum(values, axis=1))

    in_k, _, in_col_sums = pair_pass(their_x, own_x[in_idx], in_off)
    own_k, own_row_sums, _ = pair_pass(own_x[slot_row], far_x, is_live)
    degree_direct = jnp.sum(own_row_sums.reshape(block_rows, slot_width, block_len), axis=1)
    degree_mirror = collect(in_col_sums)
    degree_part = (degree_direct + degree_mirror)[:, None, :]
    inv_root = 1.0 / jnp.sqrt(1.0 + column_total(degree_part))

    def apply_partial(weights):
        their_w, far_w = both_ways(weights)
        direct = jnp.einsum(
            "rkab,rkob->roa",
            own_k.reshape(block_rows, slot_width, block_len, block_len),
            far_w.reshape(block_rows, slot_width, outputs, block_len),
            preferred_element_type=jnp.float32,
        )
        mirror = jnp.einsum("eab,eoa->eob", in_k, their_w, preferred_element_type=jnp.float32)
        return direct + collect(mirror)

    resid = targets.reshape(outputs, block_rows, block_len).transpose(1, 0, 2)
    direction = resid
    solution = jnp.zeros_like(resid)
    norm_now = jnp.sum(resid * resid, axis=(0, 2))
    first_col = lax.axis_index("cols") == 0
    for iteration in range(ITERS):
        weights = (direction * inv_root).astype(jnp.bfloat16)
        z_part = apply_partial(weights)
        own_term = jnp.where(first_col, REG * jnp.sum(direction * direction, axis=(0, 2)), 0.0)
        curv_part = own_term + jnp.sum(direction * (inv_root * z_part), axis=(0, 2))
        if iteration == 0:
            norm_part = jnp.where(first_col, norm_now, 0.0)
            z_total, both = fused_sum(z_part, jnp.concatenate([norm_part, curv_part]), 6)
            norm_now, curvature = both[:outputs], both[outputs:]
        else:
            z_total, curvature = fused_sum(z_part, curv_part, 7)
        applied = REG * direction + inv_root * z_total
        step_size = norm_now / curvature
        solution = solution + step_size[None, :, None] * direction
        resid = resid - step_size[None, :, None] * applied
        if iteration + 1 < ITERS:
            norm_next = global_sum(jnp.sum(resid * resid, axis=(0, 2)))
            direction = resid + (norm_next / norm_now)[None, :, None] * direction
            norm_now = norm_next
    return (
        solution.transpose(1, 0, 2).reshape(outputs, npoints),
        resid.transpose(1, 0, 2).reshape(outputs, npoints),
    )


def solution(mesh):
    placed = (P("rows", "cols"), P(None, "rows"), P(None, "rows"))
    return jax.shard_map(
        local,
        mesh=mesh,
        in_specs=placed,
        out_specs=(P(None, "rows"), P(None, "rows")),
        check_vma=False,
    )
```

```python
import functools

import jax
import jax.numpy as jnp
from jax import lax
from jax.experimental import pallas as pl
from jax.experimental.pallas import tpu as pltpu
from jax.sharding import PartitionSpec as P

MESH = pl.DeviceIdType.MESH

ITERS = 2


REG = 1.5
RADIUS = 0.25


def wendland(left_x, right_x):
    left_f = left_x.astype(jnp.float32)
    right_f = right_x.astype(jnp.float32)
    left_sq = jnp.sum(left_f * left_f, axis=1)
    right_sq = jnp.sum(right_f * right_f, axis=1)
    inner_prod = jnp.einsum("nda,ndb->nab", left_f, right_f, precision=lax.Precision.HIGHEST)
    dist_sq = left_sq[:, :, None] + right_sq[:, None, :] - 2.0 * inner_prod
    scaled = jnp.sqrt(jnp.maximum(dist_sq, 0.0)) / RADIUS
    remain = jnp.maximum(1.0 - scaled, 0.0)
    square = remain * remain
    return square * square * (4.0 * scaled + 1.0)


def allsum_kernel(axis, n, x_ref, o_ref, recv, send_sem, recv_sem):
    me = lax.axis_index(axis)
    barrier = pltpu.get_barrier_semaphore()

    def greet(k, carry):
        peer = lax.rem(me + k, n)
        pl.semaphore_signal(barrier, inc=1, device_id={axis: peer}, device_id_type=MESH)
        return carry

    lax.fori_loop(1, n, greet, 0)
    pl.semaphore_wait(barrier, n - 1)

    def outgoing(peer):
        return pltpu.make_async_remote_copy(
            src_ref=x_ref,
            dst_ref=recv.at[me],
            send_sem=send_sem.at[peer],
            recv_sem=recv_sem.at[me],
            device_id={axis: peer},
            device_id_type=MESH,
        )

    def incoming(peer):
        return pltpu.make_async_remote_copy(
            src_ref=x_ref,
            dst_ref=recv.at[peer],
            send_sem=send_sem.at[peer],
            recv_sem=recv_sem.at[peer],
            device_id={axis: peer},
            device_id_type=MESH,
        )

    def start(k, carry):
        outgoing(lax.rem(me + k, n)).start()
        return carry

    lax.fori_loop(1, n, start, 0)
    recv[me] = x_ref[...]

    def finish(k, carry):
        peer = lax.rem(me + k, n)
        outgoing(peer).wait_send()
        incoming(peer).wait_recv()
        return carry

    lax.fori_loop(1, n, finish, 0)
    o_ref[...] = recv[0]

    def add(s, carry):
        o_ref[...] += recv[s]
        return carry

    lax.fori_loop(1, n, add, 0)


def allsum(x, axis, cid):
    n = lax.axis_size(axis)
    shape = x.shape
    flat = x.reshape(-1)
    size = flat.shape[0]
    if size <= 128:
        tile = jnp.pad(flat, (0, 128 - size)).reshape(1, 128)
    elif size % 1024 == 0:
        tile = flat.reshape(size // 128, 128)
    else:
        rows_pad = -(-size // 1024) * 8
        tile = jnp.pad(flat, (0, rows_pad * 128 - size)).reshape(rows_pad, 128)
    out = pl.pallas_call(
        functools.partial(allsum_kernel, axis, n),
        out_shape=jax.ShapeDtypeStruct(tile.shape, jnp.float32),
        in_specs=[pl.BlockSpec(memory_space=pltpu.VMEM)],
        out_specs=pl.BlockSpec(memory_space=pltpu.VMEM),
        scratch_shapes=[
            pltpu.VMEM((n,) + tile.shape, jnp.float32),
            pltpu.SemaphoreType.DMA((n,)),
            pltpu.SemaphoreType.DMA((n,)),
        ],
        compiler_params=pltpu.CompilerParams(collective_id=cid, has_side_effects=True),
    )(tile)
    return out.reshape(-1)[:size].reshape(shape)


def fused_kernel(n_rows, n_cols, z_ref, g_ref, zo_ref, go_ref, recv_z, recv_g, recv_s, rows_sum, sems):
    row = lax.axis_index("rows")
    col = lax.axis_index("cols")
    barrier = pltpu.get_barrier_semaphore()

    def greet(k, carry):
        pl.semaphore_signal(
            barrier, inc=1, device_id={"rows": lax.rem(row + k, n_rows)}, device_id_type=MESH
        )
        return carry

    lax.fori_loop(1, n_rows, greet, 0)
    for k in range(1, n_cols):
        pl.semaphore_signal(
            barrier, inc=1, device_id={"cols": lax.rem(col + k, n_cols)}, device_id_type=MESH
        )
    pl.semaphore_wait(barrier, n_rows - 1 + n_cols - 1)
    z_send, z_recv, g_send, g_recv, s_send, s_recv = sems

    def col_copy(src, dst, send, recv, peer, slot):
        return pltpu.make_async_remote_copy(
            src_ref=src,
            dst_ref=dst.at[slot],
            send_sem=send.at[peer],
            recv_sem=recv.at[slot],
            device_id={"cols": peer},
            device_id_type=MESH,
        )

    def g_copy(peer, slot):
        return pltpu.make_async_remote_copy(
            src_ref=g_ref,
            dst_ref=recv_g.at[slot],
            send_sem=g_send.at[peer],
            recv_sem=g_recv.at[slot],
            device_id={"rows": peer},
            device_id_type=MESH,
        )

    for k in range(1, n_cols):
        col_copy(z_ref, recv_z, z_send, z_recv, lax.rem(col + k, n_cols), col).start()

    def start(k, carry):
        g_copy(lax.rem(row + k, n_rows), row).start()
        return carry

    lax.fori_loop(1, n_rows, start, 0)
    recv_z[col] = z_ref[...]
    recv_g[row] = g_ref[...]

    def finish(k, carry):
        peer = lax.rem(row + k, n_rows)
        g_copy(peer, row).wait_send()
        g_copy(peer, peer).wait_recv()
        return carry

    lax.fori_loop(1, n_rows, finish, 0)
    rows_sum[...] = recv_g[0]

    def add(s, carry):
        rows_sum[...] += recv_g[s]
        return carry

    lax.fori_loop(1, n_rows, add, 0)
    for k in range(1, n_cols):
        col_copy(rows_sum, recv_s, s_send, s_recv, lax.rem(col + k, n_cols), col).start()
    recv_s[col] = rows_sum[...]
    for k in range(1, n_cols):
        peer = lax.rem(col + k, n_cols)
        col_copy(z_ref, recv_z, z_send, z_recv, peer, col).wait_send()
        col_copy(z_ref, recv_z, z_send, z_recv, peer, peer).wait_recv()
    zo_ref[...] = recv_z[0]
    for k in range(1, n_cols):
        zo_ref[...] += recv_z[k]
    for k in range(1, n_cols):
        peer = lax.rem(col + k, n_cols)
        col_copy(rows_sum, recv_s, s_send, s_recv, peer, col).wait_send()
        col_copy(rows_sum, recv_s, s_send, s_recv, peer, peer).wait_recv()
    go_ref[...] = recv_s[0]
    for k in range(1, n_cols):
        go_ref[...] += recv_s[k]


def fused_sum(z, g, cid):
    n_rows = lax.axis_size("rows")
    n_cols = lax.axis_size("cols")
    z_tile = z.reshape(-1, z.shape[-1])
    size = g.shape[0]
    g_tile = jnp.pad(g, (0, 128 - size)).reshape(1, 128)
    vmem = pl.BlockSpec(memory_space=pltpu.VMEM)
    z_out, g_out = pl.pallas_call(
        functools.partial(fused_kernel, n_rows, n_cols),
        out_shape=[
            jax.ShapeDtypeStruct(z_tile.shape, jnp.float32),
            jax.ShapeDtypeStruct(g_tile.shape, jnp.float32),
        ],
        in_specs=[vmem, vmem],
        out_specs=[vmem, vmem],
        scratch_shapes=[
            pltpu.VMEM((n_cols,) + z_tile.shape, jnp.float32),
            pltpu.VMEM((n_rows,) + g_tile.shape, jnp.float32),
            pltpu.VMEM((n_cols,) + g_tile.shape, jnp.float32),
            pltpu.VMEM(g_tile.shape, jnp.float32),
            [
                pltpu.SemaphoreType.DMA((n_cols,)),
                pltpu.SemaphoreType.DMA((n_cols,)),
                pltpu.SemaphoreType.DMA((n_rows,)),
                pltpu.SemaphoreType.DMA((n_rows,)),
                pltpu.SemaphoreType.DMA((n_cols,)),
                pltpu.SemaphoreType.DMA((n_cols,)),
            ],
        ],
        compiler_params=pltpu.CompilerParams(collective_id=cid, has_side_effects=True),
    )(z_tile, g_tile)
    return z_out.reshape(z.shape), g_out.reshape(-1)[:size]


def local(block_list, points, targets):
    row_count = lax.axis_size("rows")
    row_index = lax.axis_index("rows")
    block_rows, slot_width = block_list.shape
    coord_dim, npoints = points.shape
    outputs = targets.shape[0]
    block_len = npoints // block_rows
    slot_count = block_rows * slot_width
    entries = block_list.reshape(slot_count)
    is_live = entries >= 0
    owners = jnp.where(is_live, entries // block_rows, 0)
    local_idx = jnp.where(is_live, entries - owners * block_rows, 0)
    slot_row = jnp.arange(slot_count, dtype=jnp.int32) // slot_width
    first_row = row_index * block_rows
    place_at = jnp.where(is_live, owners, row_count)
    pick_at = jnp.minimum(place_at, row_count - 1)
    wanted = jnp.full((row_count,), -1, jnp.int32).at[place_at].set(local_idx, mode="drop")
    asking_row = jnp.full((row_count,), -1, jnp.int32).at[place_at].set(slot_row, mode="drop")
    ask_live = asking_row >= 0
    ask_row = jnp.maximum(asking_row, 0)
    own_x = points.reshape(coord_dim, block_rows, block_len).transpose(1, 0, 2)
    asked_x = jnp.where(ask_live[:, None, None], own_x[ask_row], jnp.zeros((), own_x.dtype))
    lane = lax.broadcasted_iota(jnp.int32, (row_count, coord_dim, 128), 2)
    sublane = lax.broadcasted_iota(jnp.int32, (row_count, coord_dim, 128), 1)
    request = jnp.where(lane == 0, wanted[:, None, None], asking_row[:, None, None])
    request = jnp.where((sublane == 0) & (lane < 2), request, 0).astype(own_x.dtype)
    first_swap = lax.all_to_all(
        jnp.concatenate([asked_x, request], axis=2), "rows", split_axis=0, concat_axis=0, tiled=True
    )
    their_x = first_swap[:, :, :block_len]
    incoming = first_swap[:, 0, block_len:block_len + 2].astype(jnp.int32)
    in_live = incoming[:, 0] >= 0
    in_idx = jnp.maximum(incoming[:, 0], 0)
    their_row = jnp.arange(row_count, dtype=jnp.int32) * block_rows + jnp.maximum(incoming[:, 1], 0)
    in_off = in_live & (their_row != first_row + in_idx)
    collect_map = (
        (in_idx[None, :] == jnp.arange(block_rows, dtype=jnp.int32)[:, None]) & in_off[None, :]
    ).astype(jnp.float32)

    def swap(parts):
        return lax.all_to_all(parts, "rows", split_axis=0, concat_axis=0, tiled=True)

    peer_ids = jnp.arange(row_count, dtype=jnp.int32)
    to_lower = (peer_ids <= row_index)[:, None, None]
    from_self = (peer_ids == row_index)[:, None, None]

    def both_ways(blocks):
        got = swap(jnp.where(to_lower, asked_part(blocks), served_part(blocks)))
        their = jnp.where(peer_ids[:, None, None] >= row_index, got, jnp.zeros((), got.dtype))
        served_self = blocks[in_idx[row_index]]
        far = jnp.where(from_self, served_self[None], got)
        return their, per_slot(far)

    def asked_part(blocks):
        return jnp.where(ask_live[:, None, None], blocks[ask_row], jnp.zeros((), blocks.dtype))

    def served_part(blocks):
        return jnp.where(in_live[:, None, None], blocks[in_idx], jnp.zeros((), blocks.dtype))

    def per_slot(got):
        chosen = got[pick_at]
        return jnp.where(is_live[:, None, None], chosen, jnp.zeros((), chosen.dtype))

    def collect(terms):
        flat = terms.reshape(row_count, -1)
        summed = jnp.dot(
            collect_map, flat, precision=lax.Precision.HIGHEST, preferred_element_type=jnp.float32
        )
        return summed.reshape((block_rows,) + terms.shape[1:])

    def column_total(partial_value):
        return allsum(partial_value, "cols", 1 if partial_value.shape[1] == 1 else 2)

    def global_sum(values):
        return allsum(values, "rows", 0)

    far_x = per_slot(swap(served_part(own_x)))

    def pair_pass(lx, rx, live):
        values = jnp.where(live[:, None, None], wendland(lx, rx), 0.0)
        return (values.astype(jnp.bfloat16), jnp.sum(values, axis=2), jnp.sum(values, axis=1))

    in_k, _, in_col_sums = pair_pass(their_x, own_x[in_idx], in_off)
    own_k, own_row_sums, _ = pair_pass(own_x[slot_row], far_x, is_live)
    degree_direct = jnp.sum(own_row_sums.reshape(block_rows, slot_width, block_len), axis=1)
    degree_mirror = collect(in_col_sums)
    degree_part = (degree_direct + degree_mirror)[:, None, :]
    inv_root = 1.0 / jnp.sqrt(1.0 + column_total(degree_part))

    def apply_partial(weights):
        their_w, far_w = both_ways(weights)
        direct = jnp.einsum(
            "rkab,rkob->roa",
            own_k.reshape(block_rows, slot_width, block_len, block_len),
            far_w.reshape(block_rows, slot_width, outputs, block_len),
            preferred_element_type=jnp.float32,
        )
        mirror = jnp.einsum("eab,eoa->eob", in_k, their_w, preferred_element_type=jnp.float32)
        return direct + collect(mirror)

    resid = targets.reshape(outputs, block_rows, block_len).transpose(1, 0, 2)
    direction = resid
    solution = jnp.zeros_like(resid)
    norm_now = jnp.sum(resid * resid, axis=(0, 2))
    first_col = lax.axis_index("cols") == 0
    for iteration in range(ITERS):
        weights = (direction * inv_root).astype(jnp.bfloat16)
        z_part = apply_partial(weights)
        own_term = jnp.where(first_col, REG * jnp.sum(direction * direction, axis=(0, 2)), 0.0)
        curv_part = own_term + jnp.sum(direction * (inv_root * z_part), axis=(0, 2))
        if iteration == 0:
            norm_part = jnp.where(first_col, norm_now, 0.0)
            z_total, both = fused_sum(z_part, jnp.concatenate([norm_part, curv_part]), 6)
            norm_now, curvature = both[:outputs], both[outputs:]
        else:
            z_total, curvature = fused_sum(z_part, curv_part, 7)
        applied = REG * direction + inv_root * z_total
        step_size = norm_now / curvature
        solution = solution + step_size[None, :, None] * direction
        resid = resid - step_size[None, :, None] * applied
        if iteration + 1 < ITERS:
            norm_next = global_sum(jnp.sum(resid * resid, axis=(0, 2)))
            direction = resid + (norm_next / norm_now)[None, :, None] * direction
            norm_now = norm_next
    return (
        solution.transpose(1, 0, 2).reshape(outputs, npoints),
        resid.transpose(1, 0, 2).reshape(outputs, npoints),
    )


def solution(mesh):
    placed = (P("rows", "cols"), P(None, "rows"), P(None, "rows"))
    return jax.shard_map(
        local,
        mesh=mesh,
        in_specs=placed,
        out_specs=(P(None, "rows"), P(None, "rows")),
        check_vma=False,
    )
```

```python
import functools

import jax
import jax.numpy as jnp
from jax import lax
from jax.experimental import pallas as pl
from jax.experimental.pallas import tpu as pltpu
from jax.sharding import PartitionSpec as P

MESH = pl.DeviceIdType.MESH

ITERS = 2


REG = 1.5
RADIUS = 0.25


def wendland(left_x, right_x):
    left_f = left_x.astype(jnp.float32)
    right_f = right_x.astype(jnp.float32)
    left_sq = jnp.sum(left_f * left_f, axis=1)
    right_sq = jnp.sum(right_f * right_f, axis=1)
    inner_prod = jnp.einsum("nda,ndb->nab", left_f, right_f, precision=lax.Precision.HIGHEST)
    dist_sq = left_sq[:, :, None] + right_sq[:, None, :] - 2.0 * inner_prod
    scaled = jnp.sqrt(jnp.maximum(dist_sq, 0.0)) / RADIUS
    remain = jnp.maximum(1.0 - scaled, 0.0)
    square = remain * remain
    return square * square * (4.0 * scaled + 1.0)


def allsum_kernel(axis, n, x_ref, o_ref, recv, send_sem, recv_sem):
    me = lax.axis_index(axis)
    barrier = pltpu.get_barrier_semaphore()

    def greet(k, carry):
        peer = lax.rem(me + k, n)
        pl.semaphore_signal(barrier, inc=1, device_id={axis: peer}, device_id_type=MESH)
        return carry

    lax.fori_loop(1, n, greet, 0)
    pl.semaphore_wait(barrier, n - 1)

    def outgoing(peer):
        return pltpu.make_async_remote_copy(
            src_ref=x_ref,
            dst_ref=recv.at[me],
            send_sem=send_sem.at[peer],
            recv_sem=recv_sem.at[me],
            device_id={axis: peer},
            device_id_type=MESH,
        )

    def incoming(peer):
        return pltpu.make_async_remote_copy(
            src_ref=x_ref,
            dst_ref=recv.at[peer],
            send_sem=send_sem.at[peer],
            recv_sem=recv_sem.at[peer],
            device_id={axis: peer},
            device_id_type=MESH,
        )

    def start(k, carry):
        outgoing(lax.rem(me + k, n)).start()
        return carry

    lax.fori_loop(1, n, start, 0)
    recv[me] = x_ref[...]

    def finish(k, carry):
        peer = lax.rem(me + k, n)
        outgoing(peer).wait_send()
        incoming(peer).wait_recv()
        return carry

    lax.fori_loop(1, n, finish, 0)
    o_ref[...] = recv[0]

    def add(s, carry):
        o_ref[...] += recv[s]
        return carry

    lax.fori_loop(1, n, add, 0)


def allsum(x, axis, cid):
    n = lax.axis_size(axis)
    shape = x.shape
    flat = x.reshape(-1)
    size = flat.shape[0]
    if size <= 128:
        tile = jnp.pad(flat, (0, 128 - size)).reshape(1, 128)
    elif size % 1024 == 0:
        tile = flat.reshape(size // 128, 128)
    else:
        rows_pad = -(-size // 1024) * 8
        tile = jnp.pad(flat, (0, rows_pad * 128 - size)).reshape(rows_pad, 128)
    out = pl.pallas_call(
        functools.partial(allsum_kernel, axis, n),
        out_shape=jax.ShapeDtypeStruct(tile.shape, jnp.float32),
        in_specs=[pl.BlockSpec(memory_space=pltpu.VMEM)],
        out_specs=pl.BlockSpec(memory_space=pltpu.VMEM),
        scratch_shapes=[
            pltpu.VMEM((n,) + tile.shape, jnp.float32),
            pltpu.SemaphoreType.DMA((n,)),
            pltpu.SemaphoreType.DMA((n,)),
        ],
        compiler_params=pltpu.CompilerParams(collective_id=cid, has_side_effects=True),
    )(tile)
    return out.reshape(-1)[:size].reshape(shape)


def fused_kernel(n_rows, n_cols, z_ref, g_ref, zo_ref, go_ref, recv_z, recv_g, recv_s, rows_sum, sems):
    row = lax.axis_index("rows")
    col = lax.axis_index("cols")
    barrier = pltpu.get_barrier_semaphore()

    def greet(k, carry):
        pl.semaphore_signal(
            barrier, inc=1, device_id={"rows": lax.rem(row + k, n_rows)}, device_id_type=MESH
        )
        return carry

    lax.fori_loop(1, n_rows, greet, 0)
    for k in range(1, n_cols):
        pl.semaphore_signal(
            barrier, inc=1, device_id={"cols": lax.rem(col + k, n_cols)}, device_id_type=MESH
        )
    pl.semaphore_wait(barrier, n_rows - 1 + n_cols - 1)
    z_send, z_recv, g_send, g_recv, s_send, s_recv = sems

    def col_copy(src, dst, send, recv, peer, slot):
        return pltpu.make_async_remote_copy(
            src_ref=src,
            dst_ref=dst.at[slot],
            send_sem=send.at[peer],
            recv_sem=recv.at[slot],
            device_id={"cols": peer},
            device_id_type=MESH,
        )

    def g_copy(peer, slot):
        return pltpu.make_async_remote_copy(
            src_ref=g_ref,
            dst_ref=recv_g.at[slot],
            send_sem=g_send.at[peer],
            recv_sem=g_recv.at[slot],
            device_id={"rows": peer},
            device_id_type=MESH,
        )

    for k in range(1, n_cols):
        col_copy(z_ref, recv_z, z_send, z_recv, lax.rem(col + k, n_cols), col).start()

    def start(k, carry):
        g_copy(lax.rem(row + k, n_rows), row).start()
        return carry

    lax.fori_loop(1, n_rows, start, 0)
    recv_z[col] = z_ref[...]
    recv_g[row] = g_ref[...]

    def finish(k, carry):
        peer = lax.rem(row + k, n_rows)
        g_copy(peer, row).wait_send()
        g_copy(peer, peer).wait_recv()
        return carry

    lax.fori_loop(1, n_rows, finish, 0)
    rows_sum[...] = recv_g[0]

    def add(s, carry):
        rows_sum[...] += recv_g[s]
        return carry

    lax.fori_loop(1, n_rows, add, 0)
    for k in range(1, n_cols):
        col_copy(rows_sum, recv_s, s_send, s_recv, lax.rem(col + k, n_cols), col).start()
    recv_s[col] = rows_sum[...]
    for k in range(1, n_cols):
        peer = lax.rem(col + k, n_cols)
        col_copy(z_ref, recv_z, z_send, z_recv, peer, col).wait_send()
        col_copy(z_ref, recv_z, z_send, z_recv, peer, peer).wait_recv()
    zo_ref[...] = recv_z[0]
    for k in range(1, n_cols):
        zo_ref[...] += recv_z[k]
    for k in range(1, n_cols):
        peer = lax.rem(col + k, n_cols)
        col_copy(rows_sum, recv_s, s_send, s_recv, peer, col).wait_send()
        col_copy(rows_sum, recv_s, s_send, s_recv, peer, peer).wait_recv()
    go_ref[...] = recv_s[0]
    for k in range(1, n_cols):
        go_ref[...] += recv_s[k]


def fused_sum(z, g, cid):
    n_rows = lax.axis_size("rows")
    n_cols = lax.axis_size("cols")
    z_tile = z.reshape(-1, z.shape[-1])
    size = g.shape[0]
    g_tile = jnp.pad(g, (0, 128 - size)).reshape(1, 128)
    vmem = pl.BlockSpec(memory_space=pltpu.VMEM)
    z_out, g_out = pl.pallas_call(
        functools.partial(fused_kernel, n_rows, n_cols),
        out_shape=[
            jax.ShapeDtypeStruct(z_tile.shape, jnp.float32),
            jax.ShapeDtypeStruct(g_tile.shape, jnp.float32),
        ],
        in_specs=[vmem, vmem],
        out_specs=[vmem, vmem],
        scratch_shapes=[
            pltpu.VMEM((n_cols,) + z_tile.shape, jnp.float32),
            pltpu.VMEM((n_rows,) + g_tile.shape, jnp.float32),
            pltpu.VMEM((n_cols,) + g_tile.shape, jnp.float32),
            pltpu.VMEM(g_tile.shape, jnp.float32),
            [
                pltpu.SemaphoreType.DMA((n_cols,)),
                pltpu.SemaphoreType.DMA((n_cols,)),
                pltpu.SemaphoreType.DMA((n_rows,)),
                pltpu.SemaphoreType.DMA((n_rows,)),
                pltpu.SemaphoreType.DMA((n_cols,)),
                pltpu.SemaphoreType.DMA((n_cols,)),
            ],
        ],
        compiler_params=pltpu.CompilerParams(collective_id=cid, has_side_effects=True),
    )(z_tile, g_tile)
    return z_out.reshape(z.shape), g_out.reshape(-1)[:size]


def local(block_list, points, targets):
    row_count = lax.axis_size("rows")
    row_index = lax.axis_index("rows")
    block_rows, slot_width = block_list.shape
    coord_dim, npoints = points.shape
    outputs = targets.shape[0]
    block_len = npoints // block_rows
    slot_count = block_rows * slot_width
    entries = block_list.reshape(slot_count)
    is_live = entries >= 0
    owners = jnp.where(is_live, entries // block_rows, 0)
    local_idx = jnp.where(is_live, entries - owners * block_rows, 0)
    slot_row = jnp.arange(slot_count, dtype=jnp.int32) // slot_width
    first_row = row_index * block_rows
    place_at = jnp.where(is_live, owners, row_count)
    pick_at = jnp.minimum(place_at, row_count - 1)
    wanted = jnp.full((row_count,), -1, jnp.int32).at[place_at].set(local_idx, mode="drop")
    asking_row = jnp.full((row_count,), -1, jnp.int32).at[place_at].set(slot_row, mode="drop")
    ask_live = asking_row >= 0
    ask_row = jnp.maximum(asking_row, 0)
    own_x = points.reshape(coord_dim, block_rows, block_len).transpose(1, 0, 2)
    asked_x = jnp.where(ask_live[:, None, None], own_x[ask_row], jnp.zeros((), own_x.dtype))
    lane = lax.broadcasted_iota(jnp.int32, (row_count, coord_dim, 128), 2)
    sublane = lax.broadcasted_iota(jnp.int32, (row_count, coord_dim, 128), 1)
    request = jnp.where(lane == 0, wanted[:, None, None], asking_row[:, None, None])
    request = jnp.where((sublane == 0) & (lane < 2), request, 0).astype(own_x.dtype)
    first_swap = lax.all_to_all(
        jnp.concatenate([asked_x, request], axis=2), "rows", split_axis=0, concat_axis=0, tiled=True
    )
    their_x = first_swap[:, :, :block_len]
    incoming = first_swap[:, 0, block_len:block_len + 2].astype(jnp.int32)
    in_live = incoming[:, 0] >= 0
    in_idx = jnp.maximum(incoming[:, 0], 0)
    their_row = jnp.arange(row_count, dtype=jnp.int32) * block_rows + jnp.maximum(incoming[:, 1], 0)
    in_off = in_live & (their_row != first_row + in_idx)
    collect_map = (
        (in_idx[None, :] == jnp.arange(block_rows, dtype=jnp.int32)[:, None]) & in_off[None, :]
    ).astype(jnp.float32)

    def swap(parts):
        return lax.all_to_all(parts, "rows", split_axis=0, concat_axis=0, tiled=True)

    peer_ids = jnp.arange(row_count, dtype=jnp.int32)
    to_lower = (peer_ids <= row_index)[:, None, None]
    from_self = (peer_ids == row_index)[:, None, None]

    def both_ways(blocks):
        got = swap(jnp.where(to_lower, asked_part(blocks), served_part(blocks)))
        their = jnp.where(peer_ids[:, None, None] >= row_index, got, jnp.zeros((), got.dtype))
        served_self = blocks[in_idx[row_index]]
        far = jnp.where(from_self, served_self[None], got)
        return their, per_slot(far)

    def asked_part(blocks):
        return jnp.where(ask_live[:, None, None], blocks[ask_row], jnp.zeros((), blocks.dtype))

    def served_part(blocks):
        return jnp.where(in_live[:, None, None], blocks[in_idx], jnp.zeros((), blocks.dtype))

    def per_slot(got):
        chosen = got[pick_at]
        return jnp.where(is_live[:, None, None], chosen, jnp.zeros((), chosen.dtype))

    def collect(terms):
        flat = terms.reshape(row_count, -1)
        summed = jnp.dot(
            collect_map, flat, precision=lax.Precision.HIGHEST, preferred_element_type=jnp.float32
        )
        return summed.reshape((block_rows,) + terms.shape[1:])

    def column_total(partial_value):
        return allsum(partial_value, "cols", 1 if partial_value.shape[1] == 1 else 2)

    def global_sum(values):
        return allsum(values, "rows", 0)

    far_x = per_slot(swap(served_part(own_x)))

    def pair_pass(lx, rx, live):
        values = jnp.where(live[:, None, None], wendland(lx, rx), 0.0)
        return (values.astype(jnp.bfloat16), jnp.sum(values, axis=2), jnp.sum(values, axis=1))

    in_k, _, in_col_sums = pair_pass(their_x, own_x[in_idx], in_off)
    own_k, own_row_sums, _ = pair_pass(own_x[slot_row], far_x, is_live)
    degree_direct = jnp.sum(own_row_sums.reshape(block_rows, slot_width, block_len), axis=1)
    degree_mirror = collect(in_col_sums)
    degree_part = (degree_direct + degree_mirror)[:, None, :]
    inv_root = 1.0 / jnp.sqrt(1.0 + column_total(degree_part))

    def apply_partial(weights):
        their_w, far_w = both_ways(weights)
        direct = jnp.einsum(
            "rkab,rkob->roa",
            own_k.reshape(block_rows, slot_width, block_len, block_len),
            far_w.reshape(block_rows, slot_width, outputs, block_len),
            preferred_element_type=jnp.float32,
        )
        picked = collect_map.astype(their_w.dtype)[:, None, :, None] * jnp.swapaxes(their_w, 0, 1)[None]
        mirror = jnp.einsum("joea,eab->job", picked, in_k, preferred_element_type=jnp.float32)
        return direct + mirror

    resid = targets.reshape(outputs, block_rows, block_len).transpose(1, 0, 2)
    direction = resid
    solution = jnp.zeros_like(resid)
    norm_now = jnp.sum(resid * resid, axis=(0, 2))
    first_col = lax.axis_index("cols") == 0
    for iteration in range(ITERS):
        weights = (direction * inv_root).astype(jnp.bfloat16)
        z_part = apply_partial(weights)
        own_term = jnp.where(first_col, REG * jnp.sum(direction * direction, axis=(0, 2)), 0.0)
        curv_part = own_term + jnp.sum(direction * (inv_root * z_part), axis=(0, 2))
        if iteration == 0:
            norm_part = jnp.where(first_col, norm_now, 0.0)
            z_total, both = fused_sum(z_part, jnp.concatenate([norm_part, curv_part]), 6)
            norm_now, curvature = both[:outputs], both[outputs:]
        else:
            z_total, curvature = fused_sum(z_part, curv_part, 7)
        applied = REG * direction + inv_root * z_total
        step_size = norm_now / curvature
        solution = solution + step_size[None, :, None] * direction
        resid = resid - step_size[None, :, None] * applied
        if iteration + 1 < ITERS:
            norm_next = global_sum(jnp.sum(resid * resid, axis=(0, 2)))
            direction = resid + (norm_next / norm_now)[None, :, None] * direction
            norm_now = norm_next
    return (
        solution.transpose(1, 0, 2).reshape(outputs, npoints),
        resid.transpose(1, 0, 2).reshape(outputs, npoints),
    )


def solution(mesh):
    placed = (P("rows", "cols"), P(None, "rows"), P(None, "rows"))
    return jax.shard_map(
        local,
        mesh=mesh,
        in_specs=placed,
        out_specs=(P(None, "rows"), P(None, "rows")),
        check_vma=False,
    )
```

```python
import functools

import jax
import jax.numpy as jnp
from jax import lax
from jax.experimental import pallas as pl
from jax.experimental.pallas import tpu as pltpu
from jax.sharding import PartitionSpec as P

MESH = pl.DeviceIdType.MESH

ITERS = 2


REG = 1.5
RADIUS = 0.25


def wendland(left_x, right_x):
    left_f = left_x.astype(jnp.float32)
    right_f = right_x.astype(jnp.float32)
    left_sq = jnp.sum(left_f * left_f, axis=1)
    right_sq = jnp.sum(right_f * right_f, axis=1)
    inner_prod = jnp.einsum("nda,ndb->nab", left_f, right_f, precision=lax.Precision.HIGHEST)
    dist_sq = left_sq[:, :, None] + right_sq[:, None, :] - 2.0 * inner_prod
    scaled = jnp.sqrt(jnp.maximum(dist_sq, 0.0)) / RADIUS
    remain = jnp.maximum(1.0 - scaled, 0.0)
    square = remain * remain
    return square * square * (4.0 * scaled + 1.0)


def allsum_kernel(axis, n, x_ref, o_ref, recv, send_sem, recv_sem):
    me = lax.axis_index(axis)
    barrier = pltpu.get_barrier_semaphore()

    def greet(k, carry):
        peer = lax.rem(me + k, n)
        pl.semaphore_signal(barrier, inc=1, device_id={axis: peer}, device_id_type=MESH)
        return carry

    lax.fori_loop(1, n, greet, 0)
    pl.semaphore_wait(barrier, n - 1)

    def outgoing(peer):
        return pltpu.make_async_remote_copy(
            src_ref=x_ref,
            dst_ref=recv.at[me],
            send_sem=send_sem.at[peer],
            recv_sem=recv_sem.at[me],
            device_id={axis: peer},
            device_id_type=MESH,
        )

    def incoming(peer):
        return pltpu.make_async_remote_copy(
            src_ref=x_ref,
            dst_ref=recv.at[peer],
            send_sem=send_sem.at[peer],
            recv_sem=recv_sem.at[peer],
            device_id={axis: peer},
            device_id_type=MESH,
        )

    def start(k, carry):
        outgoing(lax.rem(me + k, n)).start()
        return carry

    lax.fori_loop(1, n, start, 0)
    recv[me] = x_ref[...]

    def finish(k, carry):
        peer = lax.rem(me + k, n)
        outgoing(peer).wait_send()
        incoming(peer).wait_recv()
        return carry

    lax.fori_loop(1, n, finish, 0)
    o_ref[...] = recv[0]

    def add(s, carry):
        o_ref[...] += recv[s]
        return carry

    lax.fori_loop(1, n, add, 0)


def allsum(x, axis, cid):
    n = lax.axis_size(axis)
    shape = x.shape
    flat = x.reshape(-1)
    size = flat.shape[0]
    if size <= 128:
        tile = jnp.pad(flat, (0, 128 - size)).reshape(1, 128)
    elif size % 1024 == 0:
        tile = flat.reshape(size // 128, 128)
    else:
        rows_pad = -(-size // 1024) * 8
        tile = jnp.pad(flat, (0, rows_pad * 128 - size)).reshape(rows_pad, 128)
    out = pl.pallas_call(
        functools.partial(allsum_kernel, axis, n),
        out_shape=jax.ShapeDtypeStruct(tile.shape, jnp.float32),
        in_specs=[pl.BlockSpec(memory_space=pltpu.VMEM)],
        out_specs=pl.BlockSpec(memory_space=pltpu.VMEM),
        scratch_shapes=[
            pltpu.VMEM((n,) + tile.shape, jnp.float32),
            pltpu.SemaphoreType.DMA((n,)),
            pltpu.SemaphoreType.DMA((n,)),
        ],
        compiler_params=pltpu.CompilerParams(collective_id=cid, has_side_effects=True),
    )(tile)
    return out.reshape(-1)[:size].reshape(shape)


def fused_kernel(
    n_rows, n_cols, z_ref, g_ref, zo_ref, go_ref, recv_z, gathered, recv_g, recv_s, rows_sum, sems
):
    row = lax.axis_index("rows")
    col = lax.axis_index("cols")
    barrier = pltpu.get_barrier_semaphore()

    def greet(k, carry):
        pl.semaphore_signal(
            barrier, inc=1, device_id={"rows": lax.rem(row + k, n_rows)}, device_id_type=MESH
        )
        return carry

    lax.fori_loop(1, n_rows, greet, 0)
    for k in range(1, n_cols):
        pl.semaphore_signal(
            barrier, inc=1, device_id={"cols": lax.rem(col + k, n_cols)}, device_id_type=MESH
        )
    pl.semaphore_wait(barrier, n_rows - 1 + n_cols - 1)
    z_send, z_recv, g_send, g_recv, s_send, s_recv, a_send, a_recv = sems

    def col_copy(src, dst, send, recv, peer, slot):
        return pltpu.make_async_remote_copy(
            src_ref=src,
            dst_ref=dst.at[slot],
            send_sem=send.at[peer],
            recv_sem=recv.at[slot],
            device_id={"cols": peer},
            device_id_type=MESH,
        )

    def g_copy(peer, slot):
        return pltpu.make_async_remote_copy(
            src_ref=g_ref,
            dst_ref=recv_g.at[slot],
            send_sem=g_send.at[peer],
            recv_sem=g_recv.at[slot],
            device_id={"rows": peer},
            device_id_type=MESH,
        )

    for k in range(1, n_cols):
        peer = lax.rem(col + k, n_cols)
        col_copy(z_ref.at[peer], recv_z, z_send, z_recv, peer, col).start()

    def start(k, carry):
        g_copy(lax.rem(row + k, n_rows), row).start()
        return carry

    lax.fori_loop(1, n_rows, start, 0)
    recv_z[col] = z_ref[col]
    recv_g[row] = g_ref[...]
    for k in range(1, n_cols):
        peer = lax.rem(col + k, n_cols)
        col_copy(z_ref.at[peer], recv_z, z_send, z_recv, peer, col).wait_send()
        col_copy(z_ref.at[peer], recv_z, z_send, z_recv, peer, peer).wait_recv()
    gathered[col] = recv_z[0]
    for k in range(1, n_cols):
        gathered[col] += recv_z[k]
    for k in range(1, n_cols):
        col_copy(gathered.at[col], gathered, a_send, a_recv, lax.rem(col + k, n_cols), col).start()

    def finish(k, carry):
        peer = lax.rem(row + k, n_rows)
        g_copy(peer, row).wait_send()
        g_copy(peer, peer).wait_recv()
        return carry

    lax.fori_loop(1, n_rows, finish, 0)
    rows_sum[...] = recv_g[0]

    def add(s, carry):
        rows_sum[...] += recv_g[s]
        return carry

    lax.fori_loop(1, n_rows, add, 0)
    for k in range(1, n_cols):
        col_copy(rows_sum, recv_s, s_send, s_recv, lax.rem(col + k, n_cols), col).start()
    recv_s[col] = rows_sum[...]
    for k in range(1, n_cols):
        peer = lax.rem(col + k, n_cols)
        col_copy(gathered.at[col], gathered, a_send, a_recv, peer, col).wait_send()
        col_copy(gathered.at[peer], gathered, a_send, a_recv, peer, peer).wait_recv()
    zo_ref[...] = gathered[...]
    for k in range(1, n_cols):
        peer = lax.rem(col + k, n_cols)
        col_copy(rows_sum, recv_s, s_send, s_recv, peer, col).wait_send()
        col_copy(rows_sum, recv_s, s_send, s_recv, peer, peer).wait_recv()
    go_ref[...] = recv_s[0]
    for k in range(1, n_cols):
        go_ref[...] += recv_s[k]


def fused_sum(z, g, cid):
    n_rows = lax.axis_size("rows")
    n_cols = lax.axis_size("cols")
    z_tile = z.reshape(n_cols, -1, z.shape[-1])
    size = g.shape[0]
    g_tile = jnp.pad(g, (0, 128 - size)).reshape(1, 128)
    vmem = pl.BlockSpec(memory_space=pltpu.VMEM)
    z_out, g_out = pl.pallas_call(
        functools.partial(fused_kernel, n_rows, n_cols),
        out_shape=[
            jax.ShapeDtypeStruct(z_tile.shape, jnp.float32),
            jax.ShapeDtypeStruct(g_tile.shape, jnp.float32),
        ],
        in_specs=[vmem, vmem],
        out_specs=[vmem, vmem],
        scratch_shapes=[
            pltpu.VMEM(z_tile.shape, jnp.float32),
            pltpu.VMEM(z_tile.shape, jnp.float32),
            pltpu.VMEM((n_rows,) + g_tile.shape, jnp.float32),
            pltpu.VMEM((n_cols,) + g_tile.shape, jnp.float32),
            pltpu.VMEM(g_tile.shape, jnp.float32),
            [
                pltpu.SemaphoreType.DMA((n_cols,)),
                pltpu.SemaphoreType.DMA((n_cols,)),
                pltpu.SemaphoreType.DMA((n_rows,)),
                pltpu.SemaphoreType.DMA((n_rows,)),
                pltpu.SemaphoreType.DMA((n_cols,)),
                pltpu.SemaphoreType.DMA((n_cols,)),
                pltpu.SemaphoreType.DMA((n_cols,)),
                pltpu.SemaphoreType.DMA((n_cols,)),
            ],
        ],
        compiler_params=pltpu.CompilerParams(collective_id=cid, has_side_effects=True),
    )(z_tile, g_tile)
    return z_out.reshape(z.shape), g_out.reshape(-1)[:size]


def local(block_list, points, targets):
    row_count = lax.axis_size("rows")
    row_index = lax.axis_index("rows")
    block_rows, slot_width = block_list.shape
    coord_dim, npoints = points.shape
    outputs = targets.shape[0]
    block_len = npoints // block_rows
    slot_count = block_rows * slot_width
    entries = block_list.reshape(slot_count)
    is_live = entries >= 0
    owners = jnp.where(is_live, entries // block_rows, 0)
    local_idx = jnp.where(is_live, entries - owners * block_rows, 0)
    slot_row = jnp.arange(slot_count, dtype=jnp.int32) // slot_width
    first_row = row_index * block_rows
    place_at = jnp.where(is_live, owners, row_count)
    pick_at = jnp.minimum(place_at, row_count - 1)
    wanted = jnp.full((row_count,), -1, jnp.int32).at[place_at].set(local_idx, mode="drop")
    asking_row = jnp.full((row_count,), -1, jnp.int32).at[place_at].set(slot_row, mode="drop")
    ask_live = asking_row >= 0
    ask_row = jnp.maximum(asking_row, 0)
    own_x = points.reshape(coord_dim, block_rows, block_len).transpose(1, 0, 2)
    asked_x = jnp.where(ask_live[:, None, None], own_x[ask_row], jnp.zeros((), own_x.dtype))
    lane = lax.broadcasted_iota(jnp.int32, (row_count, coord_dim, 128), 2)
    sublane = lax.broadcasted_iota(jnp.int32, (row_count, coord_dim, 128), 1)
    request = jnp.where(lane == 0, wanted[:, None, None], asking_row[:, None, None])
    request = jnp.where((sublane == 0) & (lane < 2), request, 0).astype(own_x.dtype)
    first_swap = lax.all_to_all(
        jnp.concatenate([asked_x, request], axis=2), "rows", split_axis=0, concat_axis=0, tiled=True
    )
    their_x = first_swap[:, :, :block_len]
    incoming = first_swap[:, 0, block_len:block_len + 2].astype(jnp.int32)
    in_live = incoming[:, 0] >= 0
    in_idx = jnp.maximum(incoming[:, 0], 0)
    their_row = jnp.arange(row_count, dtype=jnp.int32) * block_rows + jnp.maximum(incoming[:, 1], 0)
    in_off = in_live & (their_row != first_row + in_idx)
    collect_map = (
        (in_idx[None, :] == jnp.arange(block_rows, dtype=jnp.int32)[:, None]) & in_off[None, :]
    ).astype(jnp.float32)

    def swap(parts):
        return lax.all_to_all(parts, "rows", split_axis=0, concat_axis=0, tiled=True)

    peer_ids = jnp.arange(row_count, dtype=jnp.int32)
    to_lower = (peer_ids <= row_index)[:, None, None]
    from_self = (peer_ids == row_index)[:, None, None]

    def both_ways(blocks):
        got = swap(jnp.where(to_lower, asked_part(blocks), served_part(blocks)))
        their = jnp.where(peer_ids[:, None, None] >= row_index, got, jnp.zeros((), got.dtype))
        served_self = blocks[in_idx[row_index]]
        far = jnp.where(from_self, served_self[None], got)
        return their, per_slot(far)

    def asked_part(blocks):
        return jnp.where(ask_live[:, None, None], blocks[ask_row], jnp.zeros((), blocks.dtype))

    def served_part(blocks):
        return jnp.where(in_live[:, None, None], blocks[in_idx], jnp.zeros((), blocks.dtype))

    def per_slot(got):
        chosen = got[pick_at]
        return jnp.where(is_live[:, None, None], chosen, jnp.zeros((), chosen.dtype))

    def collect(terms):
        flat = terms.reshape(row_count, -1)
        summed = jnp.dot(
            collect_map, flat, precision=lax.Precision.HIGHEST, preferred_element_type=jnp.float32
        )
        return summed.reshape((block_rows,) + terms.shape[1:])

    def column_total(partial_value):
        return allsum(partial_value, "cols", 1 if partial_value.shape[1] == 1 else 2)

    def global_sum(values):
        return allsum(values, "rows", 0)

    far_x = per_slot(swap(served_part(own_x)))

    def pair_pass(lx, rx, live):
        values = jnp.where(live[:, None, None], wendland(lx, rx), 0.0)
        return (values.astype(jnp.bfloat16), jnp.sum(values, axis=2), jnp.sum(values, axis=1))

    in_k, _, in_col_sums = pair_pass(their_x, own_x[in_idx], in_off)
    own_k, own_row_sums, _ = pair_pass(own_x[slot_row], far_x, is_live)
    degree_direct = jnp.sum(own_row_sums.reshape(block_rows, slot_width, block_len), axis=1)
    degree_mirror = collect(in_col_sums)
    degree_part = (degree_direct + degree_mirror)[:, None, :]
    inv_root = 1.0 / jnp.sqrt(1.0 + column_total(degree_part))

    def apply_partial(weights):
        their_w, far_w = both_ways(weights)
        direct = jnp.einsum(
            "rkab,rkob->roa",
            own_k.reshape(block_rows, slot_width, block_len, block_len),
            far_w.reshape(block_rows, slot_width, outputs, block_len),
            preferred_element_type=jnp.float32,
        )
        picked = collect_map.astype(their_w.dtype)[:, None, :, None] * jnp.swapaxes(their_w, 0, 1)[None]
        mirror = jnp.einsum("joea,eab->job", picked, in_k, preferred_element_type=jnp.float32)
        return direct + mirror

    resid = targets.reshape(outputs, block_rows, block_len).transpose(1, 0, 2)
    direction = resid
    solution = jnp.zeros_like(resid)
    norm_now = jnp.sum(resid * resid, axis=(0, 2))
    first_col = lax.axis_index("cols") == 0
    for iteration in range(ITERS):
        weights = (direction * inv_root).astype(jnp.bfloat16)
        z_part = apply_partial(weights)
        own_term = jnp.where(first_col, REG * jnp.sum(direction * direction, axis=(0, 2)), 0.0)
        curv_part = own_term + jnp.sum(direction * (inv_root * z_part), axis=(0, 2))
        if iteration == 0:
            norm_part = jnp.where(first_col, norm_now, 0.0)
            z_total, both = fused_sum(z_part, jnp.concatenate([norm_part, curv_part]), 6)
            norm_now, curvature = both[:outputs], both[outputs:]
        else:
            z_total, curvature = fused_sum(z_part, curv_part, 7)
        applied = REG * direction + inv_root * z_total
        step_size = norm_now / curvature
        solution = solution + step_size[None, :, None] * direction
        resid = resid - step_size[None, :, None] * applied
        if iteration + 1 < ITERS:
            norm_next = global_sum(jnp.sum(resid * resid, axis=(0, 2)))
            direction = resid + (norm_next / norm_now)[None, :, None] * direction
            norm_now = norm_next
    return (
        solution.transpose(1, 0, 2).reshape(outputs, npoints),
        resid.transpose(1, 0, 2).reshape(outputs, npoints),
    )


def solution(mesh):
    placed = (P("rows", "cols"), P(None, "rows"), P(None, "rows"))
    return jax.shard_map(
        local,
        mesh=mesh,
        in_specs=placed,
        out_specs=(P(None, "rows"), P(None, "rows")),
        check_vma=False,
    )
```

```python
import functools

import jax
import jax.numpy as jnp
from jax import lax
from jax.experimental import pallas as pl
from jax.experimental.pallas import tpu as pltpu
from jax.sharding import PartitionSpec as P

MESH = pl.DeviceIdType.MESH

ITERS = 2


REG = 1.5
RADIUS = 0.25


def wendland(left_x, right_x):
    left_f = left_x.astype(jnp.float32)
    right_f = right_x.astype(jnp.float32)
    left_sq = jnp.sum(left_f * left_f, axis=1)
    right_sq = jnp.sum(right_f * right_f, axis=1)
    inner_prod = jnp.einsum("nda,ndb->nab", left_f, right_f, precision=lax.Precision.HIGHEST)
    dist_sq = left_sq[:, :, None] + right_sq[:, None, :] - 2.0 * inner_prod
    scaled = jnp.sqrt(jnp.maximum(dist_sq, 0.0)) / RADIUS
    remain = jnp.maximum(1.0 - scaled, 0.0)
    square = remain * remain
    return square * square * (4.0 * scaled + 1.0)


def allsum_kernel(axis, n, x_ref, o_ref, recv, send_sem, recv_sem):
    me = lax.axis_index(axis)
    barrier = pltpu.get_barrier_semaphore()

    def greet(k, carry):
        peer = lax.rem(me + k, n)
        pl.semaphore_signal(barrier, inc=1, device_id={axis: peer}, device_id_type=MESH)
        return carry

    lax.fori_loop(1, n, greet, 0)
    pl.semaphore_wait(barrier, n - 1)

    def outgoing(peer):
        return pltpu.make_async_remote_copy(
            src_ref=x_ref,
            dst_ref=recv.at[me],
            send_sem=send_sem.at[peer],
            recv_sem=recv_sem.at[me],
            device_id={axis: peer},
            device_id_type=MESH,
        )

    def incoming(peer):
        return pltpu.make_async_remote_copy(
            src_ref=x_ref,
            dst_ref=recv.at[peer],
            send_sem=send_sem.at[peer],
            recv_sem=recv_sem.at[peer],
            device_id={axis: peer},
            device_id_type=MESH,
        )

    def start(k, carry):
        outgoing(lax.rem(me + k, n)).start()
        return carry

    lax.fori_loop(1, n, start, 0)
    recv[me] = x_ref[...]

    def finish(k, carry):
        peer = lax.rem(me + k, n)
        outgoing(peer).wait_send()
        incoming(peer).wait_recv()
        return carry

    lax.fori_loop(1, n, finish, 0)
    o_ref[...] = recv[0]

    def add(s, carry):
        o_ref[...] += recv[s]
        return carry

    lax.fori_loop(1, n, add, 0)


def allsum(x, axis, cid):
    n = lax.axis_size(axis)
    shape = x.shape
    flat = x.reshape(-1)
    size = flat.shape[0]
    if size <= 128:
        tile = jnp.pad(flat, (0, 128 - size)).reshape(1, 128)
    elif size % 1024 == 0:
        tile = flat.reshape(size // 128, 128)
    else:
        rows_pad = -(-size // 1024) * 8
        tile = jnp.pad(flat, (0, rows_pad * 128 - size)).reshape(rows_pad, 128)
    out = pl.pallas_call(
        functools.partial(allsum_kernel, axis, n),
        out_shape=jax.ShapeDtypeStruct(tile.shape, jnp.float32),
        in_specs=[pl.BlockSpec(memory_space=pltpu.VMEM)],
        out_specs=pl.BlockSpec(memory_space=pltpu.VMEM),
        scratch_shapes=[
            pltpu.VMEM((n,) + tile.shape, jnp.float32),
            pltpu.SemaphoreType.DMA((n,)),
            pltpu.SemaphoreType.DMA((n,)),
        ],
        compiler_params=pltpu.CompilerParams(collective_id=cid, has_side_effects=True),
    )(tile)
    return out.reshape(-1)[:size].reshape(shape)


def fused_kernel(
    n_rows, n_cols, z_ref, g_ref, zo_ref, go_ref, recv_z, gathered, recv_g, recv_s, rows_sum, sems
):
    row = lax.axis_index("rows")
    col = lax.axis_index("cols")
    barrier = pltpu.get_barrier_semaphore()

    def greet(k, carry):
        pl.semaphore_signal(
            barrier, inc=1, device_id={"rows": lax.rem(row + k, n_rows)}, device_id_type=MESH
        )
        return carry

    lax.fori_loop(1, n_rows, greet, 0)
    for k in range(1, n_cols):
        pl.semaphore_signal(
            barrier, inc=1, device_id={"cols": lax.rem(col + k, n_cols)}, device_id_type=MESH
        )
    pl.semaphore_wait(barrier, n_rows - 1 + n_cols - 1)
    z_send, z_recv, g_send, g_recv, s_send, s_recv, a_send, a_recv = sems

    def col_copy(src, dst, send, recv, peer, slot):
        return pltpu.make_async_remote_copy(
            src_ref=src,
            dst_ref=dst.at[slot],
            send_sem=send.at[peer],
            recv_sem=recv.at[slot],
            device_id={"cols": peer},
            device_id_type=MESH,
        )

    def g_copy(peer, slot):
        return pltpu.make_async_remote_copy(
            src_ref=g_ref,
            dst_ref=recv_g.at[slot],
            send_sem=g_send.at[peer],
            recv_sem=g_recv.at[slot],
            device_id={"rows": peer},
            device_id_type=MESH,
        )

    for k in range(1, n_cols):
        peer = lax.rem(col + k, n_cols)
        col_copy(z_ref.at[peer], recv_z, z_send, z_recv, peer, col).start()

    def start(k, carry):
        g_copy(lax.rem(row + k, n_rows), row).start()
        return carry

    lax.fori_loop(1, n_rows, start, 0)
    recv_z[col] = z_ref[col]
    recv_g[row] = g_ref[...]
    for k in range(1, n_cols):
        peer = lax.rem(col + k, n_cols)
        col_copy(z_ref.at[peer], recv_z, z_send, z_recv, peer, col).wait_send()
        col_copy(z_ref.at[peer], recv_z, z_send, z_recv, peer, peer).wait_recv()
    gathered[col] = recv_z[0]
    for k in range(1, n_cols):
        gathered[col] += recv_z[k]
    for k in range(1, n_cols):
        col_copy(gathered.at[col], gathered, a_send, a_recv, lax.rem(col + k, n_cols), col).start()

    def finish(k, carry):
        peer = lax.rem(row + k, n_rows)
        g_copy(peer, row).wait_send()
        g_copy(peer, peer).wait_recv()
        return carry

    lax.fori_loop(1, n_rows, finish, 0)
    rows_sum[...] = recv_g[0]

    def add(s, carry):
        rows_sum[...] += recv_g[s]
        return carry

    lax.fori_loop(1, n_rows, add, 0)
    for k in range(1, n_cols):
        col_copy(rows_sum, recv_s, s_send, s_recv, lax.rem(col + k, n_cols), col).start()
    recv_s[col] = rows_sum[...]
    for k in range(1, n_cols):
        peer = lax.rem(col + k, n_cols)
        col_copy(gathered.at[col], gathered, a_send, a_recv, peer, col).wait_send()
        col_copy(gathered.at[peer], gathered, a_send, a_recv, peer, peer).wait_recv()
    zo_ref[...] = gathered[...]
    for k in range(1, n_cols):
        peer = lax.rem(col + k, n_cols)
        col_copy(rows_sum, recv_s, s_send, s_recv, peer, col).wait_send()
        col_copy(rows_sum, recv_s, s_send, s_recv, peer, peer).wait_recv()
    go_ref[...] = recv_s[0]
    for k in range(1, n_cols):
        go_ref[...] += recv_s[k]


def fused_sum(z, g, cid):
    n_rows = lax.axis_size("rows")
    n_cols = lax.axis_size("cols")
    z_tile = z.reshape(n_cols, -1, z.shape[-1])
    size = g.shape[0]
    g_tile = jnp.pad(g, (0, 128 - size)).reshape(1, 128)
    vmem = pl.BlockSpec(memory_space=pltpu.VMEM)
    z_out, g_out = pl.pallas_call(
        functools.partial(fused_kernel, n_rows, n_cols),
        out_shape=[
            jax.ShapeDtypeStruct(z_tile.shape, jnp.float32),
            jax.ShapeDtypeStruct(g_tile.shape, jnp.float32),
        ],
        in_specs=[vmem, vmem],
        out_specs=[vmem, vmem],
        scratch_shapes=[
            pltpu.VMEM(z_tile.shape, jnp.float32),
            pltpu.VMEM(z_tile.shape, jnp.float32),
            pltpu.VMEM((n_rows,) + g_tile.shape, jnp.float32),
            pltpu.VMEM((n_cols,) + g_tile.shape, jnp.float32),
            pltpu.VMEM(g_tile.shape, jnp.float32),
            [
                pltpu.SemaphoreType.DMA((n_cols,)),
                pltpu.SemaphoreType.DMA((n_cols,)),
                pltpu.SemaphoreType.DMA((n_rows,)),
                pltpu.SemaphoreType.DMA((n_rows,)),
                pltpu.SemaphoreType.DMA((n_cols,)),
                pltpu.SemaphoreType.DMA((n_cols,)),
                pltpu.SemaphoreType.DMA((n_cols,)),
                pltpu.SemaphoreType.DMA((n_cols,)),
            ],
        ],
        compiler_params=pltpu.CompilerParams(collective_id=cid, has_side_effects=True),
    )(z_tile, g_tile)
    return z_out.reshape(z.shape), g_out.reshape(-1)[:size]


def rows_sum_kernel(n, group, x_ref, o_ref, recv1, recv2, sems):
    me = lax.axis_index("rows")
    pos = lax.rem(me, group)
    base = me - pos
    grp = me // group
    groups = n // group
    barrier = pltpu.get_barrier_semaphore()

    def near(k):
        return base + lax.rem(pos + k, group)

    def far(k):
        return lax.rem(grp + k, groups) * group + pos

    for k in range(1, group):
        pl.semaphore_signal(barrier, inc=1, device_id={"rows": near(k)}, device_id_type=MESH)
    for k in range(1, groups):
        pl.semaphore_signal(barrier, inc=1, device_id={"rows": far(k)}, device_id_type=MESH)
    pl.semaphore_wait(barrier, group - 1 + groups - 1)
    send1, got1, send2, got2 = sems

    def copy(src, dst, send, got, device, slot, peer_slot):
        return pltpu.make_async_remote_copy(
            src_ref=src,
            dst_ref=dst.at[slot],
            send_sem=send.at[peer_slot],
            recv_sem=got.at[slot],
            device_id={"rows": device},
            device_id_type=MESH,
        )

    for k in range(1, group):
        copy(x_ref, recv1, send1, got1, near(k), pos, lax.rem(pos + k, group)).start()
    recv1[pos] = x_ref[...]
    for k in range(1, group):
        other = lax.rem(pos + k, group)
        copy(x_ref, recv1, send1, got1, near(k), pos, other).wait_send()
        copy(x_ref, recv1, send1, got1, near(k), other, other).wait_recv()
    recv2[grp] = recv1[0]
    for k in range(1, group):
        recv2[grp] += recv1[k]
    for k in range(1, groups):
        copy(recv2.at[grp], recv2, send2, got2, far(k), grp, lax.rem(grp + k, groups)).start()
    for k in range(1, groups):
        other = lax.rem(grp + k, groups)
        copy(recv2.at[grp], recv2, send2, got2, far(k), grp, other).wait_send()
        copy(recv2.at[grp], recv2, send2, got2, far(k), other, other).wait_recv()
    o_ref[...] = recv2[0]
    for k in range(1, groups):
        o_ref[...] += recv2[k]


def rows_sum(x, cid):
    n = lax.axis_size("rows")
    group = 16 if n % 16 == 0 and n > 16 else (4 if n % 4 == 0 else n)
    groups = n // group
    size = x.shape[0]
    tile = jnp.pad(x, (0, 128 - size)).reshape(1, 128)
    out = pl.pallas_call(
        functools.partial(rows_sum_kernel, n, group),
        out_shape=jax.ShapeDtypeStruct(tile.shape, jnp.float32),
        in_specs=[pl.BlockSpec(memory_space=pltpu.VMEM)],
        out_specs=pl.BlockSpec(memory_space=pltpu.VMEM),
        scratch_shapes=[
            pltpu.VMEM((group,) + tile.shape, jnp.float32),
            pltpu.VMEM((groups,) + tile.shape, jnp.float32),
            [
                pltpu.SemaphoreType.DMA((group,)),
                pltpu.SemaphoreType.DMA((group,)),
                pltpu.SemaphoreType.DMA((groups,)),
                pltpu.SemaphoreType.DMA((groups,)),
            ],
        ],
        compiler_params=pltpu.CompilerParams(collective_id=cid, has_side_effects=True),
    )(tile)
    return out.reshape(-1)[:size]


def local(block_list, points, targets):
    row_count = lax.axis_size("rows")
    row_index = lax.axis_index("rows")
    block_rows, slot_width = block_list.shape
    coord_dim, npoints = points.shape
    outputs = targets.shape[0]
    block_len = npoints // block_rows
    slot_count = block_rows * slot_width
    entries = block_list.reshape(slot_count)
    is_live = entries >= 0
    owners = jnp.where(is_live, entries // block_rows, 0)
    local_idx = jnp.where(is_live, entries - owners * block_rows, 0)
    slot_row = jnp.arange(slot_count, dtype=jnp.int32) // slot_width
    first_row = row_index * block_rows
    place_at = jnp.where(is_live, owners, row_count)
    pick_at = jnp.minimum(place_at, row_count - 1)
    wanted = jnp.full((row_count,), -1, jnp.int32).at[place_at].set(local_idx, mode="drop")
    asking_row = jnp.full((row_count,), -1, jnp.int32).at[place_at].set(slot_row, mode="drop")
    ask_live = asking_row >= 0
    ask_row = jnp.maximum(asking_row, 0)
    own_x = points.reshape(coord_dim, block_rows, block_len).transpose(1, 0, 2)
    asked_x = jnp.where(ask_live[:, None, None], own_x[ask_row], jnp.zeros((), own_x.dtype))
    lane = lax.broadcasted_iota(jnp.int32, (row_count, coord_dim, 128), 2)
    sublane = lax.broadcasted_iota(jnp.int32, (row_count, coord_dim, 128), 1)
    request = jnp.where(lane == 0, wanted[:, None, None], asking_row[:, None, None])
    request = jnp.where((sublane == 0) & (lane < 2), request, 0).astype(own_x.dtype)
    first_swap = lax.all_to_all(
        jnp.concatenate([asked_x, request], axis=2), "rows", split_axis=0, concat_axis=0, tiled=True
    )
    their_x = first_swap[:, :, :block_len]
    incoming = first_swap[:, 0, block_len:block_len + 2].astype(jnp.int32)
    in_live = incoming[:, 0] >= 0
    in_idx = jnp.maximum(incoming[:, 0], 0)
    their_row = jnp.arange(row_count, dtype=jnp.int32) * block_rows + jnp.maximum(incoming[:, 1], 0)
    in_off = in_live & (their_row != first_row + in_idx)
    collect_map = (
        (in_idx[None, :] == jnp.arange(block_rows, dtype=jnp.int32)[:, None]) & in_off[None, :]
    ).astype(jnp.float32)

    def swap(parts):
        return lax.all_to_all(parts, "rows", split_axis=0, concat_axis=0, tiled=True)

    peer_ids = jnp.arange(row_count, dtype=jnp.int32)
    to_lower = (peer_ids <= row_index)[:, None, None]
    from_self = (peer_ids == row_index)[:, None, None]

    def both_ways(blocks):
        got = swap(jnp.where(to_lower, asked_part(blocks), served_part(blocks)))
        their = jnp.where(peer_ids[:, None, None] >= row_index, got, jnp.zeros((), got.dtype))
        served_self = blocks[in_idx[row_index]]
        far = jnp.where(from_self, served_self[None], got)
        return their, per_slot(far)

    def asked_part(blocks):
        return jnp.where(ask_live[:, None, None], blocks[ask_row], jnp.zeros((), blocks.dtype))

    def served_part(blocks):
        return jnp.where(in_live[:, None, None], blocks[in_idx], jnp.zeros((), blocks.dtype))

    def per_slot(got):
        chosen = got[pick_at]
        return jnp.where(is_live[:, None, None], chosen, jnp.zeros((), chosen.dtype))

    def collect(terms):
        flat = terms.reshape(row_count, -1)
        summed = jnp.dot(
            collect_map, flat, precision=lax.Precision.HIGHEST, preferred_element_type=jnp.float32
        )
        return summed.reshape((block_rows,) + terms.shape[1:])

    def column_total(partial_value):
        return allsum(partial_value, "cols", 1 if partial_value.shape[1] == 1 else 2)

    def global_sum(values):
        return rows_sum(values, 8)

    far_x = per_slot(swap(served_part(own_x)))

    def pair_pass(lx, rx, live):
        values = jnp.where(live[:, None, None], wendland(lx, rx), 0.0)
        return (values.astype(jnp.bfloat16), jnp.sum(values, axis=2), jnp.sum(values, axis=1))

    in_k, _, in_col_sums = pair_pass(their_x, own_x[in_idx], in_off)
    own_k, own_row_sums, _ = pair_pass(own_x[slot_row], far_x, is_live)
    degree_direct = jnp.sum(own_row_sums.reshape(block_rows, slot_width, block_len), axis=1)
    degree_mirror = collect(in_col_sums)
    degree_part = (degree_direct + degree_mirror)[:, None, :]
    inv_root = 1.0 / jnp.sqrt(1.0 + column_total(degree_part))

    def apply_partial(weights):
        their_w, far_w = both_ways(weights)
        direct = jnp.einsum(
            "rkab,rkob->roa",
            own_k.reshape(block_rows, slot_width, block_len, block_len),
            far_w.reshape(block_rows, slot_width, outputs, block_len),
            preferred_element_type=jnp.float32,
        )
        picked = collect_map.astype(their_w.dtype)[:, None, :, None] * jnp.swapaxes(their_w, 0, 1)[None]
        mirror = jnp.einsum("joea,eab->job", picked, in_k, preferred_element_type=jnp.float32)
        return direct + mirror

    resid = targets.reshape(outputs, block_rows, block_len).transpose(1, 0, 2)
    direction = resid
    solution = jnp.zeros_like(resid)
    norm_now = jnp.sum(resid * resid, axis=(0, 2))
    first_col = lax.axis_index("cols") == 0
    for iteration in range(ITERS):
        weights = (direction * inv_root).astype(jnp.bfloat16)
        z_part = apply_partial(weights)
        own_term = jnp.where(first_col, REG * jnp.sum(direction * direction, axis=(0, 2)), 0.0)
        curv_part = own_term + jnp.sum(direction * (inv_root * z_part), axis=(0, 2))
        if iteration == 0:
            norm_part = jnp.where(first_col, norm_now, 0.0)
            z_total, both = fused_sum(z_part, jnp.concatenate([norm_part, curv_part]), 6)
            norm_now, curvature = both[:outputs], both[outputs:]
        else:
            z_total, curvature = fused_sum(z_part, curv_part, 7)
        applied = REG * direction + inv_root * z_total
        step_size = norm_now / curvature
        solution = solution + step_size[None, :, None] * direction
        resid = resid - step_size[None, :, None] * applied
        if iteration + 1 < ITERS:
            norm_next = global_sum(jnp.sum(resid * resid, axis=(0, 2)))
            direction = resid + (norm_next / norm_now)[None, :, None] * direction
            norm_now = norm_next
    return (
        solution.transpose(1, 0, 2).reshape(outputs, npoints),
        resid.transpose(1, 0, 2).reshape(outputs, npoints),
    )


def solution(mesh):
    placed = (P("rows", "cols"), P(None, "rows"), P(None, "rows"))
    return jax.shard_map(
        local,
        mesh=mesh,
        in_specs=placed,
        out_specs=(P(None, "rows"), P(None, "rows")),
        check_vma=False,
    )
```

```python
import functools

import jax
import jax.numpy as jnp
from jax import lax
from jax.experimental import pallas as pl
from jax.experimental.pallas import tpu as pltpu
from jax.sharding import PartitionSpec as P

MESH = pl.DeviceIdType.MESH

ITERS = 2


REG = 1.5
RADIUS = 0.25


def wendland(left_x, right_x):
    left_f = left_x.astype(jnp.float32)
    right_f = right_x.astype(jnp.float32)
    left_sq = jnp.sum(left_f * left_f, axis=1)
    right_sq = jnp.sum(right_f * right_f, axis=1)
    inner_prod = jnp.einsum("nda,ndb->nab", left_f, right_f, precision=lax.Precision.HIGHEST)
    dist_sq = left_sq[:, :, None] + right_sq[:, None, :] - 2.0 * inner_prod
    scaled = jnp.sqrt(jnp.maximum(dist_sq, 0.0)) / RADIUS
    remain = jnp.maximum(1.0 - scaled, 0.0)
    square = remain * remain
    return square * square * (4.0 * scaled + 1.0)


def allsum_kernel(axis, n, x_ref, o_ref, recv, send_sem, recv_sem):
    me = lax.axis_index(axis)
    barrier = pltpu.get_barrier_semaphore()

    def greet(k, carry):
        peer = lax.rem(me + k, n)
        pl.semaphore_signal(barrier, inc=1, device_id={axis: peer}, device_id_type=MESH)
        return carry

    lax.fori_loop(1, n, greet, 0)
    pl.semaphore_wait(barrier, n - 1)

    def outgoing(peer):
        return pltpu.make_async_remote_copy(
            src_ref=x_ref,
            dst_ref=recv.at[me],
            send_sem=send_sem.at[peer],
            recv_sem=recv_sem.at[me],
            device_id={axis: peer},
            device_id_type=MESH,
        )

    def incoming(peer):
        return pltpu.make_async_remote_copy(
            src_ref=x_ref,
            dst_ref=recv.at[peer],
            send_sem=send_sem.at[peer],
            recv_sem=recv_sem.at[peer],
            device_id={axis: peer},
            device_id_type=MESH,
        )

    def start(k, carry):
        outgoing(lax.rem(me + k, n)).start()
        return carry

    lax.fori_loop(1, n, start, 0)
    recv[me] = x_ref[...]

    def finish(k, carry):
        peer = lax.rem(me + k, n)
        outgoing(peer).wait_send()
        incoming(peer).wait_recv()
        return carry

    lax.fori_loop(1, n, finish, 0)
    o_ref[...] = recv[0]

    def add(s, carry):
        o_ref[...] += recv[s]
        return carry

    lax.fori_loop(1, n, add, 0)


def allsum(x, axis, cid):
    n = lax.axis_size(axis)
    shape = x.shape
    flat = x.reshape(-1)
    size = flat.shape[0]
    if size <= 128:
        tile = jnp.pad(flat, (0, 128 - size)).reshape(1, 128)
    elif size % 1024 == 0:
        tile = flat.reshape(size // 128, 128)
    else:
        rows_pad = -(-size // 1024) * 8
        tile = jnp.pad(flat, (0, rows_pad * 128 - size)).reshape(rows_pad, 128)
    out = pl.pallas_call(
        functools.partial(allsum_kernel, axis, n),
        out_shape=jax.ShapeDtypeStruct(tile.shape, jnp.float32),
        in_specs=[pl.BlockSpec(memory_space=pltpu.VMEM)],
        out_specs=pl.BlockSpec(memory_space=pltpu.VMEM),
        scratch_shapes=[
            pltpu.VMEM((n,) + tile.shape, jnp.float32),
            pltpu.SemaphoreType.DMA((n,)),
            pltpu.SemaphoreType.DMA((n,)),
        ],
        compiler_params=pltpu.CompilerParams(collective_id=cid, has_side_effects=True),
    )(tile)
    return out.reshape(-1)[:size].reshape(shape)


def fused_kernel(
    n_rows, n_cols, group, z_ref, g_ref, zo_ref, go_ref, recv_z, gathered, recv_g, recv_b, recv_s, rows_sum,
    sems,
):
    row = lax.axis_index("rows")
    col = lax.axis_index("cols")
    barrier = pltpu.get_barrier_semaphore()

    pos = lax.rem(row, group)
    grp = row // group
    groups = n_rows // group

    def near(k):
        return row - pos + lax.rem(pos + k, group)

    def far(k):
        return lax.rem(grp + k, groups) * group + pos

    for k in range(1, group):
        pl.semaphore_signal(barrier, inc=1, device_id={"rows": near(k)}, device_id_type=MESH)
    for k in range(1, groups):
        pl.semaphore_signal(barrier, inc=1, device_id={"rows": far(k)}, device_id_type=MESH)
    for k in range(1, n_cols):
        pl.semaphore_signal(
            barrier, inc=1, device_id={"cols": lax.rem(col + k, n_cols)}, device_id_type=MESH
        )
    pl.semaphore_wait(barrier, group - 1 + groups - 1 + n_cols - 1)
    z_send, z_recv, g_send, g_recv, s_send, s_recv, a_send, a_recv, b_send, b_recv = sems

    def col_copy(src, dst, send, recv, peer, slot):
        return pltpu.make_async_remote_copy(
            src_ref=src,
            dst_ref=dst.at[slot],
            send_sem=send.at[peer],
            recv_sem=recv.at[slot],
            device_id={"cols": peer},
            device_id_type=MESH,
        )

    def row_copy(src, dst, send, recv, device, slot, peer_slot):
        return pltpu.make_async_remote_copy(
            src_ref=src,
            dst_ref=dst.at[slot],
            send_sem=send.at[peer_slot],
            recv_sem=recv.at[slot],
            device_id={"rows": device},
            device_id_type=MESH,
        )

    for k in range(1, n_cols):
        peer = lax.rem(col + k, n_cols)
        col_copy(z_ref.at[peer], recv_z, z_send, z_recv, peer, col).start()

    for k in range(1, group):
        row_copy(g_ref, recv_g, g_send, g_recv, near(k), pos, lax.rem(pos + k, group)).start()
    recv_z[col] = z_ref[col]
    recv_g[pos] = g_ref[...]
    for k in range(1, n_cols):
        peer = lax.rem(col + k, n_cols)
        col_copy(z_ref.at[peer], recv_z, z_send, z_recv, peer, col).wait_send()
        col_copy(z_ref.at[peer], recv_z, z_send, z_recv, peer, peer).wait_recv()
    gathered[col] = recv_z[0]
    for k in range(1, n_cols):
        gathered[col] += recv_z[k]
    for k in range(1, n_cols):
        col_copy(gathered.at[col], gathered, a_send, a_recv, lax.rem(col + k, n_cols), col).start()

    for k in range(1, group):
        other = lax.rem(pos + k, group)
        row_copy(g_ref, recv_g, g_send, g_recv, near(k), pos, other).wait_send()
        row_copy(g_ref, recv_g, g_send, g_recv, near(k), other, other).wait_recv()
    recv_b[grp] = recv_g[0]
    for k in range(1, group):
        recv_b[grp] += recv_g[k]
    for k in range(1, groups):
        row_copy(recv_b.at[grp], recv_b, b_send, b_recv, far(k), grp, lax.rem(grp + k, groups)).start()
    for k in range(1, groups):
        other = lax.rem(grp + k, groups)
        row_copy(recv_b.at[grp], recv_b, b_send, b_recv, far(k), grp, other).wait_send()
        row_copy(recv_b.at[grp], recv_b, b_send, b_recv, far(k), other, other).wait_recv()
    rows_sum[...] = recv_b[0]
    for k in range(1, groups):
        rows_sum[...] += recv_b[k]
    for k in range(1, n_cols):
        col_copy(rows_sum, recv_s, s_send, s_recv, lax.rem(col + k, n_cols), col).start()
    recv_s[col] = rows_sum[...]
    for k in range(1, n_cols):
        peer = lax.rem(col + k, n_cols)
        col_copy(gathered.at[col], gathered, a_send, a_recv, peer, col).wait_send()
        col_copy(gathered.at[peer], gathered, a_send, a_recv, peer, peer).wait_recv()
    zo_ref[...] = gathered[...]
    for k in range(1, n_cols):
        peer = lax.rem(col + k, n_cols)
        col_copy(rows_sum, recv_s, s_send, s_recv, peer, col).wait_send()
        col_copy(rows_sum, recv_s, s_send, s_recv, peer, peer).wait_recv()
    go_ref[...] = recv_s[0]
    for k in range(1, n_cols):
        go_ref[...] += recv_s[k]


def fused_sum(z, g, cid):
    n_rows = lax.axis_size("rows")
    n_cols = lax.axis_size("cols")
    z_tile = z.reshape(n_cols, -1, z.shape[-1])
    size = g.shape[0]
    g_tile = jnp.pad(g, (0, 128 - size)).reshape(1, 128)
    vmem = pl.BlockSpec(memory_space=pltpu.VMEM)
    group = 16 if n_rows % 16 == 0 and n_rows > 16 else (4 if n_rows % 4 == 0 else n_rows)
    groups = n_rows // group
    z_out, g_out = pl.pallas_call(
        functools.partial(fused_kernel, n_rows, n_cols, group),
        out_shape=[
            jax.ShapeDtypeStruct(z_tile.shape, jnp.float32),
            jax.ShapeDtypeStruct(g_tile.shape, jnp.float32),
        ],
        in_specs=[vmem, vmem],
        out_specs=[vmem, vmem],
        scratch_shapes=[
            pltpu.VMEM(z_tile.shape, jnp.float32),
            pltpu.VMEM(z_tile.shape, jnp.float32),
            pltpu.VMEM((group,) + g_tile.shape, jnp.float32),
            pltpu.VMEM((groups,) + g_tile.shape, jnp.float32),
            pltpu.VMEM((n_cols,) + g_tile.shape, jnp.float32),
            pltpu.VMEM(g_tile.shape, jnp.float32),
            [
                pltpu.SemaphoreType.DMA((n_cols,)),
                pltpu.SemaphoreType.DMA((n_cols,)),
                pltpu.SemaphoreType.DMA((group,)),
                pltpu.SemaphoreType.DMA((group,)),
                pltpu.SemaphoreType.DMA((n_cols,)),
                pltpu.SemaphoreType.DMA((n_cols,)),
                pltpu.SemaphoreType.DMA((n_cols,)),
                pltpu.SemaphoreType.DMA((n_cols,)),
                pltpu.SemaphoreType.DMA((groups,)),
                pltpu.SemaphoreType.DMA((groups,)),
            ],
        ],
        compiler_params=pltpu.CompilerParams(collective_id=cid, has_side_effects=True),
    )(z_tile, g_tile)
    return z_out.reshape(z.shape), g_out.reshape(-1)[:size]


def rows_sum_kernel(n, group, x_ref, o_ref, recv1, recv2, sems):
    me = lax.axis_index("rows")
    pos = lax.rem(me, group)
    base = me - pos
    grp = me // group
    groups = n // group
    barrier = pltpu.get_barrier_semaphore()

    def near(k):
        return base + lax.rem(pos + k, group)

    def far(k):
        return lax.rem(grp + k, groups) * group + pos

    for k in range(1, group):
        pl.semaphore_signal(barrier, inc=1, device_id={"rows": near(k)}, device_id_type=MESH)
    for k in range(1, groups):
        pl.semaphore_signal(barrier, inc=1, device_id={"rows": far(k)}, device_id_type=MESH)
    pl.semaphore_wait(barrier, group - 1 + groups - 1)
    send1, got1, send2, got2 = sems

    def copy(src, dst, send, got, device, slot, peer_slot):
        return pltpu.make_async_remote_copy(
            src_ref=src,
            dst_ref=dst.at[slot],
            send_sem=send.at[peer_slot],
            recv_sem=got.at[slot],
            device_id={"rows": device},
            device_id_type=MESH,
        )

    for k in range(1, group):
        copy(x_ref, recv1, send1, got1, near(k), pos, lax.rem(pos + k, group)).start()
    recv1[pos] = x_ref[...]
    for k in range(1, group):
        other = lax.rem(pos + k, group)
        copy(x_ref, recv1, send1, got1, near(k), pos, other).wait_send()
        copy(x_ref, recv1, send1, got1, near(k), other, other).wait_recv()
    recv2[grp] = recv1[0]
    for k in range(1, group):
        recv2[grp] += recv1[k]
    for k in range(1, groups):
        copy(recv2.at[grp], recv2, send2, got2, far(k), grp, lax.rem(grp + k, groups)).start()
    for k in range(1, groups):
        other = lax.rem(grp + k, groups)
        copy(recv2.at[grp], recv2, send2, got2, far(k), grp, other).wait_send()
        copy(recv2.at[grp], recv2, send2, got2, far(k), other, other).wait_recv()
    o_ref[...] = recv2[0]
    for k in range(1, groups):
        o_ref[...] += recv2[k]


def rows_sum(x, cid):
    n = lax.axis_size("rows")
    group = 16 if n % 16 == 0 and n > 16 else (4 if n % 4 == 0 else n)
    groups = n // group
    size = x.shape[0]
    tile = jnp.pad(x, (0, 128 - size)).reshape(1, 128)
    out = pl.pallas_call(
        functools.partial(rows_sum_kernel, n, group),
        out_shape=jax.ShapeDtypeStruct(tile.shape, jnp.float32),
        in_specs=[pl.BlockSpec(memory_space=pltpu.VMEM)],
        out_specs=pl.BlockSpec(memory_space=pltpu.VMEM),
        scratch_shapes=[
            pltpu.VMEM((group,) + tile.shape, jnp.float32),
            pltpu.VMEM((groups,) + tile.shape, jnp.float32),
            [
                pltpu.SemaphoreType.DMA((group,)),
                pltpu.SemaphoreType.DMA((group,)),
                pltpu.SemaphoreType.DMA((groups,)),
                pltpu.SemaphoreType.DMA((groups,)),
            ],
        ],
        compiler_params=pltpu.CompilerParams(collective_id=cid, has_side_effects=True),
    )(tile)
    return out.reshape(-1)[:size]


def local(block_list, points, targets):
    row_count = lax.axis_size("rows")
    row_index = lax.axis_index("rows")
    block_rows, slot_width = block_list.shape
    coord_dim, npoints = points.shape
    outputs = targets.shape[0]
    block_len = npoints // block_rows
    slot_count = block_rows * slot_width
    entries = block_list.reshape(slot_count)
    is_live = entries >= 0
    owners = jnp.where(is_live, entries // block_rows, 0)
    local_idx = jnp.where(is_live, entries - owners * block_rows, 0)
    slot_row = jnp.arange(slot_count, dtype=jnp.int32) // slot_width
    first_row = row_index * block_rows
    place_at = jnp.where(is_live, owners, row_count)
    pick_at = jnp.minimum(place_at, row_count - 1)
    wanted = jnp.full((row_count,), -1, jnp.int32).at[place_at].set(local_idx, mode="drop")
    asking_row = jnp.full((row_count,), -1, jnp.int32).at[place_at].set(slot_row, mode="drop")
    ask_live = asking_row >= 0
    ask_row = jnp.maximum(asking_row, 0)
    own_x = points.reshape(coord_dim, block_rows, block_len).transpose(1, 0, 2)
    asked_x = jnp.where(ask_live[:, None, None], own_x[ask_row], jnp.zeros((), own_x.dtype))
    lane = lax.broadcasted_iota(jnp.int32, (row_count, coord_dim, 128), 2)
    sublane = lax.broadcasted_iota(jnp.int32, (row_count, coord_dim, 128), 1)
    request = jnp.where(lane == 0, wanted[:, None, None], asking_row[:, None, None])
    request = jnp.where((sublane == 0) & (lane < 2), request, 0).astype(own_x.dtype)
    first_swap = lax.all_to_all(
        jnp.concatenate([asked_x, request], axis=2), "rows", split_axis=0, concat_axis=0, tiled=True
    )
    their_x = first_swap[:, :, :block_len]
    incoming = first_swap[:, 0, block_len:block_len + 2].astype(jnp.int32)
    in_live = incoming[:, 0] >= 0
    in_idx = jnp.maximum(incoming[:, 0], 0)
    their_row = jnp.arange(row_count, dtype=jnp.int32) * block_rows + jnp.maximum(incoming[:, 1], 0)
    in_off = in_live & (their_row != first_row + in_idx)
    collect_map = (
        (in_idx[None, :] == jnp.arange(block_rows, dtype=jnp.int32)[:, None]) & in_off[None, :]
    ).astype(jnp.float32)

    def swap(parts):
        return lax.all_to_all(parts, "rows", split_axis=0, concat_axis=0, tiled=True)

    peer_ids = jnp.arange(row_count, dtype=jnp.int32)
    to_lower = (peer_ids <= row_index)[:, None, None]
    from_self = (peer_ids == row_index)[:, None, None]

    def both_ways(blocks):
        got = swap(jnp.where(to_lower, asked_part(blocks), served_part(blocks)))
        their = jnp.where(peer_ids[:, None, None] >= row_index, got, jnp.zeros((), got.dtype))
        served_self = blocks[in_idx[row_index]]
        far = jnp.where(from_self, served_self[None], got)
        return their, per_slot(far)

    def asked_part(blocks):
        return jnp.where(ask_live[:, None, None], blocks[ask_row], jnp.zeros((), blocks.dtype))

    def served_part(blocks):
        return jnp.where(in_live[:, None, None], blocks[in_idx], jnp.zeros((), blocks.dtype))

    def per_slot(got):
        chosen = got[pick_at]
        return jnp.where(is_live[:, None, None], chosen, jnp.zeros((), chosen.dtype))

    def collect(terms):
        flat = terms.reshape(row_count, -1)
        summed = jnp.dot(
            collect_map, flat, precision=lax.Precision.HIGHEST, preferred_element_type=jnp.float32
        )
        return summed.reshape((block_rows,) + terms.shape[1:])

    def column_total(partial_value):
        return allsum(partial_value, "cols", 1 if partial_value.shape[1] == 1 else 2)

    def global_sum(values):
        return rows_sum(values, 8)

    far_x = per_slot(swap(served_part(own_x)))

    def pair_pass(lx, rx, live):
        values = jnp.where(live[:, None, None], wendland(lx, rx), 0.0)
        return (values.astype(jnp.bfloat16), jnp.sum(values, axis=2), jnp.sum(values, axis=1))

    in_k, _, in_col_sums = pair_pass(their_x, own_x[in_idx], in_off)
    own_k, own_row_sums, _ = pair_pass(own_x[slot_row], far_x, is_live)
    degree_direct = jnp.sum(own_row_sums.reshape(block_rows, slot_width, block_len), axis=1)
    degree_mirror = collect(in_col_sums)
    degree_part = (degree_direct + degree_mirror)[:, None, :]
    inv_root = 1.0 / jnp.sqrt(1.0 + column_total(degree_part))

    def apply_partial(weights):
        their_w, far_w = both_ways(weights)
        direct = jnp.einsum(
            "rkab,rkob->roa",
            own_k.reshape(block_rows, slot_width, block_len, block_len),
            far_w.reshape(block_rows, slot_width, outputs, block_len),
            preferred_element_type=jnp.float32,
        )
        picked = collect_map.astype(their_w.dtype)[:, None, :, None] * jnp.swapaxes(their_w, 0, 1)[None]
        mirror = jnp.einsum("joea,eab->job", picked, in_k, preferred_element_type=jnp.float32)
        return direct + mirror

    resid = targets.reshape(outputs, block_rows, block_len).transpose(1, 0, 2)
    direction = resid
    solution = jnp.zeros_like(resid)
    norm_now = jnp.sum(resid * resid, axis=(0, 2))
    first_col = lax.axis_index("cols") == 0
    for iteration in range(ITERS):
        weights = (direction * inv_root).astype(jnp.bfloat16)
        z_part = apply_partial(weights)
        own_term = jnp.where(first_col, REG * jnp.sum(direction * direction, axis=(0, 2)), 0.0)
        curv_part = own_term + jnp.sum(direction * (inv_root * z_part), axis=(0, 2))
        if iteration == 0:
            norm_part = jnp.where(first_col, norm_now, 0.0)
            z_total, both = fused_sum(z_part, jnp.concatenate([norm_part, curv_part]), 6)
            norm_now, curvature = both[:outputs], both[outputs:]
        else:
            z_total, curvature = fused_sum(z_part, curv_part, 7)
        applied = REG * direction + inv_root * z_total
        step_size = norm_now / curvature
        solution = solution + step_size[None, :, None] * direction
        resid = resid - step_size[None, :, None] * applied
        if iteration + 1 < ITERS:
            norm_next = global_sum(jnp.sum(resid * resid, axis=(0, 2)))
            direction = resid + (norm_next / norm_now)[None, :, None] * direction
            norm_now = norm_next
    return (
        solution.transpose(1, 0, 2).reshape(outputs, npoints),
        resid.transpose(1, 0, 2).reshape(outputs, npoints),
    )


def solution(mesh):
    placed = (P("rows", "cols"), P(None, "rows"), P(None, "rows"))
    return jax.shard_map(
        local,
        mesh=mesh,
        in_specs=placed,
        out_specs=(P(None, "rows"), P(None, "rows")),
        check_vma=False,
    )
```

```python
import functools

import jax
import jax.numpy as jnp
from jax import lax
from jax.experimental import pallas as pl
from jax.experimental.pallas import tpu as pltpu
from jax.sharding import PartitionSpec as P

MESH = pl.DeviceIdType.MESH

ITERS = 2


REG = 1.5
RADIUS = 0.25


def wendland(left_x, right_x):
    left_f = left_x.astype(jnp.float32)
    right_f = right_x.astype(jnp.float32)
    left_sq = jnp.sum(left_f * left_f, axis=1)
    right_sq = jnp.sum(right_f * right_f, axis=1)
    inner_prod = jnp.einsum("nda,ndb->nab", left_f, right_f, precision=lax.Precision.HIGHEST)
    dist_sq = left_sq[:, :, None] + right_sq[:, None, :] - 2.0 * inner_prod
    scaled = jnp.sqrt(jnp.maximum(dist_sq, 0.0)) / RADIUS
    remain = jnp.maximum(1.0 - scaled, 0.0)
    square = remain * remain
    return square * square * (4.0 * scaled + 1.0)


def allsum_kernel(axis, n, x_ref, o_ref, recv, send_sem, recv_sem):
    me = lax.axis_index(axis)
    barrier = pltpu.get_barrier_semaphore()

    def greet(k, carry):
        peer = lax.rem(me + k, n)
        pl.semaphore_signal(barrier, inc=1, device_id={axis: peer}, device_id_type=MESH)
        return carry

    lax.fori_loop(1, n, greet, 0)
    pl.semaphore_wait(barrier, n - 1)

    def outgoing(peer):
        return pltpu.make_async_remote_copy(
            src_ref=x_ref,
            dst_ref=recv.at[me],
            send_sem=send_sem.at[peer],
            recv_sem=recv_sem.at[me],
            device_id={axis: peer},
            device_id_type=MESH,
        )

    def incoming(peer):
        return pltpu.make_async_remote_copy(
            src_ref=x_ref,
            dst_ref=recv.at[peer],
            send_sem=send_sem.at[peer],
            recv_sem=recv_sem.at[peer],
            device_id={axis: peer},
            device_id_type=MESH,
        )

    def start(k, carry):
        outgoing(lax.rem(me + k, n)).start()
        return carry

    lax.fori_loop(1, n, start, 0)
    recv[me] = x_ref[...]

    def finish(k, carry):
        peer = lax.rem(me + k, n)
        outgoing(peer).wait_send()
        incoming(peer).wait_recv()
        return carry

    lax.fori_loop(1, n, finish, 0)
    o_ref[...] = recv[0]

    def add(s, carry):
        o_ref[...] += recv[s]
        return carry

    lax.fori_loop(1, n, add, 0)


def allsum(x, axis, cid):
    n = lax.axis_size(axis)
    shape = x.shape
    flat = x.reshape(-1)
    size = flat.shape[0]
    if size <= 128:
        tile = jnp.pad(flat, (0, 128 - size)).reshape(1, 128)
    elif size % 1024 == 0:
        tile = flat.reshape(size // 128, 128)
    else:
        rows_pad = -(-size // 1024) * 8
        tile = jnp.pad(flat, (0, rows_pad * 128 - size)).reshape(rows_pad, 128)
    out = pl.pallas_call(
        functools.partial(allsum_kernel, axis, n),
        out_shape=jax.ShapeDtypeStruct(tile.shape, jnp.float32),
        in_specs=[pl.BlockSpec(memory_space=pltpu.VMEM)],
        out_specs=pl.BlockSpec(memory_space=pltpu.VMEM),
        scratch_shapes=[
            pltpu.VMEM((n,) + tile.shape, jnp.float32),
            pltpu.SemaphoreType.DMA((n,)),
            pltpu.SemaphoreType.DMA((n,)),
        ],
        compiler_params=pltpu.CompilerParams(collective_id=cid, has_side_effects=True),
    )(tile)
    return out.reshape(-1)[:size].reshape(shape)


def fused_kernel(
    n_rows, n_cols, group, z_ref, g_ref, zo_ref, go_ref, recv_z, gathered, recv_g, recv_b, recv_s, rows_sum,
    sems,
):
    row = lax.axis_index("rows")
    col = lax.axis_index("cols")
    barrier = pltpu.get_barrier_semaphore()

    pos = lax.rem(row, group)
    grp = row // group
    groups = n_rows // group

    def near(k):
        return row - pos + lax.rem(pos + k, group)

    def far(k):
        return lax.rem(grp + k, groups) * group + pos

    for k in range(1, group):
        pl.semaphore_signal(barrier, inc=1, device_id={"rows": near(k)}, device_id_type=MESH)
    for k in range(1, groups):
        pl.semaphore_signal(barrier, inc=1, device_id={"rows": far(k)}, device_id_type=MESH)
    for k in range(1, n_cols):
        pl.semaphore_signal(
            barrier, inc=1, device_id={"cols": lax.rem(col + k, n_cols)}, device_id_type=MESH
        )
    pl.semaphore_wait(barrier, group - 1 + groups - 1 + n_cols - 1)
    z_send, z_recv, g_send, g_recv, s_send, s_recv, a_send, a_recv, b_send, b_recv = sems

    def col_copy(src, dst, send, recv, peer, slot):
        return pltpu.make_async_remote_copy(
            src_ref=src,
            dst_ref=dst.at[slot],
            send_sem=send.at[peer],
            recv_sem=recv.at[slot],
            device_id={"cols": peer},
            device_id_type=MESH,
        )

    def row_copy(src, dst, send, recv, device, slot, peer_slot):
        return pltpu.make_async_remote_copy(
            src_ref=src,
            dst_ref=dst.at[slot],
            send_sem=send.at[peer_slot],
            recv_sem=recv.at[slot],
            device_id={"rows": device},
            device_id_type=MESH,
        )

    for k in range(1, n_cols):
        peer = lax.rem(col + k, n_cols)
        col_copy(z_ref.at[peer], recv_z, z_send, z_recv, peer, col).start()

    for k in range(1, group):
        row_copy(g_ref, recv_g, g_send, g_recv, near(k), pos, lax.rem(pos + k, group)).start()
    recv_z[col] = z_ref[col]
    recv_g[pos] = g_ref[...]
    for k in range(1, n_cols):
        peer = lax.rem(col + k, n_cols)
        col_copy(z_ref.at[peer], recv_z, z_send, z_recv, peer, col).wait_send()
        col_copy(z_ref.at[peer], recv_z, z_send, z_recv, peer, peer).wait_recv()
    gathered[col] = recv_z[0]
    for k in range(1, n_cols):
        gathered[col] += recv_z[k]
    for k in range(1, n_cols):
        col_copy(gathered.at[col], gathered, a_send, a_recv, lax.rem(col + k, n_cols), col).start()

    for k in range(1, group):
        other = lax.rem(pos + k, group)
        row_copy(g_ref, recv_g, g_send, g_recv, near(k), pos, other).wait_send()
        row_copy(g_ref, recv_g, g_send, g_recv, near(k), other, other).wait_recv()
    recv_b[grp] = recv_g[0]
    for k in range(1, group):
        recv_b[grp] += recv_g[k]
    for k in range(1, groups):
        row_copy(recv_b.at[grp], recv_b, b_send, b_recv, far(k), grp, lax.rem(grp + k, groups)).start()
    for k in range(1, groups):
        other = lax.rem(grp + k, groups)
        row_copy(recv_b.at[grp], recv_b, b_send, b_recv, far(k), grp, other).wait_send()
        row_copy(recv_b.at[grp], recv_b, b_send, b_recv, far(k), other, other).wait_recv()
    rows_sum[...] = recv_b[0]
    for k in range(1, groups):
        rows_sum[...] += recv_b[k]
    for k in range(1, n_cols):
        col_copy(rows_sum, recv_s, s_send, s_recv, lax.rem(col + k, n_cols), col).start()
    recv_s[col] = rows_sum[...]
    for k in range(1, n_cols):
        peer = lax.rem(col + k, n_cols)
        col_copy(gathered.at[col], gathered, a_send, a_recv, peer, col).wait_send()
        col_copy(gathered.at[peer], gathered, a_send, a_recv, peer, peer).wait_recv()
    zo_ref[...] = gathered[...]
    for k in range(1, n_cols):
        peer = lax.rem(col + k, n_cols)
        col_copy(rows_sum, recv_s, s_send, s_recv, peer, col).wait_send()
        col_copy(rows_sum, recv_s, s_send, s_recv, peer, peer).wait_recv()
    go_ref[...] = recv_s[0]
    for k in range(1, n_cols):
        go_ref[...] += recv_s[k]


def fused_sum(z, g, cid):
    n_rows = lax.axis_size("rows")
    n_cols = lax.axis_size("cols")
    z_tile = z.reshape(n_cols, -1, z.shape[-1])
    size = g.shape[0]
    g_tile = jnp.pad(g, (0, 128 - size)).reshape(1, 128)
    vmem = pl.BlockSpec(memory_space=pltpu.VMEM)
    group = 8 if n_rows % 8 == 0 and n_rows > 8 else (4 if n_rows % 4 == 0 else n_rows)
    groups = n_rows // group
    z_out, g_out = pl.pallas_call(
        functools.partial(fused_kernel, n_rows, n_cols, group),
        out_shape=[
            jax.ShapeDtypeStruct(z_tile.shape, jnp.float32),
            jax.ShapeDtypeStruct(g_tile.shape, jnp.float32),
        ],
        in_specs=[vmem, vmem],
        out_specs=[vmem, vmem],
        scratch_shapes=[
            pltpu.VMEM(z_tile.shape, jnp.float32),
            pltpu.VMEM(z_tile.shape, jnp.float32),
            pltpu.VMEM((group,) + g_tile.shape, jnp.float32),
            pltpu.VMEM((groups,) + g_tile.shape, jnp.float32),
            pltpu.VMEM((n_cols,) + g_tile.shape, jnp.float32),
            pltpu.VMEM(g_tile.shape, jnp.float32),
            [
                pltpu.SemaphoreType.DMA((n_cols,)),
                pltpu.SemaphoreType.DMA((n_cols,)),
                pltpu.SemaphoreType.DMA((group,)),
                pltpu.SemaphoreType.DMA((group,)),
                pltpu.SemaphoreType.DMA((n_cols,)),
                pltpu.SemaphoreType.DMA((n_cols,)),
                pltpu.SemaphoreType.DMA((n_cols,)),
                pltpu.SemaphoreType.DMA((n_cols,)),
                pltpu.SemaphoreType.DMA((groups,)),
                pltpu.SemaphoreType.DMA((groups,)),
            ],
        ],
        compiler_params=pltpu.CompilerParams(collective_id=cid, has_side_effects=True),
    )(z_tile, g_tile)
    return z_out.reshape(z.shape), g_out.reshape(-1)[:size]


def rows_sum_kernel(n, group, x_ref, o_ref, recv1, recv2, sems):
    me = lax.axis_index("rows")
    pos = lax.rem(me, group)
    base = me - pos
    grp = me // group
    groups = n // group
    barrier = pltpu.get_barrier_semaphore()

    def near(k):
        return base + lax.rem(pos + k, group)

    def far(k):
        return lax.rem(grp + k, groups) * group + pos

    for k in range(1, group):
        pl.semaphore_signal(barrier, inc=1, device_id={"rows": near(k)}, device_id_type=MESH)
    for k in range(1, groups):
        pl.semaphore_signal(barrier, inc=1, device_id={"rows": far(k)}, device_id_type=MESH)
    pl.semaphore_wait(barrier, group - 1 + groups - 1)
    send1, got1, send2, got2 = sems

    def copy(src, dst, send, got, device, slot, peer_slot):
        return pltpu.make_async_remote_copy(
            src_ref=src,
            dst_ref=dst.at[slot],
            send_sem=send.at[peer_slot],
            recv_sem=got.at[slot],
            device_id={"rows": device},
            device_id_type=MESH,
        )

    for k in range(1, group):
        copy(x_ref, recv1, send1, got1, near(k), pos, lax.rem(pos + k, group)).start()
    recv1[pos] = x_ref[...]
    for k in range(1, group):
        other = lax.rem(pos + k, group)
        copy(x_ref, recv1, send1, got1, near(k), pos, other).wait_send()
        copy(x_ref, recv1, send1, got1, near(k), other, other).wait_recv()
    recv2[grp] = recv1[0]
    for k in range(1, group):
        recv2[grp] += recv1[k]
    for k in range(1, groups):
        copy(recv2.at[grp], recv2, send2, got2, far(k), grp, lax.rem(grp + k, groups)).start()
    for k in range(1, groups):
        other = lax.rem(grp + k, groups)
        copy(recv2.at[grp], recv2, send2, got2, far(k), grp, other).wait_send()
        copy(recv2.at[grp], recv2, send2, got2, far(k), other, other).wait_recv()
    o_ref[...] = recv2[0]
    for k in range(1, groups):
        o_ref[...] += recv2[k]


def rows_sum(x, cid):
    n = lax.axis_size("rows")
    group = 8 if n % 8 == 0 and n > 8 else (4 if n % 4 == 0 else n)
    groups = n // group
    size = x.shape[0]
    tile = jnp.pad(x, (0, 128 - size)).reshape(1, 128)
    out = pl.pallas_call(
        functools.partial(rows_sum_kernel, n, group),
        out_shape=jax.ShapeDtypeStruct(tile.shape, jnp.float32),
        in_specs=[pl.BlockSpec(memory_space=pltpu.VMEM)],
        out_specs=pl.BlockSpec(memory_space=pltpu.VMEM),
        scratch_shapes=[
            pltpu.VMEM((group,) + tile.shape, jnp.float32),
            pltpu.VMEM((groups,) + tile.shape, jnp.float32),
            [
                pltpu.SemaphoreType.DMA((group,)),
                pltpu.SemaphoreType.DMA((group,)),
                pltpu.SemaphoreType.DMA((groups,)),
                pltpu.SemaphoreType.DMA((groups,)),
            ],
        ],
        compiler_params=pltpu.CompilerParams(collective_id=cid, has_side_effects=True),
    )(tile)
    return out.reshape(-1)[:size]


def local(block_list, points, targets):
    row_count = lax.axis_size("rows")
    row_index = lax.axis_index("rows")
    block_rows, slot_width = block_list.shape
    coord_dim, npoints = points.shape
    outputs = targets.shape[0]
    block_len = npoints // block_rows
    slot_count = block_rows * slot_width
    entries = block_list.reshape(slot_count)
    is_live = entries >= 0
    owners = jnp.where(is_live, entries // block_rows, 0)
    local_idx = jnp.where(is_live, entries - owners * block_rows, 0)
    slot_row = jnp.arange(slot_count, dtype=jnp.int32) // slot_width
    first_row = row_index * block_rows
    place_at = jnp.where(is_live, owners, row_count)
    pick_at = jnp.minimum(place_at, row_count - 1)
    wanted = jnp.full((row_count,), -1, jnp.int32).at[place_at].set(local_idx, mode="drop")
    asking_row = jnp.full((row_count,), -1, jnp.int32).at[place_at].set(slot_row, mode="drop")
    ask_live = asking_row >= 0
    ask_row = jnp.maximum(asking_row, 0)
    own_x = points.reshape(coord_dim, block_rows, block_len).transpose(1, 0, 2)
    asked_x = jnp.where(ask_live[:, None, None], own_x[ask_row], jnp.zeros((), own_x.dtype))
    lane = lax.broadcasted_iota(jnp.int32, (row_count, coord_dim, 128), 2)
    sublane = lax.broadcasted_iota(jnp.int32, (row_count, coord_dim, 128), 1)
    request = jnp.where(lane == 0, wanted[:, None, None], asking_row[:, None, None])
    request = jnp.where((sublane == 0) & (lane < 2), request, 0).astype(own_x.dtype)
    first_swap = lax.all_to_all(
        jnp.concatenate([asked_x, request], axis=2), "rows", split_axis=0, concat_axis=0, tiled=True
    )
    their_x = first_swap[:, :, :block_len]
    incoming = first_swap[:, 0, block_len:block_len + 2].astype(jnp.int32)
    in_live = incoming[:, 0] >= 0
    in_idx = jnp.maximum(incoming[:, 0], 0)
    their_row = jnp.arange(row_count, dtype=jnp.int32) * block_rows + jnp.maximum(incoming[:, 1], 0)
    in_off = in_live & (their_row != first_row + in_idx)
    collect_map = (
        (in_idx[None, :] == jnp.arange(block_rows, dtype=jnp.int32)[:, None]) & in_off[None, :]
    ).astype(jnp.float32)

    def swap(parts):
        return lax.all_to_all(parts, "rows", split_axis=0, concat_axis=0, tiled=True)

    peer_ids = jnp.arange(row_count, dtype=jnp.int32)
    to_lower = (peer_ids <= row_index)[:, None, None]
    from_self = (peer_ids == row_index)[:, None, None]

    def both_ways(blocks):
        got = swap(jnp.where(to_lower, asked_part(blocks), served_part(blocks)))
        their = jnp.where(peer_ids[:, None, None] >= row_index, got, jnp.zeros((), got.dtype))
        served_self = blocks[in_idx[row_index]]
        far = jnp.where(from_self, served_self[None], got)
        return their, per_slot(far)

    def asked_part(blocks):
        return jnp.where(ask_live[:, None, None], blocks[ask_row], jnp.zeros((), blocks.dtype))

    def served_part(blocks):
        return jnp.where(in_live[:, None, None], blocks[in_idx], jnp.zeros((), blocks.dtype))

    def per_slot(got):
        chosen = got[pick_at]
        return jnp.where(is_live[:, None, None], chosen, jnp.zeros((), chosen.dtype))

    def collect(terms):
        flat = terms.reshape(row_count, -1)
        summed = jnp.dot(
            collect_map, flat, precision=lax.Precision.HIGHEST, preferred_element_type=jnp.float32
        )
        return summed.reshape((block_rows,) + terms.shape[1:])

    def column_total(partial_value):
        return allsum(partial_value, "cols", 1 if partial_value.shape[1] == 1 else 2)

    def global_sum(values):
        return rows_sum(values, 8)

    far_x = per_slot(swap(served_part(own_x)))

    def pair_pass(lx, rx, live):
        values = jnp.where(live[:, None, None], wendland(lx, rx), 0.0)
        return (values.astype(jnp.bfloat16), jnp.sum(values, axis=2), jnp.sum(values, axis=1))

    in_k, _, in_col_sums = pair_pass(their_x, own_x[in_idx], in_off)
    own_k, own_row_sums, _ = pair_pass(own_x[slot_row], far_x, is_live)
    degree_direct = jnp.sum(own_row_sums.reshape(block_rows, slot_width, block_len), axis=1)
    degree_mirror = collect(in_col_sums)
    degree_part = (degree_direct + degree_mirror)[:, None, :]
    inv_root = 1.0 / jnp.sqrt(1.0 + column_total(degree_part))

    def apply_partial(weights):
        their_w, far_w = both_ways(weights)
        direct = jnp.einsum(
            "rkab,rkob->roa",
            own_k.reshape(block_rows, slot_width, block_len, block_len),
            far_w.reshape(block_rows, slot_width, outputs, block_len),
            preferred_element_type=jnp.float32,
        )
        picked = collect_map.astype(their_w.dtype)[:, None, :, None] * jnp.swapaxes(their_w, 0, 1)[None]
        mirror = jnp.einsum("joea,eab->job", picked, in_k, preferred_element_type=jnp.float32)
        return direct + mirror

    resid = targets.reshape(outputs, block_rows, block_len).transpose(1, 0, 2)
    direction = resid
    solution = jnp.zeros_like(resid)
    norm_now = jnp.sum(resid * resid, axis=(0, 2))
    first_col = lax.axis_index("cols") == 0
    for iteration in range(ITERS):
        weights = (direction * inv_root).astype(jnp.bfloat16)
        z_part = apply_partial(weights)
        own_term = jnp.where(first_col, REG * jnp.sum(direction * direction, axis=(0, 2)), 0.0)
        curv_part = own_term + jnp.sum(direction * (inv_root * z_part), axis=(0, 2))
        if iteration == 0:
            norm_part = jnp.where(first_col, norm_now, 0.0)
            z_total, both = fused_sum(z_part, jnp.concatenate([norm_part, curv_part]), 6)
            norm_now, curvature = both[:outputs], both[outputs:]
        else:
            z_total, curvature = fused_sum(z_part, curv_part, 7)
        applied = REG * direction + inv_root * z_total
        step_size = norm_now / curvature
        solution = solution + step_size[None, :, None] * direction
        resid = resid - step_size[None, :, None] * applied
        if iteration + 1 < ITERS:
            norm_next = global_sum(jnp.sum(resid * resid, axis=(0, 2)))
            direction = resid + (norm_next / norm_now)[None, :, None] * direction
            norm_now = norm_next
    return (
        solution.transpose(1, 0, 2).reshape(outputs, npoints),
        resid.transpose(1, 0, 2).reshape(outputs, npoints),
    )


def solution(mesh):
    placed = (P("rows", "cols"), P(None, "rows"), P(None, "rows"))
    return jax.shard_map(
        local,
        mesh=mesh,
        in_specs=placed,
        out_specs=(P(None, "rows"), P(None, "rows")),
        check_vma=False,
    )
```

```python
import functools

import jax
import jax.numpy as jnp
from jax import lax
from jax.experimental import pallas as pl
from jax.experimental.pallas import tpu as pltpu
from jax.sharding import PartitionSpec as P

MESH = pl.DeviceIdType.MESH

ITERS = 2


REG = 1.5
RADIUS = 0.25


def wendland(left_x, right_x):
    left_f = left_x.astype(jnp.float32)
    right_f = right_x.astype(jnp.float32)
    left_sq = jnp.sum(left_f * left_f, axis=1)
    right_sq = jnp.sum(right_f * right_f, axis=1)
    inner_prod = jnp.einsum("nda,ndb->nab", left_f, right_f, precision=lax.Precision.HIGHEST)
    dist_sq = left_sq[:, :, None] + right_sq[:, None, :] - 2.0 * inner_prod
    scaled = jnp.sqrt(jnp.maximum(dist_sq, 0.0)) / RADIUS
    remain = jnp.maximum(1.0 - scaled, 0.0)
    square = remain * remain
    return square * square * (4.0 * scaled + 1.0)


def allsum_kernel(axis, n, x_ref, o_ref, recv, send_sem, recv_sem):
    me = lax.axis_index(axis)
    barrier = pltpu.get_barrier_semaphore()

    def greet(k, carry):
        peer = lax.rem(me + k, n)
        pl.semaphore_signal(barrier, inc=1, device_id={axis: peer}, device_id_type=MESH)
        return carry

    lax.fori_loop(1, n, greet, 0)
    pl.semaphore_wait(barrier, n - 1)

    def outgoing(peer):
        return pltpu.make_async_remote_copy(
            src_ref=x_ref,
            dst_ref=recv.at[me],
            send_sem=send_sem.at[peer],
            recv_sem=recv_sem.at[me],
            device_id={axis: peer},
            device_id_type=MESH,
        )

    def incoming(peer):
        return pltpu.make_async_remote_copy(
            src_ref=x_ref,
            dst_ref=recv.at[peer],
            send_sem=send_sem.at[peer],
            recv_sem=recv_sem.at[peer],
            device_id={axis: peer},
            device_id_type=MESH,
        )

    def start(k, carry):
        outgoing(lax.rem(me + k, n)).start()
        return carry

    lax.fori_loop(1, n, start, 0)
    recv[me] = x_ref[...]

    def finish(k, carry):
        peer = lax.rem(me + k, n)
        outgoing(peer).wait_send()
        incoming(peer).wait_recv()
        return carry

    lax.fori_loop(1, n, finish, 0)
    o_ref[...] = recv[0]

    def add(s, carry):
        o_ref[...] += recv[s]
        return carry

    lax.fori_loop(1, n, add, 0)


def allsum(x, axis, cid):
    n = lax.axis_size(axis)
    shape = x.shape
    flat = x.reshape(-1)
    size = flat.shape[0]
    if size <= 128:
        tile = jnp.pad(flat, (0, 128 - size)).reshape(1, 128)
    elif size % 1024 == 0:
        tile = flat.reshape(size // 128, 128)
    else:
        rows_pad = -(-size // 1024) * 8
        tile = jnp.pad(flat, (0, rows_pad * 128 - size)).reshape(rows_pad, 128)
    out = pl.pallas_call(
        functools.partial(allsum_kernel, axis, n),
        out_shape=jax.ShapeDtypeStruct(tile.shape, jnp.float32),
        in_specs=[pl.BlockSpec(memory_space=pltpu.VMEM)],
        out_specs=pl.BlockSpec(memory_space=pltpu.VMEM),
        scratch_shapes=[
            pltpu.VMEM((n,) + tile.shape, jnp.float32),
            pltpu.SemaphoreType.DMA((n,)),
            pltpu.SemaphoreType.DMA((n,)),
        ],
        compiler_params=pltpu.CompilerParams(collective_id=cid, has_side_effects=True),
    )(tile)
    return out.reshape(-1)[:size].reshape(shape)


def fused_kernel(
    n_rows, n_cols, group, z_ref, g_ref, zo_ref, go_ref, recv_z, gathered, recv_g, recv_b, recv_s, rows_sum,
    sems,
):
    row = lax.axis_index("rows")
    col = lax.axis_index("cols")
    barrier = pltpu.get_barrier_semaphore()

    pos = lax.rem(row, group)
    grp = row // group
    groups = n_rows // group

    def near(k):
        return row - pos + lax.rem(pos + k, group)

    def far(k):
        return lax.rem(grp + k, groups) * group + pos

    for k in range(1, group):
        pl.semaphore_signal(barrier, inc=1, device_id={"rows": near(k)}, device_id_type=MESH)
    for k in range(1, groups):
        pl.semaphore_signal(barrier, inc=1, device_id={"rows": far(k)}, device_id_type=MESH)
    for k in range(1, n_cols):
        pl.semaphore_signal(
            barrier, inc=1, device_id={"cols": lax.rem(col + k, n_cols)}, device_id_type=MESH
        )
    pl.semaphore_wait(barrier, group - 1 + groups - 1 + n_cols - 1)
    z_send, z_recv, g_send, g_recv, s_send, s_recv, a_send, a_recv, b_send, b_recv = sems

    def col_copy(src, dst, send, recv, peer, slot):
        return pltpu.make_async_remote_copy(
            src_ref=src,
            dst_ref=dst.at[slot],
            send_sem=send.at[peer],
            recv_sem=recv.at[slot],
            device_id={"cols": peer},
            device_id_type=MESH,
        )

    def row_copy(src, dst, send, recv, device, slot, peer_slot):
        return pltpu.make_async_remote_copy(
            src_ref=src,
            dst_ref=dst.at[slot],
            send_sem=send.at[peer_slot],
            recv_sem=recv.at[slot],
            device_id={"rows": device},
            device_id_type=MESH,
        )

    for k in range(1, n_cols):
        peer = lax.rem(col + k, n_cols)
        col_copy(z_ref.at[peer], recv_z, z_send, z_recv, peer, col).start()

    for k in range(1, group):
        row_copy(g_ref, recv_g, g_send, g_recv, near(k), pos, lax.rem(pos + k, group)).start()
    recv_z[col] = z_ref[col]
    recv_g[pos] = g_ref[...]
    for k in range(1, n_cols):
        peer = lax.rem(col + k, n_cols)
        col_copy(z_ref.at[peer], recv_z, z_send, z_recv, peer, col).wait_send()
        col_copy(z_ref.at[peer], recv_z, z_send, z_recv, peer, peer).wait_recv()
    gathered[col] = recv_z[0]
    for k in range(1, n_cols):
        gathered[col] += recv_z[k]
    for k in range(1, n_cols):
        col_copy(gathered.at[col], gathered, a_send, a_recv, lax.rem(col + k, n_cols), col).start()

    for k in range(1, group):
        other = lax.rem(pos + k, group)
        row_copy(g_ref, recv_g, g_send, g_recv, near(k), pos, other).wait_send()
        row_copy(g_ref, recv_g, g_send, g_recv, near(k), other, other).wait_recv()
    recv_b[grp] = recv_g[0]
    for k in range(1, group):
        recv_b[grp] += recv_g[k]
    for k in range(1, groups):
        row_copy(recv_b.at[grp], recv_b, b_send, b_recv, far(k), grp, lax.rem(grp + k, groups)).start()
    for k in range(1, groups):
        other = lax.rem(grp + k, groups)
        row_copy(recv_b.at[grp], recv_b, b_send, b_recv, far(k), grp, other).wait_send()
        row_copy(recv_b.at[grp], recv_b, b_send, b_recv, far(k), other, other).wait_recv()
    rows_sum[...] = recv_b[0]
    for k in range(1, groups):
        rows_sum[...] += recv_b[k]
    for k in range(1, n_cols):
        col_copy(rows_sum, recv_s, s_send, s_recv, lax.rem(col + k, n_cols), col).start()
    recv_s[col] = rows_sum[...]
    for k in range(1, n_cols):
        peer = lax.rem(col + k, n_cols)
        col_copy(gathered.at[col], gathered, a_send, a_recv, peer, col).wait_send()
        col_copy(gathered.at[peer], gathered, a_send, a_recv, peer, peer).wait_recv()
    zo_ref[...] = gathered[...]
    for k in range(1, n_cols):
        peer = lax.rem(col + k, n_cols)
        col_copy(rows_sum, recv_s, s_send, s_recv, peer, col).wait_send()
        col_copy(rows_sum, recv_s, s_send, s_recv, peer, peer).wait_recv()
    go_ref[...] = recv_s[0]
    for k in range(1, n_cols):
        go_ref[...] += recv_s[k]


def fused_sum(z, g, cid):
    n_rows = lax.axis_size("rows")
    n_cols = lax.axis_size("cols")
    z_tile = z.reshape(n_cols, -1, z.shape[-1])
    size = g.shape[0]
    g_tile = jnp.pad(g, (0, 128 - size)).reshape(1, 128)
    vmem = pl.BlockSpec(memory_space=pltpu.VMEM)
    group = 32 if n_rows % 32 == 0 and n_rows > 32 else (4 if n_rows % 4 == 0 else n_rows)
    groups = n_rows // group
    z_out, g_out = pl.pallas_call(
        functools.partial(fused_kernel, n_rows, n_cols, group),
        out_shape=[
            jax.ShapeDtypeStruct(z_tile.shape, jnp.float32),
            jax.ShapeDtypeStruct(g_tile.shape, jnp.float32),
        ],
        in_specs=[vmem, vmem],
        out_specs=[vmem, vmem],
        scratch_shapes=[
            pltpu.VMEM(z_tile.shape, jnp.float32),
            pltpu.VMEM(z_tile.shape, jnp.float32),
            pltpu.VMEM((group,) + g_tile.shape, jnp.float32),
            pltpu.VMEM((groups,) + g_tile.shape, jnp.float32),
            pltpu.VMEM((n_cols,) + g_tile.shape, jnp.float32),
            pltpu.VMEM(g_tile.shape, jnp.float32),
            [
                pltpu.SemaphoreType.DMA((n_cols,)),
                pltpu.SemaphoreType.DMA((n_cols,)),
                pltpu.SemaphoreType.DMA((group,)),
                pltpu.SemaphoreType.DMA((group,)),
                pltpu.SemaphoreType.DMA((n_cols,)),
                pltpu.SemaphoreType.DMA((n_cols,)),
                pltpu.SemaphoreType.DMA((n_cols,)),
                pltpu.SemaphoreType.DMA((n_cols,)),
                pltpu.SemaphoreType.DMA((groups,)),
                pltpu.SemaphoreType.DMA((groups,)),
            ],
        ],
        compiler_params=pltpu.CompilerParams(collective_id=cid, has_side_effects=True),
    )(z_tile, g_tile)
    return z_out.reshape(z.shape), g_out.reshape(-1)[:size]


def rows_sum_kernel(n, group, x_ref, o_ref, recv1, recv2, sems):
    me = lax.axis_index("rows")
    pos = lax.rem(me, group)
    base = me - pos
    grp = me // group
    groups = n // group
    barrier = pltpu.get_barrier_semaphore()

    def near(k):
        return base + lax.rem(pos + k, group)

    def far(k):
        return lax.rem(grp + k, groups) * group + pos

    for k in range(1, group):
        pl.semaphore_signal(barrier, inc=1, device_id={"rows": near(k)}, device_id_type=MESH)
    for k in range(1, groups):
        pl.semaphore_signal(barrier, inc=1, device_id={"rows": far(k)}, device_id_type=MESH)
    pl.semaphore_wait(barrier, group - 1 + groups - 1)
    send1, got1, send2, got2 = sems

    def copy(src, dst, send, got, device, slot, peer_slot):
        return pltpu.make_async_remote_copy(
            src_ref=src,
            dst_ref=dst.at[slot],
            send_sem=send.at[peer_slot],
            recv_sem=got.at[slot],
            device_id={"rows": device},
            device_id_type=MESH,
        )

    for k in range(1, group):
        copy(x_ref, recv1, send1, got1, near(k), pos, lax.rem(pos + k, group)).start()
    recv1[pos] = x_ref[...]
    for k in range(1, group):
        other = lax.rem(pos + k, group)
        copy(x_ref, recv1, send1, got1, near(k), pos, other).wait_send()
        copy(x_ref, recv1, send1, got1, near(k), other, other).wait_recv()
    recv2[grp] = recv1[0]
    for k in range(1, group):
        recv2[grp] += recv1[k]
    for k in range(1, groups):
        copy(recv2.at[grp], recv2, send2, got2, far(k), grp, lax.rem(grp + k, groups)).start()
    for k in range(1, groups):
        other = lax.rem(grp + k, groups)
        copy(recv2.at[grp], recv2, send2, got2, far(k), grp, other).wait_send()
        copy(recv2.at[grp], recv2, send2, got2, far(k), other, other).wait_recv()
    o_ref[...] = recv2[0]
    for k in range(1, groups):
        o_ref[...] += recv2[k]


def rows_sum(x, cid):
    n = lax.axis_size("rows")
    group = 32 if n % 32 == 0 and n > 32 else (4 if n % 4 == 0 else n)
    groups = n // group
    size = x.shape[0]
    tile = jnp.pad(x, (0, 128 - size)).reshape(1, 128)
    out = pl.pallas_call(
        functools.partial(rows_sum_kernel, n, group),
        out_shape=jax.ShapeDtypeStruct(tile.shape, jnp.float32),
        in_specs=[pl.BlockSpec(memory_space=pltpu.VMEM)],
        out_specs=pl.BlockSpec(memory_space=pltpu.VMEM),
        scratch_shapes=[
            pltpu.VMEM((group,) + tile.shape, jnp.float32),
            pltpu.VMEM((groups,) + tile.shape, jnp.float32),
            [
                pltpu.SemaphoreType.DMA((group,)),
                pltpu.SemaphoreType.DMA((group,)),
                pltpu.SemaphoreType.DMA((groups,)),
                pltpu.SemaphoreType.DMA((groups,)),
            ],
        ],
        compiler_params=pltpu.CompilerParams(collective_id=cid, has_side_effects=True),
    )(tile)
    return out.reshape(-1)[:size]


def local(block_list, points, targets):
    row_count = lax.axis_size("rows")
    row_index = lax.axis_index("rows")
    block_rows, slot_width = block_list.shape
    coord_dim, npoints = points.shape
    outputs = targets.shape[0]
    block_len = npoints // block_rows
    slot_count = block_rows * slot_width
    entries = block_list.reshape(slot_count)
    is_live = entries >= 0
    owners = jnp.where(is_live, entries // block_rows, 0)
    local_idx = jnp.where(is_live, entries - owners * block_rows, 0)
    slot_row = jnp.arange(slot_count, dtype=jnp.int32) // slot_width
    first_row = row_index * block_rows
    place_at = jnp.where(is_live, owners, row_count)
    pick_at = jnp.minimum(place_at, row_count - 1)
    wanted = jnp.full((row_count,), -1, jnp.int32).at[place_at].set(local_idx, mode="drop")
    asking_row = jnp.full((row_count,), -1, jnp.int32).at[place_at].set(slot_row, mode="drop")
    ask_live = asking_row >= 0
    ask_row = jnp.maximum(asking_row, 0)
    own_x = points.reshape(coord_dim, block_rows, block_len).transpose(1, 0, 2)
    asked_x = jnp.where(ask_live[:, None, None], own_x[ask_row], jnp.zeros((), own_x.dtype))
    lane = lax.broadcasted_iota(jnp.int32, (row_count, coord_dim, 128), 2)
    sublane = lax.broadcasted_iota(jnp.int32, (row_count, coord_dim, 128), 1)
    request = jnp.where(lane == 0, wanted[:, None, None], asking_row[:, None, None])
    request = jnp.where((sublane == 0) & (lane < 2), request, 0).astype(own_x.dtype)
    first_swap = lax.all_to_all(
        jnp.concatenate([asked_x, request], axis=2), "rows", split_axis=0, concat_axis=0, tiled=True
    )
    their_x = first_swap[:, :, :block_len]
    incoming = first_swap[:, 0, block_len:block_len + 2].astype(jnp.int32)
    in_live = incoming[:, 0] >= 0
    in_idx = jnp.maximum(incoming[:, 0], 0)
    their_row = jnp.arange(row_count, dtype=jnp.int32) * block_rows + jnp.maximum(incoming[:, 1], 0)
    in_off = in_live & (their_row != first_row + in_idx)
    collect_map = (
        (in_idx[None, :] == jnp.arange(block_rows, dtype=jnp.int32)[:, None]) & in_off[None, :]
    ).astype(jnp.float32)

    def swap(parts):
        return lax.all_to_all(parts, "rows", split_axis=0, concat_axis=0, tiled=True)

    peer_ids = jnp.arange(row_count, dtype=jnp.int32)
    to_lower = (peer_ids <= row_index)[:, None, None]
    from_self = (peer_ids == row_index)[:, None, None]

    def both_ways(blocks):
        got = swap(jnp.where(to_lower, asked_part(blocks), served_part(blocks)))
        their = jnp.where(peer_ids[:, None, None] >= row_index, got, jnp.zeros((), got.dtype))
        served_self = blocks[in_idx[row_index]]
        far = jnp.where(from_self, served_self[None], got)
        return their, per_slot(far)

    def asked_part(blocks):
        return jnp.where(ask_live[:, None, None], blocks[ask_row], jnp.zeros((), blocks.dtype))

    def served_part(blocks):
        return jnp.where(in_live[:, None, None], blocks[in_idx], jnp.zeros((), blocks.dtype))

    def per_slot(got):
        chosen = got[pick_at]
        return jnp.where(is_live[:, None, None], chosen, jnp.zeros((), chosen.dtype))

    def collect(terms):
        flat = terms.reshape(row_count, -1)
        summed = jnp.dot(
            collect_map, flat, precision=lax.Precision.HIGHEST, preferred_element_type=jnp.float32
        )
        return summed.reshape((block_rows,) + terms.shape[1:])

    def column_total(partial_value):
        return allsum(partial_value, "cols", 1 if partial_value.shape[1] == 1 else 2)

    def global_sum(values):
        return rows_sum(values, 8)

    far_x = per_slot(swap(served_part(own_x)))

    def pair_pass(lx, rx, live):
        values = jnp.where(live[:, None, None], wendland(lx, rx), 0.0)
        return (values.astype(jnp.bfloat16), jnp.sum(values, axis=2), jnp.sum(values, axis=1))

    in_k, _, in_col_sums = pair_pass(their_x, own_x[in_idx], in_off)
    own_k, own_row_sums, _ = pair_pass(own_x[slot_row], far_x, is_live)
    degree_direct = jnp.sum(own_row_sums.reshape(block_rows, slot_width, block_len), axis=1)
    degree_mirror = collect(in_col_sums)
    degree_part = (degree_direct + degree_mirror)[:, None, :]
    inv_root = 1.0 / jnp.sqrt(1.0 + column_total(degree_part))

    def apply_partial(weights):
        their_w, far_w = both_ways(weights)
        direct = jnp.einsum(
            "rkab,rkob->roa",
            own_k.reshape(block_rows, slot_width, block_len, block_len),
            far_w.reshape(block_rows, slot_width, outputs, block_len),
            preferred_element_type=jnp.float32,
        )
        picked = collect_map.astype(their_w.dtype)[:, None, :, None] * jnp.swapaxes(their_w, 0, 1)[None]
        mirror = jnp.einsum("joea,eab->job", picked, in_k, preferred_element_type=jnp.float32)
        return direct + mirror

    resid = targets.reshape(outputs, block_rows, block_len).transpose(1, 0, 2)
    direction = resid
    solution = jnp.zeros_like(resid)
    norm_now = jnp.sum(resid * resid, axis=(0, 2))
    first_col = lax.axis_index("cols") == 0
    for iteration in range(ITERS):
        weights = (direction * inv_root).astype(jnp.bfloat16)
        z_part = apply_partial(weights)
        own_term = jnp.where(first_col, REG * jnp.sum(direction * direction, axis=(0, 2)), 0.0)
        curv_part = own_term + jnp.sum(direction * (inv_root * z_part), axis=(0, 2))
        if iteration == 0:
            norm_part = jnp.where(first_col, norm_now, 0.0)
            z_total, both = fused_sum(z_part, jnp.concatenate([norm_part, curv_part]), 6)
            norm_now, curvature = both[:outputs], both[outputs:]
        else:
            z_total, curvature = fused_sum(z_part, curv_part, 7)
        applied = REG * direction + inv_root * z_total
        step_size = norm_now / curvature
        solution = solution + step_size[None, :, None] * direction
        resid = resid - step_size[None, :, None] * applied
        if iteration + 1 < ITERS:
            norm_next = global_sum(jnp.sum(resid * resid, axis=(0, 2)))
            direction = resid + (norm_next / norm_now)[None, :, None] * direction
            norm_now = norm_next
    return (
        solution.transpose(1, 0, 2).reshape(outputs, npoints),
        resid.transpose(1, 0, 2).reshape(outputs, npoints),
    )


def solution(mesh):
    placed = (P("rows", "cols"), P(None, "rows"), P(None, "rows"))
    return jax.shard_map(
        local,
        mesh=mesh,
        in_specs=placed,
        out_specs=(P(None, "rows"), P(None, "rows")),
        check_vma=False,
    )
```
